32 devices in a mesh: pb: 4 (over y, x), ka: 8 (over z, core).
Axes of the slice: x: 2, y: 2, z: 4, core: 2. Of those that a mesh axis runs over, the one named last changes fastest.
Arguments:
- q_single: float32 [128, 384], P(('pb', 'ka')), may hold values from -6 to 6
- k_single: float32 [1024, 384], P(('pb', 'ka')), may hold values from -6 to 6
- q_frames: float32 [12, 128], P(None, ('pb', 'ka')), may hold values from -64 to 64, as said below
- k_frames: float32 [12, 1024], P(None, ('pb', 'ka')), may hold values from -150 to 150, as said below
- pair_tile: bfloat16 [128, 1024, 128], P('pb', 'ka'), may hold values from -6 to 6
- w_query: bfloat16 [384, 336], replicated, may hold values from -0.3125 to 0.3125
- w_key: bfloat16 [384, 816], replicated, may hold values from -0.3125 to 0.3125
- w_bias: bfloat16 [128, 12], replicated, may hold values from -0.5 to 0.5
- w_out: bfloat16 [2112, 384], replicated, may hold values from -0.125 to 0.125
- head_weight: float32 [12], replicated, may hold values from -4 to 1
- chain_bias: float32 [12], replicated, may hold values from -2 to 2
- q_chain: int32 [128], P('pb'), may hold values from 0 to 3
- k_chain: int32 [1024], P('ka'), may hold values from 0 to 3
- k_mask: int32 [1024], P('ka'), may hold values 0 or 1
- d_update: float32 [128, 384], P(('pb', 'ka')), may hold values from -6 to 6
Outputs:
- update: bfloat16 [128, 384], P(('pb', 'ka'))
- d_pair: bfloat16 [128, 1024, 128], P('pb', 'ka')
- d_query_single: bfloat16 [128, 384], P(('pb', 'ka'))
- d_key_single: float32 [1024, 384], P(('ka', 'pb'))
The draws below stay inside these ranges and needn't reach their ends.
Inputs may be any that keep to these rules, and one draw needn't show every extreme that they name: `q_frames`: rows 0 to 8 of each column hold a rotation matrix row by row, rows 9 to 11 its translation. `k_frames`: rows 0 to 8 of each column hold a rotation matrix row by row, rows 9 to 11 its translation.
All inputs are finite; a program needn't handle non-finite values. No bound on the sum of `k_mask` on one device may be relied on, other than what follows from the above.
Results may differ from the reference program's by a relative error of at most 0.0028.
Values sent between devices are 32-bit elements; how exact they have to be, the bound alone decides.
No kernel may reach another device: no remote copies, remote signals or barrier semaphores. Data moves between devices by JAX's collectives and lax.ppermute only.
A program may use at most 64 MiB of HBM per device.

```python
import math
import jax
import jax.numpy as jnp
from jax import lax

CS = 384
CP = 128
H = 12
HEAD = 16
PQ = 4
PV = 8
Q_DEV = 32
QUERIES = 128
NRES = 1024
QF = 336
KF = 816
FEAT = 2112


def frame_table(key, count, spread, limit):
    quat = jax.random.normal(jax.random.fold_in(key, 11), (4, count), jnp.float32)
    quat = quat / jnp.sqrt(jnp.sum(quat * quat, axis=0, keepdims=True) + 1e-06)
    scalar_w = quat[0]
    scalar_x = quat[1]
    scalar_y = quat[2]
    scalar_z = quat[3]
    rotation = jnp.stack([1.0 - 2.0 * (scalar_y * scalar_y + scalar_z * scalar_z), 2.0 * (scalar_x * scalar_y - scalar_w * scalar_z), 2.0 * (scalar_x * scalar_z + scalar_w * scalar_y), 2.0 * (scalar_x * scalar_y + scalar_w * scalar_z), 1.0 - 2.0 * (scalar_x * scalar_x + scalar_z * scalar_z), 2.0 * (scalar_y * scalar_z - scalar_w * scalar_x), 2.0 * (scalar_x * scalar_z - scalar_w * scalar_y), 2.0 * (scalar_y * scalar_z + scalar_w * scalar_x), 1.0 - 2.0 * (scalar_x * scalar_x + scalar_y * scalar_y)])
    offset = spread * jax.random.normal(jax.random.fold_in(key, 12), (3, count), jnp.float32)
    offset = jnp.clip(offset, -limit, limit)
    return jnp.concatenate([rotation, offset], axis=0)


def draw_q_frames(key, part):
    own_key = jax.random.fold_in(key, 101)
    table = frame_table(own_key, QUERIES, 3.0, 64.0)
    return table


def draw_k_frames(key, part):
    own_key = jax.random.fold_in(key, 202)
    table = frame_table(own_key, NRES, 3.0, 150.0)
    return table


def place_ends(values, key, smallest, high):
    extent = values.shape
    spot = [jax.random.randint(jax.random.fold_in(key, axis), (), 0, extent[axis]) for axis in range(len(extent))]
    values = values.at[tuple(spot)].set(smallest)
    longest = extent.index(max(extent))
    spot[longest] = (spot[longest] + 1) % extent[longest]
    return values.at[tuple(spot)].set(high)


def block_scale(key, dims, split, least, high):
    loudness = 1.0
    for dim, shards_of in split:
        draws = jax.random.uniform(jax.random.fold_in(jax.random.fold_in(key, 6), dim), (shards_of,), jnp.float32, least / len(split), high / len(split))
        loudness = loudness * jnp.repeat(jnp.exp(draws), dims[dim] // shards_of).reshape((-1,) + (1,) * (len(dims) - 1 - dim))
    return loudness


def noise(key, extent, scale, bound, shards=(), held_as=jnp.bfloat16):
    result = scale * jax.random.normal(key, extent, jnp.float32)
    if shards:
        result = result * block_scale(key, extent, shards, -0.22, 0.18)
    return jnp.clip(result, -bound, bound).astype(held_as)


def setup_inputs(seed: int = 0) -> dict:
    key_of = jax.random.split(jax.random.key(seed), 16)
    return {
        "q_single": noise(key_of[0], (QUERIES, CS), 1.0, 6.0, ((0, 32),), jnp.float32),
        "k_single": noise(key_of[1], (NRES, CS), 1.0, 6.0, ((0, 32),), jnp.float32),
        "q_frames": draw_q_frames(jax.random.fold_in(key_of[15], 71), 0),
        "k_frames": draw_k_frames(jax.random.fold_in(key_of[15], 71), 0),
        "pair_tile": noise(key_of[4], (QUERIES, NRES, CP), 1.0, 6.0, ((0, 4), (1, 8))),
        "w_query": noise(key_of[5], (CS, QF), CS ** -0.5, 0.3125),
        "w_key": noise(key_of[6], (CS, KF), CS ** -0.5, 0.3125),
        "w_bias": noise(key_of[7], (CP, H), CP ** -0.5, 0.5),
        "w_out": noise(key_of[8], (FEAT, CS), FEAT ** -0.5, 0.125),
        "head_weight": jnp.clip(jax.random.uniform(key_of[9], (H,), jnp.float32, -4.0, 1.0), -4.0, 1.0),
        "chain_bias": jnp.clip(jax.random.uniform(key_of[10], (H,), jnp.float32, -2.0, 2.0), -2.0, 2.0),
        "q_chain": place_ends(jax.random.randint(key_of[11], (QUERIES,), 0, 4), jax.random.fold_in(key_of[11], 1), 0, 3).astype(jnp.int32),
        "k_chain": place_ends(jax.random.randint(key_of[12], (NRES,), 0, 4), jax.random.fold_in(key_of[12], 1), 0, 3).astype(jnp.int32),
        "k_mask": place_ends((jax.random.randint(key_of[13], (NRES,), 0, 8) < 7).astype(jnp.int32), jax.random.fold_in(key_of[13], 1), 0, 1),
        "d_update": noise(key_of[14], (QUERIES, CS), 1.0, 6.0, ((0, 32),), jnp.float32),
    }


PRECISE = lax.Precision.HIGHEST
MASKED = -1000000000.0
LOGIT_WEIGHT = math.sqrt(1.0 / 3.0)

def coefficients(head_weight):
    return LOGIT_WEIGHT * jax.nn.softplus(head_weight) * math.sqrt(2.0 / (9.0 * PQ)) / 2.0

def rotations(frames):
    rotation = jnp.transpose(frames[0:9]).reshape(frames.shape[1], 3, 3)
    offset = jnp.transpose(frames[9:12])
    return (rotation, offset)

def to_world(rotation, offset, local_pts):
    return jnp.einsum('ixy,iyp->ixp', rotation, local_pts, precision=PRECISE) + offset[:, :, None]

def to_local(rotation, grad_pts):
    return jnp.einsum('ixy,ixp->iyp', rotation, grad_pts, precision=PRECISE)

def project_query(single, frames, w_query):
    row_count = single.shape[0]
    projected = jnp.dot(single, w_query.astype(jnp.float32), precision=PRECISE)
    rotation, offset = rotations(frames)
    local_pts = projected[:, H * HEAD:].reshape(row_count, 3, H * PQ)
    world_pts = to_world(rotation, offset, local_pts)
    return jnp.concatenate([projected[:, :H * HEAD], world_pts.reshape(row_count, -1)], axis=1)

def project_key(single, frames, w_key):
    row_count = single.shape[0]
    projected = jnp.dot(single, w_key.astype(jnp.float32), precision=PRECISE)
    rotation, offset = rotations(frames)
    head_cols = 2 * H * HEAD
    key_pts = projected[:, head_cols:head_cols + 3 * H * PQ].reshape(row_count, 3, H * PQ)
    value_pts = projected[:, head_cols + 3 * H * PQ:].reshape(row_count, 3, H * PV)
    key_world = to_world(rotation, offset, key_pts)
    value_world = to_world(rotation, offset, value_pts)
    return jnp.concatenate([projected[:, :head_cols], key_world.reshape(row_count, -1), value_world.reshape(row_count, -1)], axis=1)

def split_query(qfeat):
    n_query = qfeat.shape[0]
    q_heads = qfeat[:, :H * HEAD].reshape(n_query, H, HEAD)
    q_points = qfeat[:, H * HEAD:].reshape(n_query, 3, H, PQ)
    return (q_heads, q_points)

def split_key(kfeat):
    n_key = kfeat.shape[0]
    head_cols = 2 * H * HEAD
    k_heads = kfeat[:, :H * HEAD].reshape(n_key, H, HEAD)
    v_heads = kfeat[:, H * HEAD:head_cols].reshape(n_key, H, HEAD)
    k_points = kfeat[:, head_cols:head_cols + 3 * H * PQ].reshape(n_key, 3, H, PQ)
    v_points = kfeat[:, head_cols + 3 * H * PQ:].reshape(n_key, 3, H, PV)
    return (k_heads, v_heads, k_points, v_points)

def attend_logits(qfeat, kfeat, pair_tile, w_bias, point_scale, chain_bias, q_chain, k_chain, k_mask):
    q_heads, q_points = split_query(qfeat)
    k_heads, v_heads, k_points, v_points = split_key(kfeat)
    qk_dots = jnp.einsum('qhc,khc->hqk', q_heads, k_heads, precision=PRECISE)
    cross_pts = jnp.einsum('qxhp,kxhp->hqk', q_points, k_points, precision=PRECISE)
    q_square = lax.optimization_barrier(jnp.sum(q_points * q_points, axis=(1, 3)))
    k_square = lax.optimization_barrier(jnp.sum(k_points * k_points, axis=(1, 3)))
    distance = jnp.transpose(q_square)[:, :, None] + jnp.transpose(k_square)[:, None, :] - 2.0 * cross_pts
    pair_bias = jnp.einsum('qke,eh->hqk', pair_tile.astype(jnp.float32), w_bias.astype(jnp.float32), precision=PRECISE)
    cross_chain = (q_chain[:, None] != k_chain[None, :]).astype(jnp.float32)
    logits = LOGIT_WEIGHT * (qk_dots / math.sqrt(HEAD) + pair_bias) - point_scale[:, None, None] * distance
    logits = logits + chain_bias[:, None, None] * cross_chain[None, :, :]
    return jnp.where(k_mask[None, None, :] == 1, logits, jnp.float32(MASKED))

def weighted_sums(weights, kfeat, pair_tile):
    k_heads, v_heads, k_points, v_points = split_key(kfeat)
    n_query = weights.shape[1]
    totals = jnp.transpose(lax.optimization_barrier(jnp.sum(weights, axis=2)))
    num_v = jnp.einsum('hqk,khc->qhc', weights, v_heads, precision=PRECISE)
    weights_b = weights.astype(jnp.bfloat16)
    num_pair = jnp.einsum('hqk,qke->qhe', weights_b.astype(jnp.float32), pair_tile.astype(jnp.float32), precision=PRECISE)
    num_pt = jnp.einsum('hqk,kxhp->qxhp', weights, v_points, precision=PRECISE)
    return (totals, num_v.reshape(n_query, -1), num_pair.reshape(n_query, -1), num_pt.reshape(n_query, -1))

def readout(out_v, out_pair, out_pt, frames, w_out):
    row_count = out_v.shape[0]
    rotation, offset = rotations(frames)
    world_pts = out_pt.reshape(row_count, 3, H * PV) - offset[:, :, None]
    local_pts = to_local(rotation, world_pts)
    length = jnp.sqrt(lax.optimization_barrier(jnp.sum(local_pts * local_pts, axis=1)) + 1e-08)
    features = jnp.concatenate([out_v, out_pair, local_pts.reshape(row_count, -1), length], axis=1)
    return jnp.dot(features, w_out.astype(jnp.float32), precision=PRECISE)

def owner_step(own_sums, frames, w_out, d_update):
    totals, num_v, num_pair, num_pt = own_sums
    row_count = totals.shape[0]
    inv_total = 1.0 / totals
    out_v = (num_v.reshape(row_count, H, HEAD) * inv_total[:, :, None]).reshape(row_count, -1)
    out_pair = (num_pair.reshape(row_count, H, CP) * inv_total[:, :, None]).reshape(row_count, -1)
    out_pt = (num_pt.reshape(row_count, 3, H, PV) * inv_total[:, None, :, None]).reshape(row_count, -1)

    def readout_of(value_out, pair_out, point_out):
        return readout(value_out, pair_out, point_out, frames, w_out)
    update, pullback = jax.vjp(readout_of, out_v, out_pair, out_pt)
    d_out_v, d_out_pair, d_out_pt = pullback(d_update)
    delta = lax.optimization_barrier(jnp.sum((d_out_v * out_v).reshape(row_count, H, HEAD), axis=2))
    delta = delta + lax.optimization_barrier(jnp.sum((d_out_pair * out_pair).reshape(row_count, H, CP), axis=2))
    delta = delta + lax.optimization_barrier(jnp.sum((d_out_pt * out_pt).reshape(row_count, 3, H, PV), axis=(1, 3)))
    return (update, d_out_v, d_out_pair, d_out_pt, delta, inv_total)

def tile_grads(weights, inv_total, d_out_v, d_out_pair, d_out_pt, delta, qfeat, kfeat, pair_tile, w_bias, point_scale):
    n_query, n_key = (qfeat.shape[0], kfeat.shape[0])
    q_heads, q_points = split_query(qfeat)
    k_heads, v_heads, k_points, v_points = split_key(kfeat)
    attention = weights * jnp.transpose(inv_total)[:, :, None]
    grad_v = d_out_v.reshape(n_query, H, HEAD)
    grad_pair = d_out_pair.reshape(n_query, H, CP)
    grad_pt = d_out_pt.reshape(n_query, 3, H, PV)
    pair_wide = pair_tile.astype(jnp.float32)
    d_attention = jnp.einsum('qhc,khc->hqk', grad_v, v_heads, precision=PRECISE)
    d_attention = d_attention + jnp.einsum('qhe,qke->hqk', grad_pair, pair_wide, precision=PRECISE)
    d_attention = d_attention + jnp.einsum('qxhp,kxhp->hqk', grad_pt, v_points, precision=PRECISE)
    d_logits = attention * (d_attention - jnp.transpose(delta)[:, :, None])
    d_tile = jnp.einsum('hqk,qhe->qke', attention, grad_pair, precision=PRECISE)
    d_tile = d_tile + LOGIT_WEIGHT * jnp.einsum('hqk,eh->qke', d_logits, w_bias.astype(jnp.float32), precision=PRECISE)
    scale_qk = LOGIT_WEIGHT / math.sqrt(HEAD)
    grad_keys = scale_qk * jnp.einsum('hqk,qhc->khc', d_logits, q_heads, precision=PRECISE)
    grad_values = jnp.einsum('hqk,qhc->khc', attention, grad_v, precision=PRECISE)
    col_sum = jnp.transpose(lax.optimization_barrier(jnp.sum(d_logits, axis=1)))
    grad_kpts = 2.0 * point_scale[None, None, :, None] * (jnp.einsum('hqk,qxhp->kxhp', d_logits, q_points, precision=PRECISE) - col_sum[:, None, :, None] * k_points)
    grad_vpts = jnp.einsum('hqk,qxhp->kxhp', attention, grad_pt, precision=PRECISE)
    row_sum = jnp.transpose(lax.optimization_barrier(jnp.sum(d_logits, axis=2)))
    grad_query = scale_qk * jnp.einsum('hqk,khc->qhc', d_logits, k_heads, precision=PRECISE)
    grad_qpts = -2.0 * point_scale[None, None, :, None] * (row_sum[:, None, :, None] * q_points - jnp.einsum('hqk,kxhp->qxhp', d_logits, k_points, precision=PRECISE))
    key_part = jnp.concatenate([grad_keys.reshape(n_key, -1), grad_values.reshape(n_key, -1), grad_kpts.reshape(n_key, -1), grad_vpts.reshape(n_key, -1)], axis=1)
    query_part = jnp.concatenate([grad_query.reshape(n_query, -1), grad_qpts.reshape(n_query, -1)], axis=1)
    return (d_tile.astype(jnp.bfloat16), key_part, query_part)

def key_back(key_part, frames, w_key):
    row_count = key_part.shape[0]
    rotation, offset = rotations(frames)
    head_cols = 2 * H * HEAD
    key_pts = to_local(rotation, key_part[:, head_cols:head_cols + 3 * H * PQ].reshape(row_count, 3, H * PQ))
    value_pts = to_local(rotation, key_part[:, head_cols + 3 * H * PQ:].reshape(row_count, 3, H * PV))
    local_grad = jnp.concatenate([key_part[:, :head_cols], key_pts.reshape(row_count, -1), value_pts.reshape(row_count, -1)], axis=1)
    return jnp.dot(local_grad, jnp.transpose(w_key.astype(jnp.float32)), precision=PRECISE)

def query_back(query_part, frames, w_query):
    row_count = query_part.shape[0]
    rotation, offset = rotations(frames)
    query_pts = to_local(rotation, query_part[:, H * HEAD:].reshape(row_count, 3, H * PQ))
    local_grad = jnp.concatenate([query_part[:, :H * HEAD], query_pts.reshape(row_count, -1)], axis=1)
    return jnp.dot(local_grad, jnp.transpose(w_query.astype(jnp.float32)), precision=PRECISE)

def reference(q_single, k_single, q_frames, k_frames, pair_tile, w_query, w_key, w_bias, w_out, head_weight, chain_bias, q_chain, k_chain, k_mask, d_update):
    point_scale = coefficients(head_weight)
    qfeat_all = project_query(q_single, q_frames, w_query)
    kfeat_all = project_key(k_single, k_frames, w_key)

    def block_step(carry, block_index):
        start_row = (block_index * Q_DEV).astype(jnp.int32)
        qfeat = lax.dynamic_slice_in_dim(qfeat_all, start_row, Q_DEV, 0)
        pair_block = lax.dynamic_slice_in_dim(pair_tile, start_row, Q_DEV, 0)
        chain_block = lax.dynamic_slice_in_dim(q_chain, start_row, Q_DEV, 0)
        frame_block = lax.dynamic_slice_in_dim(q_frames, start_row, Q_DEV, 1)
        grad_block = lax.dynamic_slice_in_dim(d_update, start_row, Q_DEV, 0)
        logits = attend_logits(qfeat, kfeat_all, pair_block, w_bias, point_scale, chain_bias, chain_block, k_chain, k_mask)
        row_top = lax.optimization_barrier(jnp.max(logits, axis=2))
        weights = jnp.exp(logits - row_top[:, :, None])
        own_sums = weighted_sums(weights, kfeat_all, pair_block)
        update, d_out_v, d_out_pair, d_out_pt, delta, inv_total = owner_step(own_sums, frame_block, w_out, grad_block)
        d_tile, key_part, query_part = tile_grads(weights, inv_total, d_out_v, d_out_pair, d_out_pt, delta, qfeat, kfeat_all, pair_block, w_bias, point_scale)
        return (carry + key_part, (update, d_tile, query_part))
    block_count = QUERIES // Q_DEV
    start_carry = jnp.zeros((NRES, KF), qfeat_all.dtype)
    key_total, stacked = lax.scan(block_step, start_carry, jnp.arange(block_count, dtype=jnp.int32))
    updates, d_tiles, query_parts = stacked
    update = updates.reshape(QUERIES, CS).astype(jnp.bfloat16)
    d_pair = d_tiles.reshape(QUERIES, NRES, CP)
    d_query_single = query_back(query_parts.reshape(QUERIES, QF), q_frames, w_query).astype(jnp.bfloat16)
    d_key_single = key_back(key_total, k_frames, w_key)
    return (update, d_pair, d_query_single, d_key_single)
```

```python
import functools
import math

import jax
import jax.numpy as jnp
import numpy as np
from jax import lax
from jax.experimental import pallas as pl
from jax.experimental.pallas import tpu as pltpu
from jax.sharding import PartitionSpec as P

H = 12
HP = 16
HEAD = 16
PQ = 4
PV = 8
HC = H * HEAD
QP = 3 * H * PQ
VP = 3 * H * PV
QW = 384
PW = 384
MASKED = -1000000000.0
WL = math.sqrt(1.0 / 3.0)
F32 = jnp.float32
BF16 = jnp.bfloat16


def dot(a, b, ca=1, cb=0, precision=None):
    return lax.dot_general(
        a, b, (((ca,), (cb,)), ((), ())), precision=precision, preferred_element_type=F32
    )


def dot_full(a, b, ca=1, cb=0):
    return dot(a, b, ca, cb, lax.Precision.HIGHEST)


def split2(x):
    high = x.astype(BF16)
    return high, (x - high.astype(F32)).astype(BF16)


def split3(x):
    high = x.astype(BF16)
    rest = x - high.astype(F32)
    mid = rest.astype(BF16)
    return high, mid, (rest - mid.astype(F32)).astype(BF16)


def rows3(x, b, ca=1, cb=0):
    n = x.shape[0]
    out = dot(jnp.concatenate(split3(x), axis=0), b, ca, cb)
    return out[0:n] + out[n : 2 * n] + out[2 * n : 3 * n]


def pair3(a, b, ca=1, cb=0):
    ah, al = split2(a)
    bh, bl = split2(b)
    return dot(ah, bh, ca, cb) + (dot(ah, bl, ca, cb) + dot(al, bh, ca, cb))


def per_head(x, n):
    return jnp.broadcast_to(x[:, None, :], (n, HP, x.shape[1])).reshape(n * HP, x.shape[1])


def tiled(x, n):
    return jnp.broadcast_to(x[None], (n,) + x.shape).reshape(n * HP, x.shape[1])


def head_sum(x, n):
    return jnp.sum(x.reshape(n, HP, x.shape[1]), axis=1)


def frame_row(fr, index):
    return fr[index : index + 1, :]


def to_world(fr, loc, rows):
    out = []
    for x in range(3):
        acc = frame_row(fr, 9 + x) + frame_row(fr, 3 * x) * loc[0]
        for y in range(1, 3):
            acc = acc + frame_row(fr, 3 * x + y) * loc[y]
        out.append(acc)
    return out


def to_local(fr, g):
    out = []
    for y in range(3):
        acc = frame_row(fr, y) * g[0]
        for x in range(1, 3):
            acc = acc + frame_row(fr, 3 * x + y) * g[x]
        out.append(acc)
    return out


def three(x, rows):
    return [x[k * rows : (k + 1) * rows] for k in range(3)]


def transpose_tiles(dst, src, tiles):
    for t in range(tiles):
        dst[t * 128 : (t + 1) * 128, :] = jnp.transpose(src[:, t * 128 : (t + 1) * 128])


def soft_coef(head_weight):
    return WL * jax.nn.softplus(head_weight) * math.sqrt(2.0 / (9.0 * PQ)) / 2.0


def constants(ni, ka, oq, slot):
    perm = np.zeros((2 * ni, ka * slot), np.float32)
    for i in range(ni):
        perm[i, (i // oq) * slot + i % oq] = 1.0
        perm[ni + i, (i // oq) * slot + oq + i % oq] = 1.0
    expand = np.zeros((128, ni * HP), np.float32)
    heads = np.zeros((HP, ni * HP), np.float32)
    for i in range(ni):
        expand[i, i * HP : (i + 1) * HP] = 1.0
        for h in range(HP):
            heads[h, i * HP + h] = 1.0
    mq = np.zeros((HP, QW), np.float32)
    for h in range(H):
        mq[h, h * HEAD : (h + 1) * HEAD] = 1.0
        for x in range(3):
            base = HC + x * H * PQ + h * PQ
            mq[h, base : base + PQ] = 1.0
    mv = np.zeros((HP, 256), np.float32)
    mp = np.zeros((HP, PW), np.float32)
    for h in range(H):
        mv[h, h * HEAD : (h + 1) * HEAD] = 1.0
        for x in range(3):
            base = x * H * PV + h * PV
            mp[h, base : base + PV] = 1.0
    stat = np.zeros((HP, 128), np.float32)
    stats = np.zeros((2, HP, PW), np.float32)
    for h in range(HP):
        stat[h, h] = 1.0
        for k in range(2):
            stats[k, h, VP + k * HP + h] = 1.0
    spread = np.zeros((128, PW), np.float32)
    for h in range(H):
        spread[VP + h - 256] = mp[h] + stats[0, h] + stats[1, h]
    return dict(
        perm=perm, expand=expand, heads=heads, mq=mq, mv=mv, mp=mp, stat=stat, stats=stats,
        spread=spread,
    )


def query_kernel(
    ni, ka, slot, n_pieces, meta, *refs
):
    pieces = refs[:n_pieces]
    (pair, w_query, w_out, wb_t, perm, bias_o, dap_o, g_o, q_o, qt_o, dv_o, dvt_o, dlt_o, frt_o,
     qd, nat, dnat) = refs[n_pieces:]
    me = meta[0]
    chip, core = me // 2, lax.rem(me, 2)
    for d in range(n_pieces):
        for e in range(2):
            owner = (chip ^ d) * 2 + (core ^ e)
            qd[pl.ds(pl.multiple_of(owner * slot, 8), slot), :] = pieces[d][e]
    rows = dot_full(perm[...], qd[...])
    width = w_query.shape[0]
    q_raw, d_up = rows[:ni, :width], rows[ni:, :width]
    nat[...] = jnp.zeros_like(nat)
    nat[0:ni, 0:128] = rows[:ni, width : width + 128]
    frt_o[...] = jnp.transpose(nat[:, 0:128])
    fr = frt_o[...]
    nat[0:ni, 0 : HC + QP] = rows3(q_raw, w_query[...])
    transpose_tiles(qt_o, nat, QW // 128)
    rp = H * PQ
    world = to_world(fr, three(qt_o[HC : HC + QP, :], rp), rp)
    for x in range(3):
        qt_o[HC + x * rp : HC + (x + 1) * rp, :] = world[x]
    for t in range(QW // 128):
        nat[:, t * 128 : (t + 1) * 128] = jnp.transpose(qt_o[t * 128 : (t + 1) * 128, :])
    q_o[...] = nat[0:ni, :]
    split = jnp.concatenate(split3(d_up), axis=0)

    def d_out(lo, hi):
        out = dot(split, w_out[lo:hi, :], 1, 1)
        return out[0:ni] + out[ni : 2 * ni] + out[2 * ni : 3 * ni]

    dnat[...] = jnp.zeros_like(dnat)
    dnat[0:ni, 0:HC] = d_out(0, HC)
    dv_o[...] = dnat[0:ni, 0:256]
    transpose_tiles(dvt_o, dnat, 2)
    cp = pair.shape[2]
    first = HC + H * cp
    dnat[0:ni, :] = d_out(first, first + VP + H * PV)
    transpose_tiles(dlt_o, dnat, 3)
    g_o[...] = jnp.zeros_like(g_o)
    for h in range(H):
        g_o[pl.ds(h, ni, stride=HP), :] = d_out(HC + h * cp, HC + (h + 1) * cp)
    for i in range(ni):
        gh, gl = split2(g_o[i * HP : (i + 1) * HP, :])
        out = dot(jnp.concatenate([wb_t[...], gh, gl], axis=0), pair[i], 1, 1)
        bias_o[i * HP : (i + 1) * HP, :] = out[0:HP]
        dap_o[i * HP : (i + 1) * HP, :] = out[HP : 2 * HP] + out[2 * HP : 3 * HP]


def key_kernel(
    ni, nk, pieces_n, meta, q_chain, *refs
):
    pieces = refs[:pieces_n]
    (w_key, q_feat, dv, bias, coef_c, chain_c, k_chain, k_mask, mq, mv, stat,
     lg_o, dav_o, top_o, kq_o, vt_o, kfr_o, kraw, knat, kt) = refs[pieces_n:]
    pb = meta[1]
    for s in range(pieces_n):
        m = lax.rem(pb // 2 - s + pieces_n, pieces_n)
        for e in range(2):
            owner = m * 2 + (lax.rem(pb, 2) ^ e)
            kraw[pl.ds(pl.multiple_of(owner * nk, 8), nk), :] = pieces[s][e]
    width = w_key.shape[0]
    kfr_o[...] = jnp.transpose(kraw[:, width : width + 128])
    fr = kfr_o[...]
    knat[:, 0 : w_key.shape[1]] = rows3(kraw[:, 0:width], w_key[...])
    transpose_tiles(kt, knat, knat.shape[1] // 128)
    rk, rv = H * PQ, H * PV
    kp = to_world(fr, three(kt[2 * HC : 2 * HC + QP, :], rk), rk)
    vp = to_world(fr, three(kt[2 * HC + QP : 2 * HC + QP + VP, :], rv), rv)
    kq_o[0:HC, :] = kt[0:HC, :]
    vt_o[0:HC, :] = kt[HC : 2 * HC, :]
    for x in range(3):
        kq_o[HC + x * rk : HC + (x + 1) * rk, :] = kp[x]
        vt_o[HC + x * rv : HC + (x + 1) * rv, :] = vp[x]
    kq_o[HC + QP :, :] = jnp.zeros_like(kq_o[HC + QP :, :])
    vt_o[HC + VP :, :] = jnp.zeros_like(vt_o[HC + VP :, :])
    lane = lax.broadcasted_iota(jnp.int32, (HP, QW), 1)
    is_pt = lane >= HC
    scale = mq[...] * jnp.where(is_pt, 2.0 * coef_c[:, 0:1], WL / math.sqrt(HEAD))
    q_rows = per_head(q_feat[...], ni)
    left = q_rows * tiled(scale, ni)
    q_sq = jnp.sum(
        q_rows * q_rows * tiled(mq[...] * jnp.where(is_pt, coef_c[:, 0:1], 0.0), ni),
        axis=1, keepdims=True,
    )
    kpt = kq_o[HC : HC + QP, :]
    k_sq = dot_full(mq[:, HC : HC + QP] * coef_c[:, 0:1], kpt * kpt)
    logits = dot_full(left, kq_o[...]) + WL * bias[...] - q_sq - tiled(k_sq, ni)
    cross = jnp.concatenate(
        [
            jnp.where(k_chain[...] != q_chain[i], chain_c[...], 0.0)
            for i in range(ni)
        ],
        axis=0,
    )
    logits = logits + cross
    logits = jnp.where(k_mask[...] == 1, logits, MASKED)
    lg_o[...] = logits
    top = jnp.max(logits, axis=1, keepdims=True)
    top_o[...] = head_sum(top * tiled(stat[...], ni), ni)
    dvm = per_head(dv[...], ni) * tiled(mv[...], ni)
    dav_o[...] = pair3(dvm, vt_o[0:256, :])


def weight_kernel(ni, logits, tops, dav, dap, vt, mp, stats, stat, w_o, pay_o):
    top = jnp.sum(per_head(tops[...], ni) * tiled(stat[...], ni), axis=1, keepdims=True)
    weights = jnp.exp(logits[...] - top)
    w_o[...] = weights
    total = jnp.sum(weights, axis=1, keepdims=True)
    rounded = weights.astype(BF16).astype(F32)
    s_sum = jnp.sum(weights * dav[...] + rounded * dap[...], axis=1, keepdims=True)
    num = pair3(weights, vt[HC : HC + PW, :], 1, 1)
    num = num * tiled(mp[...], ni)
    num = num + total * tiled(stats[0], ni) + s_sum * tiled(stats[1], ni)
    pay_o[...] = head_sum(num, ni)


def value_kernel(ni, w, pair, vt, mv, np_o, nv_o):
    for i in range(ni):
        np_o[i * HP : (i + 1) * HP, :] = dot(
            w[i * HP : (i + 1) * HP, :].astype(BF16), pair[i], 1, 0
        )
    nv_o[...] = pair3(w[...], vt[0:256, :], 1, 1) * tiled(mv[...], ni)


def grad_kernel(
    ni, oq, meta, pay, w, dav, dap, g, q_feat, qt, dv, dvt, dlt, frt, kq, vt, kfr,
    n_pair, n_v, coef_c, mq, mv, mp, stats, spread, expand, heads, w_out, w_key, w_query,
    a_o, dl_o, ka_o, key_o, nat, tr, knat, kt, npx,
):
    me = meta[0]
    fr = frt[...]
    totals = dot_full(pay[:, 256:384], spread[...])
    inv = jnp.where(totals > 0.0, 1.0 / totals, 0.0)
    f_col = jnp.sum(per_head(inv, ni) * tiled(stats[0], ni), axis=1, keepdims=True)
    att = w[...] * f_col
    a_o[...] = att
    scaled = pay[...] * inv
    nat[...] = jnp.zeros_like(nat)
    nat[0:ni, :] = scaled
    transpose_tiles(tr, nat, 3)
    rv = H * PV
    out_pt = three(tr[0:VP, :], rv)
    shifted = [out_pt[x] - frame_row(fr, 9 + x) for x in range(3)]
    loc = to_local(fr, shifted)
    length = jnp.sqrt(loc[0] * loc[0] + loc[1] * loc[1] + loc[2] * loc[2] + 1e-08)
    ratio = dlt[VP : VP + rv, :] / length
    d_loc = [dlt[y * rv : (y + 1) * rv, :] + ratio * loc[y] for y in range(3)]
    d_pt = []
    for x in range(3):
        acc = frame_row(fr, 3 * x) * d_loc[0]
        for y in range(1, 3):
            acc = acc + frame_row(fr, 3 * x + y) * d_loc[y]
        d_pt.append(acc)
    for y in range(3):
        tr[y * rv : (y + 1) * rv, :] = loc[y]
    tr[VP : VP + rv, :] = length
    for t in range(3):
        nat[:, t * 128 : (t + 1) * 128] = jnp.transpose(tr[t * 128 : (t + 1) * 128, :])
    cp = g.shape[1]
    first = HC + H * cp
    own = rows3(nat[0:ni, :], w_out[first : first + PW, :])
    row = lax.broadcasted_iota(jnp.int32, (ni, 1), 0)
    upd = jnp.where((row >= me * oq) & (row < (me + 1) * oq), own, 0.0)
    for x in range(3):
        tr[x * rv : (x + 1) * rv, :] = d_pt[x]
    tr[VP:, :] = jnp.zeros_like(tr[VP:, :])
    d_pt_t = tr[0:VP, :]
    for t in range(3):
        nat[:, t * 128 : (t + 1) * 128] = jnp.transpose(tr[t * 128 : (t + 1) * 128, :])
    d_nat = nat[0:ni, :]
    lane = lax.broadcasted_iota(jnp.int32, (ni, PW), 1)
    dots = jnp.where(lane < VP, d_nat * scaled, scaled)
    delta = jnp.sum(per_head(dots, ni) * tiled(mp[...] + stats[1], ni), axis=1, keepdims=True)
    dptm = per_head(d_nat, ni) * tiled(mp[...], ni)
    d_att = dav[...] + dap[...] + pair3(dptm, vt[HC : HC + PW, :])
    dl = att * (d_att - delta)
    dl_o[...] = dl
    npx[...] = n_pair[...] * f_col
    upd = upd + rows3(head_sum(n_v[...] * f_col, ni)[:, 0:HC], w_out[0:HC, :])
    for h in range(H):
        part = npx[pl.ds(h, ni, stride=HP), :]
        upd = upd + rows3(part, w_out[HC + h * cp : HC + (h + 1) * cp, :])
    lane_h = lax.broadcasted_iota(jnp.int32, (HP, QW), 1)
    is_pt = lane_h >= HC
    scale = mq[...] * jnp.where(is_pt, 2.0 * coef_c[:, 0:1], WL / math.sqrt(HEAD))
    row_sum = jnp.sum(dl, axis=1, keepdims=True)
    gq = pair3(dl, kq[...], 1, 1) - per_head(jnp.where(lane >= HC, q_feat[...], 0.0), ni) * row_sum
    nat[0:ni, :] = head_sum(gq * tiled(scale, ni), ni)
    nat[ni:, :] = jnp.zeros_like(nat[ni:, :])
    transpose_tiles(tr, nat, 3)
    rq = H * PQ
    gl = to_local(fr, three(tr[HC : HC + QP, :], rq))
    for x in range(3):
        tr[HC + x * rq : HC + (x + 1) * rq, :] = gl[x]
    for t in range(3):
        nat[:, t * 128 : (t + 1) * 128] = jnp.transpose(tr[t * 128 : (t + 1) * 128, :])
    d_query = rows3(nat[0:ni, 0 : HC + QP], w_query[...], 1, 1)
    width = w_query.shape[0]
    ka_o[:, 0:width] = upd
    ka_o[:, width : 2 * width] = d_query
    mask_all = dot_full(scale, heads[...], 0, 0)
    e = expand[...]
    lt = dot_full(qt[...], e) * mask_all
    kt[0:HC, :] = pair3(lt[0:HC], dl)
    gk = pair3(lt[HC : HC + QP], dl)
    col_sum = jnp.sum(dl.reshape(ni, HP, dl.shape[1]), axis=0)
    col = dot_full(scale[:, HC : HC + QP], col_sum, 0, 0)
    gk = gk - col * kq[HC : HC + QP, :]
    dvm = dot_full(dvt[0:HC, :], e) * dot_full(mv[:, 0:HC], heads[...], 0, 0)
    kt[HC : 2 * HC, :] = pair3(dvm, att)
    dpm = dot_full(d_pt_t, e) * dot_full(mp[:, 0:VP], heads[...], 0, 0)
    gv = pair3(dpm, att)
    kf = kfr[...]
    gkl = to_local(kf, three(gk, rq))
    gvl = to_local(kf, three(gv, rv))
    for x in range(3):
        kt[2 * HC + x * rq : 2 * HC + (x + 1) * rq, :] = gkl[x]
        kt[2 * HC + QP + x * rv : 2 * HC + QP + (x + 1) * rv, :] = gvl[x]
    for t in range(kt.shape[0] // 128):
        knat[:, t * 128 : (t + 1) * 128] = jnp.transpose(kt[t * 128 : (t + 1) * 128, :])
    key_o[...] = rows3(knat[:, 0 : w_key.shape[1]], w_key[...], 1, 1)


def pair_kernel(ni, att, dl, g, wb_t, out):
    for i in range(ni):
        sl = slice(i * HP, (i + 1) * HP)
        ah, al = split2(att[sl, :])
        dh, dlo = split2(dl[sl, :] * WL)
        gh, gl = split2(g[sl, :])
        left = jnp.concatenate([ah, al, ah, dh, dlo], axis=0)
        right = jnp.concatenate([gh, gh, gl, wb_t[...], wb_t[...]], axis=0)
        out[i] = dot(left, right, 0, 0).astype(BF16)


def call(kernel, outs, args, smem=1, scratch=(), name=None):
    return pl.pallas_call(
        kernel,
        out_shape=[jax.ShapeDtypeStruct(s, d) for s, d in outs],
        in_specs=[pl.BlockSpec(memory_space=pltpu.SMEM)] * smem
        + [pl.BlockSpec(memory_space=pltpu.VMEM)] * (len(args) - smem),
        out_specs=[pl.BlockSpec(memory_space=pltpu.VMEM)] * len(outs),
        scratch_shapes=[pltpu.VMEM(s, d) for s, d in scratch],
        compiler_params=pltpu.CompilerParams(vmem_limit_bytes=48 * 1024 * 1024),
        name=name,
    )(*args)


def local(
    q_single, k_single, q_frames, k_frames, pair_tile, w_query, w_key, w_bias, w_out,
    head_weight, chain_bias, q_chain, k_chain, k_mask, d_update,
):
    pbc = lax.axis_size("pb")
    kac = lax.axis_size("ka")
    pb = lax.axis_index("pb")
    ka = lax.axis_index("ka")
    ni, nj, cp = pair_tile.shape
    oq, width = q_single.shape
    nk = k_single.shape[0]
    slot = -(-2 * oq // 8) * 8
    c = {k: jnp.asarray(v) for k, v in constants(ni, kac, oq, slot).items()}
    meta = jnp.stack([ka, pb]).astype(jnp.int32)
    coef = jnp.pad(soft_coef(head_weight), (0, HP - H))
    coef_c = jnp.broadcast_to(coef[:, None], (HP, 128))
    chain_c = jnp.broadcast_to(jnp.pad(chain_bias, (0, HP - H))[:, None], (HP, nj))
    wb_t = jnp.pad(jnp.transpose(w_bias), ((0, HP - H), (0, 0)))

    def ka_xor(x, d):
        return lax.ppermute(x, "ka", [(i, i ^ d) for i in range(kac)])

    def pb_xor(x, d):
        return lax.ppermute(x, "pb", [(i, i ^ d) for i in range(pbc)])

    def with_frames(x, fr):
        fr_t = jnp.pad(jnp.transpose(fr), ((0, 0), (0, 128 - 12)))
        return jnp.concatenate([x, fr_t], axis=1)

    tail = jnp.zeros((slot - 2 * oq, width + 128), F32)
    pack = jnp.concatenate(
        [
            with_frames(k_single, k_frames),
            with_frames(q_single, q_frames),
            jnp.pad(d_update, ((0, 0), (0, 128))),
            tail,
        ],
        axis=0,
    )
    other = ka_xor(pack, 1)
    k2 = jnp.stack([pack[:nk], other[:nk]])
    q2 = jnp.stack([pack[nk:], other[nk:]])
    half = pbc // 2
    key_pieces = []
    for s in range(half):
        table = []
        for p in range(pbc):
            for a in range(kac):
                chip = (p * kac + a) // 2
                block, m = chip // half, chip % half
                target = 2 * ((m + s) % half) + a % 2
                table.append((p * kac + a, target * kac + block))
        key_pieces.append(lax.ppermute(k2, ("pb", "ka"), table))
    query_pieces = [q2] + [ka_xor(q2, 2 * d) for d in range(1, kac // 2)]

    n_row = ni * HP
    f32 = lambda *s: (s, F32)
    bias, dap, g, q_feat, qt, dv, dvt, dlt, frt = call(
        functools.partial(query_kernel, ni, kac, slot, kac // 2),
        [f32(n_row, nj), f32(n_row, nj), f32(n_row, cp), f32(ni, QW), f32(QW, 128),
         f32(ni, 256), f32(256, 128), f32(384, 128), f32(128, 128)],
        [meta, *query_pieces, pair_tile, w_query, w_out, wb_t, c["perm"]],
        smem=1,
        scratch=[f32(kac * slot, width + 128), f32(128, QW), f32(128, 384)],
        name="query",
    )
    logits, dav, tops, kq, vt, kfr = call(
        functools.partial(key_kernel, ni, nk, half),
        [f32(n_row, nj), f32(n_row, nj), f32(ni, 128), f32(QW, nj), f32(HC + PW, nj),
         f32(128, nj)],
        [meta, q_chain, *key_pieces, w_key, q_feat, dv, bias, coef_c, chain_c,
         k_chain[None, :], k_mask[None, :], c["mq"], c["mv"], c["stat"]],
        smem=2,
        scratch=[f32(nj, width + 128), f32(nj, 896), f32(896, nj)],
        name="key",
    )
    step = 1
    while step < kac:
        tops = jnp.maximum(tops, ka_xor(tops, step))
        step *= 2
    weights, total = call(
        functools.partial(weight_kernel, ni),
        [f32(n_row, nj), f32(ni, PW)],
        [logits, tops, dav, dap, vt, c["mp"], c["stats"], c["stat"]],
        smem=0,
        name="weight",
    )
    n_pair, n_v = call(
        functools.partial(value_kernel, ni),
        [f32(n_row, cp), f32(n_row, 256)],
        [weights, pair_tile, vt, c["mv"]],
        smem=0,
        name="value",
    )
    step = 1
    while step < kac:
        total = total + ka_xor(total, step)
        step *= 2
    att, dl, part, key_part = call(
        functools.partial(grad_kernel, ni, oq),
        [f32(n_row, nj), f32(n_row, nj), f32(ni, 2 * width), f32(nj, width)],
        [meta, total, weights, dav, dap, g, q_feat, qt, dv, dvt, dlt, frt, kq, vt, kfr,
         n_pair, n_v, coef_c, c["mq"], c["mv"], c["mp"], c["stats"], c["spread"],
         c["expand"], c["heads"], w_out, w_key, w_query],
        smem=1,
        scratch=[f32(128, 384), f32(384, 128), f32(nj, 896), f32(896, nj), f32(n_row, cp)],
        name="grad",
    )
    (d_pair,) = call(
        functools.partial(pair_kernel, ni),
        [((ni, nj, cp), BF16)],
        [att, dl, g, wb_t],
        smem=0,
        name="pair",
    )

    split = part.reshape(kac // 2, 2, oq, 2 * width)
    core = ka % 2
    mine = lax.dynamic_index_in_dim(split, core, 1, keepdims=False)
    theirs = lax.dynamic_index_in_dim(split, 1 - core, 1, keepdims=False)
    mine = mine + ka_xor(theirs, 1)
    chip = ka // 2
    own = lax.dynamic_index_in_dim(mine, chip, 0, keepdims=False)
    for d in range(1, kac // 2):
        own = own + ka_xor(lax.dynamic_index_in_dim(mine, chip ^ d, 0, keepdims=False), 2 * d)
    blocks = key_part.reshape(pbc, nj // pbc, width)
    key_own = lax.dynamic_index_in_dim(blocks, pb, 0, keepdims=False)
    for d in range(1, pbc):
        key_own = key_own + pb_xor(
            lax.dynamic_index_in_dim(blocks, pb ^ d, 0, keepdims=False), d
        )
    return (
        own[:, :width].astype(BF16),
        d_pair,
        own[:, width:].astype(BF16),
        key_own,
    )


def solution(mesh):
    both = ("pb", "ka")
    placed = (
        P(both, None), P(both, None), P(None, both), P(None, both), P("pb", "ka", None),
        P(), P(), P(), P(), P(), P(), P("pb"), P("ka"), P("ka"), P(both, None),
    )
    return jax.shard_map(
        local,
        mesh=mesh,
        in_specs=placed,
        out_specs=(
            P(both, None), P("pb", "ka", None), P(both, None), P(("ka", "pb"), None),
        ),
        check_vma=False,
    )
```

```python
import functools
import math

import jax
import jax.numpy as jnp
from jax import lax
from jax.experimental import pallas as pl
from jax.experimental.pallas import tpu as pltpu
from jax.sharding import PartitionSpec as P

H = 12
HP = 16
HEAD = 16
PQ = 4
PV = 8
HC = H * HEAD
QP = 3 * H * PQ
VP = 3 * H * PV
QW = 384
PW = 384
MASKED = -1000000000.0
WL = math.sqrt(1.0 / 3.0)
F32 = jnp.float32
BF16 = jnp.bfloat16


def dot(a, b, ca=1, cb=0, precision=None):
    return lax.dot_general(
        a, b, (((ca,), (cb,)), ((), ())), precision=precision, preferred_element_type=F32
    )


def dot_full(a, b, ca=1, cb=0):
    return dot(a, b, ca, cb, lax.Precision.HIGHEST)


def split2(x):
    high = x.astype(BF16)
    return high, (x - high.astype(F32)).astype(BF16)


def split3(x):
    high = x.astype(BF16)
    rest = x - high.astype(F32)
    mid = rest.astype(BF16)
    return high, mid, (rest - mid.astype(F32)).astype(BF16)


def rows3(x, b, ca=1, cb=0):
    n = x.shape[0]
    out = dot(jnp.concatenate(split3(x), axis=0), b, ca, cb)
    return out[0:n] + out[n : 2 * n] + out[2 * n : 3 * n]


def rows2(x, b, ca=1, cb=0):
    n = x.shape[0]
    out = dot(jnp.concatenate(split2(x), axis=0), b, ca, cb)
    return out[0:n] + out[n : 2 * n]


def pair3(a, b, ca=1, cb=0):
    ah, al = split2(a)
    bh, bl = split2(b)
    return dot(ah, bh, ca, cb) + (dot(ah, bl, ca, cb) + dot(al, bh, ca, cb))


def per_head(x, n):
    return jnp.broadcast_to(x[:, None, :], (n, HP, x.shape[1])).reshape(n * HP, x.shape[1])


def tiled(x, n):
    return jnp.broadcast_to(x[None], (n,) + x.shape).reshape(n * HP, x.shape[1])


def head_sum(x, n):
    return jnp.sum(x.reshape(n, HP, x.shape[1]), axis=1)


def frame_row(fr, index):
    return fr[index : index + 1, :]


def to_world(fr, loc, rows):
    out = []
    for x in range(3):
        acc = frame_row(fr, 9 + x) + frame_row(fr, 3 * x) * loc[0]
        for y in range(1, 3):
            acc = acc + frame_row(fr, 3 * x + y) * loc[y]
        out.append(acc)
    return out


def to_local(fr, g):
    out = []
    for y in range(3):
        acc = frame_row(fr, y) * g[0]
        for x in range(1, 3):
            acc = acc + frame_row(fr, 3 * x + y) * g[x]
        out.append(acc)
    return out


def three(x, rows):
    return [x[k * rows : (k + 1) * rows] for k in range(3)]


def transpose_tiles(dst, src, tiles):
    for t in range(tiles):
        dst[t * 128 : (t + 1) * 128, :] = jnp.transpose(src[:, t * 128 : (t + 1) * 128])


def column(row, n):
    at = lax.broadcasted_iota(jnp.int32, (HP, n), 0) == lax.broadcasted_iota(
        jnp.int32, (HP, n), 1
    )
    return jnp.sum(jnp.where(at, jnp.broadcast_to(row, (HP, n)), 0.0), axis=1, keepdims=True)


def coefficient(head_weight):
    x = head_weight[...]
    soft = jnp.maximum(x, 0.0) + jnp.log1p(jnp.exp(-jnp.abs(x)))
    return column(WL * soft * math.sqrt(2.0 / (9.0 * PQ)) / 2.0, H)


def rows_mask(blocks, width):
    parts = []
    for rows, shift in blocks:
        head = lax.broadcasted_iota(jnp.int32, (rows, width), 0) >> shift
        parts.append(head == (lax.broadcasted_iota(jnp.int32, (rows, width), 1) & (HP - 1)))
    return parts


def expand_rows(x, blocks, expand):
    keep = rows_mask(blocks, expand.shape[1])
    out = []
    for part in split2(x):
        wide = dot(part, expand)
        pieces, start = [], 0
        for (rows, _), mask in zip(blocks, keep):
            pieces.append(jnp.where(mask, wide[start : start + rows], 0.0).astype(BF16))
            start += rows
        out.append(jnp.concatenate(pieces, axis=0))
    return out


Q_BLOCKS = ((HC, 4),) + ((H * PQ, 2),) * 3
V_BLOCKS = ((HC, 4),)
P_BLOCKS = ((H * PV, 3),) * 3


def grid(shape):
    return tuple(lax.broadcasted_iota(jnp.int32, shape, d) for d in range(2))


def lanes_of(shape, row, blocks):
    lane = lax.broadcasted_iota(jnp.int32, shape, 1)
    keep = None
    for first, count, shift in blocks:
        hit = (lane >= first) & (lane < first + count) & (((lane - first) >> shift) == row)
        keep = hit if keep is None else keep | hit
    return keep


Q_LANES = ((0, HC, 4),) + tuple((HC + x * H * PQ, H * PQ, 2) for x in range(3))
V_LANES = ((0, HC, 4),)
P_LANES = tuple((x * H * PV, H * PV, 3) for x in range(3))


def head_mask(width, blocks):
    shape = (HP, width)
    return lanes_of(shape, grid(shape)[0], blocks).astype(F32)


def stat_mask(width, first):
    row, lane = grid((HP, width))
    return (lane == row + first).astype(F32)


def spread_mask():
    shape = (128, PW)
    head = grid(shape)[0] - (VP - 256)
    lane = grid(shape)[1]
    keep = lanes_of(shape, head, P_LANES) | (lane == head + VP) | (lane == head + VP + HP)
    return (keep & (head >= 0) & (head < H)).astype(F32)


def expand_mask(ni):
    row, lane = grid((ni, ni * HP))
    return ((lane // HP) == row).astype(BF16)


def row_order(ni, ka, oq, slot):
    row, lane = grid((2 * ni, ka * slot))
    shift = oq.bit_length() - 1
    index = row & (ni - 1)
    source = (index >> shift) * slot + (index & (oq - 1))
    return (lane == source + jnp.where(row >= ni, oq, 0)).astype(F32)


class Fetched:
    def __init__(self, src, dst, sem):
        self.ref, self.pending = dst, pltpu.make_async_copy(src, dst, sem)
        self.shape = dst.shape
        self.pending.start()

    def get(self):
        if self.pending is not None:
            self.pending.wait()
            self.pending = None
        return self.ref

    def __getitem__(self, index):
        return self.get()[index]


def pack_kernel(pbc, k, kf, q, qf, du, pk, pq):
    nk, width = k.shape
    oq = q.shape[0]
    spot = lax.rem(lax.axis_index("ka"), pbc)
    for t in range(width // 128):
        pk[t * nk : (t + 1) * nk, :] = k[:, t * 128 : (t + 1) * 128]
    row = lax.broadcasted_iota(jnp.int32, (nk, 128), 0)
    lane = lax.broadcasted_iota(jnp.int32, (nk, 128), 1)
    pk[width // 128 * nk :, :] = jnp.zeros_like(pk[width // 128 * nk :, :])
    pk[width // 128 * nk : width // 128 * nk + 12, :] = dot_full(
        kf[...], (lane == row + spot * nk).astype(F32)
    )
    pq[...] = jnp.zeros_like(pq)
    pq[0:oq, 0:width] = q[...]
    pq[0:oq, width : width + 12] = qf[...]
    pq[oq : 2 * oq, 0:width] = du[...]


def route_kernel(pbc, *refs):
    pieces, rest = refs[:pbc], refs[pbc:]
    held = rest[-1]
    chips = (len(rest) - pbc - 2)
    rows, outs, gathered = rest[:chips], rest[chips : chips + pbc], rest[chips + pbc]
    spot = lax.rem(lax.axis_index("ka"), pbc)
    mine = lax.axis_index("pb")
    for d in range(pbc):
        held[d] = pieces[d][...]
    for s in range(pbc):
        outs[s][...] = held[(spot ^ s) ^ mine]
    for d in range(chips):
        gathered[d] = rows[d][...]


def query_kernel(ni, ka, oq, slot, *refs):
    pieces = refs[:2]
    (pair, w_query_t, w_out, w_bias_t, bias_o, dap_o, g_o, q_o, qt_o, dv_o, dvt_o, dlt_o,
     frt_o, wb_o, qd, nat, dnat) = refs[2:]
    me = lax.axis_index("ka")
    chip, core = me // 2, lax.rem(me, 2)
    for d in range(ka // 2):
        for e in range(2):
            owner = (chip ^ d) * 2 + (core ^ e)
            qd[pl.ds(pl.multiple_of(owner * slot, 8), slot), :] = pieces[e][d]
    wb_o[...] = jnp.zeros_like(wb_o)
    wb_o[0:H, :] = w_bias_t[...].astype(F32)
    wb_t = wb_o[...].astype(BF16)
    rows = dot_full(row_order(ni, ka, oq, slot), qd[...])
    width = w_query_t.shape[1]
    q_raw, d_up = rows[:ni, :width], rows[ni:, :width]
    nat[...] = jnp.zeros_like(nat)
    nat[0:ni, 0:128] = rows[:ni, width : width + 128]
    frt_o[...] = jnp.transpose(nat[:, 0:128])
    fr = frt_o[...]
    nat[0:ni, 0 : HC + QP] = rows3(q_raw, w_query_t[...], 1, 1)
    transpose_tiles(qt_o, nat, QW // 128)
    rp = H * PQ
    world = to_world(fr, three(qt_o[HC : HC + QP, :], rp), rp)
    for x in range(3):
        qt_o[HC + x * rp : HC + (x + 1) * rp, :] = world[x]
    for t in range(QW // 128):
        nat[:, t * 128 : (t + 1) * 128] = jnp.transpose(qt_o[t * 128 : (t + 1) * 128, :])
    q_o[...] = nat[0:ni, :]
    split = jnp.concatenate(split3(d_up), axis=0)

    def d_out(lo, hi):
        out = dot(split, w_out[lo:hi, :], 1, 1)
        return out[0:ni] + out[ni : 2 * ni] + out[2 * ni : 3 * ni]

    dnat[...] = jnp.zeros_like(dnat)
    dnat[0:ni, 0:HC] = d_out(0, HC)
    dv_o[...] = dnat[0:ni, 0:256]
    transpose_tiles(dvt_o, dnat, 2)
    cp = pair.shape[2]
    first = HC + H * cp
    dnat[0:ni, :] = d_out(first, first + VP + H * PV)
    transpose_tiles(dlt_o, dnat, 3)
    g_o[...] = jnp.zeros_like(g_o)
    for h in range(H):
        g_o[pl.ds(h, ni, stride=HP), :] = d_out(HC + h * cp, HC + (h + 1) * cp)
    for i in range(ni):
        gh, gl = split2(g_o[i * HP : (i + 1) * HP, :])
        out = dot(jnp.concatenate([wb_t, gh, gl], axis=0), pair[i], 1, 1)
        bias_o[i * HP : (i + 1) * HP, :] = out[0:HP]
        dap_o[i * HP : (i + 1) * HP, :] = out[HP : 2 * HP] + out[2 * HP : 3 * HP]


def key_kernel(ni, nk, n_pieces, q_chain, *refs):
    pieces = refs[:n_pieces]
    (w_key_t, q_feat, dv, bias, head_weight, chain_bias, k_chain, k_mask,
     lg_o, dav_o, top_o, kq_o, vt_o, kfr_o, coef_o, kraw, kt) = refs[n_pieces:]
    chip = lax.axis_index("ka") // 2
    width = w_key_t.shape[1]
    tiles = width // 128
    fr = None
    for s in range(n_pieces):
        start = pl.multiple_of((chip ^ s) * nk, 8)
        for t in range(tiles):
            kraw[pl.ds(start, nk), t * 128 : (t + 1) * 128] = pieces[s][t * nk : (t + 1) * nk, :]
        part = pieces[s][tiles * nk : tiles * nk + 16, :]
        fr = part if fr is None else fr + part
    kfr_o[...] = fr
    parts = split3(kraw[...])
    w_t = w_key_t[...]
    kt[...] = dot(w_t, parts[0], 1, 1) + (dot(w_t, parts[1], 1, 1) + dot(w_t, parts[2], 1, 1))
    coef = coefficient(head_weight)
    coef_o[...] = jnp.broadcast_to(coef, coef_o.shape)
    chain = column(chain_bias[...], H)
    rk, rv = H * PQ, H * PV
    kp = to_world(fr, three(kt[2 * HC : 2 * HC + QP, :], rk), rk)
    vp = to_world(fr, three(kt[2 * HC + QP : 2 * HC + QP + VP, :], rv), rv)
    kq_o[0:HC, :] = kt[0:HC, :]
    vt_o[0:HC, :] = kt[HC : 2 * HC, :]
    for x in range(3):
        kq_o[HC + x * rk : HC + (x + 1) * rk, :] = kp[x]
        vt_o[HC + x * rv : HC + (x + 1) * rv, :] = vp[x]
    kq_o[HC + QP :, :] = jnp.zeros_like(kq_o[HC + QP :, :])
    vt_o[HC + VP :, :] = jnp.zeros_like(vt_o[HC + VP :, :])
    mq, mv, stat = head_mask(QW, Q_LANES), head_mask(256, V_LANES), stat_mask(128, 0)
    lane = lax.broadcasted_iota(jnp.int32, (HP, QW), 1)
    is_pt = lane >= HC
    scale = mq * jnp.where(is_pt, 2.0 * coef, WL / math.sqrt(HEAD))
    q_rows = per_head(q_feat[...], ni)
    left = q_rows * tiled(scale, ni)
    q_sq = jnp.sum(
        q_rows * q_rows * tiled(mq * jnp.where(is_pt, coef, 0.0), ni),
        axis=1, keepdims=True,
    )
    kpt = kq_o[HC : HC + QP, :]
    k_sq = dot_full(mq[:, HC : HC + QP] * coef, kpt * kpt)
    logits = dot_full(left, kq_o[...]) + WL * bias[...] - q_sq - tiled(k_sq, ni)
    cross = jnp.concatenate(
        [
            jnp.where(k_chain[...] != q_chain[i], chain, 0.0)
            for i in range(ni)
        ],
        axis=0,
    )
    logits = logits + cross
    logits = jnp.where(k_mask[...] == 1, logits, MASKED)
    lg_o[...] = logits
    top = jnp.max(logits, axis=1, keepdims=True)
    top_o[...] = head_sum(top * tiled(stat, ni), ni)
    dvm = per_head(dv[...], ni) * tiled(mv, ni)
    dav_o[...] = pair3(dvm, vt_o[0:256, :])


def weight_kernel(ni, logits, tops, dav, dap, vt, _, w_o, pay_o):
    stat = stat_mask(128, 0)
    top = jnp.sum(per_head(tops[...], ni) * tiled(stat, ni), axis=1, keepdims=True)
    weights = jnp.exp(logits[...] - top)
    w_o[...] = weights
    total = jnp.sum(weights, axis=1, keepdims=True)
    rounded = weights.astype(BF16).astype(F32)
    s_sum = jnp.sum(weights * dav[...] + rounded * dap[...], axis=1, keepdims=True)
    num = pair3(weights, vt[HC : HC + PW, :], 1, 1)
    num = num * tiled(head_mask(PW, P_LANES), ni)
    num = num + total * tiled(stat_mask(PW, VP), ni) + s_sum * tiled(stat_mask(PW, VP + HP), ni)
    pay_o[...] = head_sum(num, ni)


def value_kernel(ni, w, pair, vt, w_out, u_o, npx, nv0, nv1):
    cp = pair.shape[2]
    for i in range(ni):
        npx[i * HP : (i + 1) * HP, :] = dot(
            w[i * HP : (i + 1) * HP, :].astype(BF16), pair[i], 1, 0
        )
    nv = pair3(w[...], vt[0:256, :], 1, 1) * tiled(head_mask(256, V_LANES), ni)
    nv0[...] = nv[:, 0:128]
    nv1[...] = nv[:, 128:256]
    for h in range(H):
        t = h * HEAD // 128
        u_o[h] = rows2(npx[pl.ds(h, ni, stride=HP), :], w_out[HC + h * cp : HC + (h + 1) * cp, :])
        wv = w_out[t * 128 : min(t * 128 + 128, HC), :]
        part = (nv0, nv1)[t][pl.ds(h, ni, stride=HP), :]
        u_o[h] += rows2(part[:, 0 : wv.shape[0]], wv)


def spread_kernel(ni, qt, dvt, coef, lh_o, ll_o, dh_o, dlo_o):
    e = expand_mask(ni)
    rq = H * PQ
    head = lax.broadcasted_iota(jnp.int32, (rq, HP), 0) >> 2
    pick = (head == lax.broadcasted_iota(jnp.int32, (rq, HP), 1)).astype(F32)
    twice = 2.0 * dot_full(pick, coef[...])[:, 0:1]
    qs = qt[0:HC, 0:ni] * (WL / math.sqrt(HEAD))
    qp = qt[HC : HC + QP, 0:ni] * jnp.concatenate([twice] * 3, axis=0)
    lh_o[...], ll_o[...] = expand_rows(jnp.concatenate([qs, qp], axis=0), Q_BLOCKS, e)
    dh_o[...], dlo_o[...] = expand_rows(dvt[0:HC, 0:ni], V_BLOCKS, e)


def cross3(ah, al, bh, bl):
    return dot(ah, bh) + (dot(ah, bl) + dot(al, bh))


def grad_kernel(
    ni, oq, pay, w, dav, dap, q_feat, dlt, frt, kq, vt, kfr, u, lh, ll, dvh, dvl, coef_c,
    w_out, w_key_t, w_query_t,
    a_o, dl_o, ka_o, key_o, nat, tr, knat, kt,
):
    me = lax.axis_index("ka")
    fr = frt[...]
    mp, mq = head_mask(PW, P_LANES), head_mask(QW, Q_LANES)
    stats = (stat_mask(PW, VP), stat_mask(PW, VP + HP))
    totals = dot_full(pay[:, 256:384], spread_mask())
    inv = jnp.where(totals > 0.0, 1.0 / totals, 0.0)
    f_col = jnp.sum(per_head(inv, ni) * tiled(stats[0], ni), axis=1, keepdims=True)
    att = w[...] * f_col
    a_o[...] = att
    scaled = pay[...] * inv
    nat[...] = jnp.zeros_like(nat)
    nat[0:ni, :] = scaled
    transpose_tiles(tr, nat, 3)
    rv = H * PV
    out_pt = three(tr[0:VP, :], rv)
    shifted = [out_pt[x] - frame_row(fr, 9 + x) for x in range(3)]
    loc = to_local(fr, shifted)
    length = jnp.sqrt(loc[0] * loc[0] + loc[1] * loc[1] + loc[2] * loc[2] + 1e-08)
    ratio = dlt[VP : VP + rv, :] / length
    d_loc = [dlt[y * rv : (y + 1) * rv, :] + ratio * loc[y] for y in range(3)]
    d_pt = []
    for x in range(3):
        acc = frame_row(fr, 3 * x) * d_loc[0]
        for y in range(1, 3):
            acc = acc + frame_row(fr, 3 * x + y) * d_loc[y]
        d_pt.append(acc)
    for y in range(3):
        tr[y * rv : (y + 1) * rv, :] = loc[y]
    tr[VP : VP + rv, :] = length
    for t in range(3):
        nat[:, t * 128 : (t + 1) * 128] = jnp.transpose(tr[t * 128 : (t + 1) * 128, :])
    own = rows2(nat[0:ni, :], w_out[...])
    row = lax.broadcasted_iota(jnp.int32, (ni, 1), 0)
    upd = jnp.where((row >= me * oq) & (row < (me + 1) * oq), own, 0.0)
    for h in range(H):
        upd = upd + u[h] * inv[:, VP + h : VP + h + 1]
    for x in range(3):
        tr[x * rv : (x + 1) * rv, :] = d_pt[x]
    tr[VP:, :] = jnp.zeros_like(tr[VP:, :])
    d_pt_t = tr[0:VP, 0:ni]
    for t in range(3):
        nat[:, t * 128 : (t + 1) * 128] = jnp.transpose(tr[t * 128 : (t + 1) * 128, :])
    d_nat = nat[0:ni, :]
    lane = lax.broadcasted_iota(jnp.int32, (ni, PW), 1)
    dots = jnp.where(lane < VP, d_nat * scaled, scaled)
    delta = jnp.sum(per_head(dots, ni) * tiled(mp + stats[1], ni), axis=1, keepdims=True)
    dptm = per_head(d_nat, ni) * tiled(mp, ni)
    d_att = dav[...] + dap[...] + pair3(dptm, vt[HC : HC + PW, :])
    dl = att * (d_att - delta)
    dl_o[...] = dl
    coef = coef_c[:, 0:1]
    lane_h = lax.broadcasted_iota(jnp.int32, (HP, QW), 1)
    scale = mq * jnp.where(lane_h >= HC, 2.0 * coef, WL / math.sqrt(HEAD))
    row_sum = jnp.sum(dl, axis=1, keepdims=True)
    gq = pair3(dl, kq[...], 1, 1) - per_head(jnp.where(lane >= HC, q_feat[...], 0.0), ni) * row_sum
    nat[0:ni, :] = head_sum(gq * tiled(scale, ni), ni)
    nat[ni:, :] = jnp.zeros_like(nat[ni:, :])
    transpose_tiles(tr, nat, 3)
    rq = H * PQ
    gl = to_local(fr, three(tr[HC : HC + QP, :], rq))
    for x in range(3):
        tr[HC + x * rq : HC + (x + 1) * rq, :] = gl[x]
    for t in range(3):
        nat[:, t * 128 : (t + 1) * 128] = jnp.transpose(tr[t * 128 : (t + 1) * 128, :])
    width = w_query_t.shape[1]
    ka_o[:, 0:width] = upd
    ka_o[:, width : 2 * width] = rows2(nat[0:ni, 0 : HC + QP], w_query_t[...])
    dlh, dll = split2(dl)
    ath, atl = split2(att)
    gk = cross3(lh[...], ll[...], dlh, dll)
    kt[0:HC, :] = gk[0:HC]
    col_sum = jnp.sum(dl.reshape(ni, HP, dl.shape[1]), axis=0)
    col = dot_full(scale[:, HC : HC + QP], col_sum, 0, 0)
    gkp = gk[HC : HC + QP] - col * kq[HC : HC + QP, :]
    kt[HC : 2 * HC, :] = cross3(dvh[...], dvl[...], ath, atl)
    ph, plo = expand_rows(d_pt_t, P_BLOCKS, expand_mask(ni))
    gv = cross3(ph, plo, ath, atl)
    kf = kfr[...]
    gkl = to_local(kf, three(gkp, rq))
    gvl = to_local(kf, three(gv, rv))
    for x in range(3):
        kt[2 * HC + x * rq : 2 * HC + (x + 1) * rq, :] = gkl[x]
        kt[2 * HC + QP + x * rv : 2 * HC + QP + (x + 1) * rv, :] = gvl[x]
    for t in range(kt.shape[0] // 128):
        knat[:, t * 128 : (t + 1) * 128] = jnp.transpose(kt[t * 128 : (t + 1) * 128, :])
    key_o[...] = rows2(knat[:, 0 : w_key_t.shape[0]], w_key_t[...])


def pair_kernel(ni, att, dl, g, wb, out):
    wb_t = wb[...].astype(BF16)
    for i in range(ni):
        sl = slice(i * HP, (i + 1) * HP)
        ah, al = split2(att[sl, :])
        dh, dlo = split2(dl[sl, :] * WL)
        gh, gl = split2(g[sl, :])
        left = jnp.concatenate([ah, al, ah, dh, dlo], axis=0)
        right = jnp.concatenate([gh, gh, gl, wb_t, wb_t], axis=0)
        out[i] = dot(left, right, 0, 0).astype(BF16)


class Kept:
    def __init__(self, value):
        self.value = value


def call(kernel, outs, args, far=(), cut=None, kept=(), smem=0, scratch=(), name=None, limit=24):
    n_in, n_out = len(args), len(outs)
    held = [k for k, x in enumerate(args) if isinstance(x, Kept)]
    args = [x.value if isinstance(x, Kept) else x for x in args]
    far, far_out, after = list(far), [], []
    cut = cut or {}

    def body(*refs):
        ins, rest = list(refs[:n_in]), list(refs[n_in:])
        results, rest = rest[:n_out], rest[n_out:]
        own, rest = rest[: len(scratch)], rest[len(scratch) :]
        bufs, rest = rest[: len(far)], rest[len(far) :]
        out_bufs, sems = rest[: len(far_out)], rest[len(far_out) :]
        for k, (at, buf) in enumerate(zip(far, bufs)):
            src = ins[at]
            if at in cut:
                src = src.at[pl.ds(args[at].shape[0] - cut[at], cut[at]), :]
            ins[at] = Fetched(src, buf, sems[0].at[k])
        targets = list(results)
        for at, buf in zip(far_out, out_bufs):
            targets[at] = buf
        kernel(*ins, *targets, *own)
        copies = [
            pltpu.make_async_copy(buf, results[at], sems[0].at[len(far) + k])
            for k, (at, buf) in enumerate(zip(far_out, out_bufs))
        ]
        for copy in copies:
            copy.start()
        for at in far:
            ins[at].get()
        for copy in copies:
            copy.wait()

    specs = []
    for k in range(n_in):
        space = pltpu.SMEM if k < smem else pltpu.HBM if k in far or k in after else pltpu.VMEM
        specs.append(pl.BlockSpec(memory_space=space))
    results = pl.pallas_call(
        body,
        out_shape=[
            pltpu.VMEM(s, d) if k in kept else jax.ShapeDtypeStruct(s, d)
            for k, (s, d) in enumerate(outs)
        ],
        in_specs=specs,
        out_specs=[
            pl.BlockSpec(memory_space=pltpu.HBM if k in far_out else pltpu.VMEM)
            for k in range(n_out)
        ],
        scratch_shapes=[pltpu.VMEM(s, d) for s, d in scratch]
        + [pltpu.VMEM((cut.get(k, args[k].shape[0]),) + args[k].shape[1:], args[k].dtype)
           for k in far]
        + [pltpu.VMEM(*outs[k]) for k in far_out]
        + ([pltpu.SemaphoreType.DMA((len(far) + len(far_out),))] if far or far_out else []),
        compiler_params=pltpu.CompilerParams(vmem_limit_bytes=limit * 1024 * 1024),
        name=name,
    )(*[
        pltpu.with_memory_space_constraint(x, pltpu.HBM) if k in far
        else pltpu.with_memory_space_constraint(x, pltpu.VMEM) if k in held else x
        for k, x in enumerate(args)
    ])
    return [Kept(x) if k in kept else x for k, x in enumerate(results)]


def local(
    q_single, k_single, q_frames, k_frames, pair_tile, w_query, w_key, w_bias, w_out,
    head_weight, chain_bias, q_chain, k_chain, k_mask, d_update,
):
    pbc = lax.axis_size("pb")
    kac = lax.axis_size("ka")
    pb = lax.axis_index("pb")
    ka = lax.axis_index("ka")
    ni, nj, cp = pair_tile.shape
    oq, width = q_single.shape
    nk = k_single.shape[0]
    slot = -(-2 * oq // 8) * 8
    w_query_t, w_key_t, w_bias_t = (jnp.transpose(x) for x in (w_query, w_key, w_bias))

    def ka_xor(x, d):
        return lax.ppermute(x, "ka", [(i, i ^ d) for i in range(kac)])

    def pb_xor(x, d):
        return lax.ppermute(x, "pb", [(i, i ^ d) for i in range(pbc)])

    n_row = ni * HP
    f32 = lambda *s: (s, F32)
    bf16 = lambda *s: (s, BF16)
    k_rows = width // 128 * nk + 16
    pk, pq = call(
        functools.partial(pack_kernel, pbc),
        [f32(k_rows, 128), f32(slot, width + 128)],
        [k_single, k_frames, q_single, jnp.transpose(q_frames), d_update],
        far=range(5),
        name="pack",
    )
    own_pieces = [pq] + [ka_xor(pq, 2 * d) for d in range(1, kac // 2)]
    routed = call(
        functools.partial(route_kernel, pbc),
        [f32(k_rows, 128)] * pbc + [f32(kac // 2, slot, width + 128)],
        [pk] + [pb_xor(pk, d) for d in range(1, pbc)] + own_pieces,
        scratch=[f32(pbc, k_rows, 128)],
        name="route",
    )
    query_own = routed[pbc]
    query_other = ka_xor(query_own, 1)
    key_pieces = [
        lax.ppermute(
            routed[s], "ka",
            [(a, ((a % pbc) ^ s) * 2 + a // pbc) for a in range(kac)],
        )
        for s in range(pbc)
    ]
    bias, dap, g, q_feat, qt, dv, dvt, dlt, frt, wb = call(
        functools.partial(query_kernel, ni, kac, oq, slot),
        [f32(n_row, nj), f32(n_row, nj), f32(n_row, cp), f32(ni, QW), f32(QW, 128),
         f32(ni, 256), f32(256, 128), f32(384, 128), f32(128, 128), f32(HP, cp)],
        [query_own, query_other, pair_tile, w_query_t, w_out, w_bias_t],
        far=range(2, 6),
        kept=range(10),
        scratch=[f32(kac * slot, width + 128), f32(128, QW), f32(128, 384)],
        name="query",
    )
    logits, dav, tops, kq, vt, kfr, coef = call(
        functools.partial(key_kernel, ni, nk, pbc),
        [f32(n_row, nj), f32(n_row, nj), f32(ni, 128), f32(QW, nj), f32(HC + PW, nj),
         f32(16, nj), f32(HP, 128)],
        [q_chain, *key_pieces, w_key_t, q_feat, dv, bias, head_weight[None, :],
         chain_bias[None, :], k_chain[None, :], k_mask[None, :]],
        far=[pbc + 1, pbc + 5, pbc + 6, pbc + 7, pbc + 8],
        kept=[0, 1, 3, 4, 5, 6],
        smem=1,
        scratch=[f32(nj, width), f32(w_key_t.shape[0], nj)],
        name="key",
    )
    tops = jnp.maximum(tops, ka_xor(tops, 1))
    tops = functools.reduce(
        jnp.maximum, [ka_xor(tops, 2 * d) for d in range(1, kac // 2)], tops
    )
    lh, ll, dvh, dvl = call(
        functools.partial(spread_kernel, ni),
        [bf16(HC + QP, n_row), bf16(HC + QP, n_row), bf16(HC, n_row), bf16(HC, n_row)],
        [qt, dvt, coef],
        kept=range(4),
        name="spread",
    )
    weights, total = call(
        functools.partial(weight_kernel, ni),
        [f32(n_row, nj), f32(ni, PW)],
        [logits, tops, dav, dap, vt, lh],
        kept=[0],
        name="weight",
    )
    (u,) = call(
        functools.partial(value_kernel, ni),
        [f32(H, ni, width)],
        [weights, pair_tile, vt, w_out],
        far=[1, 3],
        kept=[0],
        scratch=[f32(n_row, cp), f32(n_row, 128), f32(n_row, 128)],
        name="value",
    )
    step = 1
    while step < kac:
        total = total + ka_xor(total, step)
        step *= 2
    att, dl, part, key_part = call(
        functools.partial(grad_kernel, ni, oq),
        [f32(n_row, nj), f32(n_row, nj), f32(ni, 2 * width), f32(nj, width)],
        [total, weights, dav, dap, q_feat, dlt, frt, kq, vt, kfr, u, lh, ll, dvh, dvl, coef,
         w_out, w_key_t, w_query_t],
        far=[16, 17, 18],
        cut={16: PW},
        kept=[0, 1],
        scratch=[f32(128, 384), f32(384, 128), f32(nj, 896), f32(896, nj)],
        name="grad",
    )
    (d_pair,) = call(
        functools.partial(pair_kernel, ni),
        [((ni, nj, cp), BF16)],
        [att, dl, g, wb],
        name="pair",
    )

    split = part.reshape(kac // 2, 2, oq, 2 * width)
    core = ka % 2
    mine = lax.dynamic_index_in_dim(split, core, 1, keepdims=False)
    theirs = lax.dynamic_index_in_dim(split, 1 - core, 1, keepdims=False)
    mine = mine + ka_xor(theirs, 1)
    chip = ka // 2
    own = lax.dynamic_index_in_dim(mine, chip, 0, keepdims=False)
    for d in range(1, kac // 2):
        own = own + ka_xor(lax.dynamic_index_in_dim(mine, chip ^ d, 0, keepdims=False), 2 * d)
    blocks = key_part.reshape(pbc, nj // pbc, width)
    key_own = lax.dynamic_index_in_dim(blocks, pb, 0, keepdims=False)
    for d in range(1, pbc):
        key_own = key_own + pb_xor(
            lax.dynamic_index_in_dim(blocks, pb ^ d, 0, keepdims=False), d
        )
    return (
        own[:, :width].astype(BF16),
        d_pair,
        own[:, width:].astype(BF16),
        key_own,
    )


def solution(mesh):
    both = ("pb", "ka")
    placed = (
        P(both, None), P(both, None), P(None, both), P(None, both), P("pb", "ka", None),
        P(), P(), P(), P(), P(), P(), P("pb"), P("ka"), P("ka"), P(both, None),
    )
    return jax.shard_map(
        local,
        mesh=mesh,
        in_specs=placed,
        out_specs=(
            P(both, None), P("pb", "ka", None), P(both, None), P(("ka", "pb"), None),
        ),
        check_vma=False,
    )
```

```python
import functools
import math

import jax
import jax.numpy as jnp
from jax import lax
from jax.experimental import pallas as pl
from jax.experimental.pallas import tpu as pltpu
from jax.sharding import PartitionSpec as P

H = 12
HP = 16
HEAD = 16
PQ = 4
PV = 8
HC = H * HEAD
QP = 3 * H * PQ
VP = 3 * H * PV
QW = 384
PW = 384
MASKED = -1000000000.0
WL = math.sqrt(1.0 / 3.0)
F32 = jnp.float32
BF16 = jnp.bfloat16


def dot(a, b, ca=1, cb=0, precision=None):
    return lax.dot_general(
        a, b, (((ca,), (cb,)), ((), ())), precision=precision, preferred_element_type=F32
    )


def dot_full(a, b, ca=1, cb=0):
    return dot(a, b, ca, cb, lax.Precision.HIGHEST)


def split2(x):
    high = x.astype(BF16)
    return high, (x - high.astype(F32)).astype(BF16)


def split3(x):
    high = x.astype(BF16)
    rest = x - high.astype(F32)
    mid = rest.astype(BF16)
    return high, mid, (rest - mid.astype(F32)).astype(BF16)


def rows3(x, b, ca=1, cb=0):
    n = x.shape[0]
    out = dot(jnp.concatenate(split3(x), axis=0), b, ca, cb)
    return out[0:n] + out[n : 2 * n] + out[2 * n : 3 * n]


def rows2(x, b, ca=1, cb=0):
    n = x.shape[0]
    out = dot(jnp.concatenate(split2(x), axis=0), b, ca, cb)
    return out[0:n] + out[n : 2 * n]


def pair3(a, b, ca=1, cb=0):
    ah, al = split2(a)
    bh, bl = split2(b)
    return dot(ah, bh, ca, cb) + (dot(ah, bl, ca, cb) + dot(al, bh, ca, cb))


def per_head(x, n):
    return jnp.broadcast_to(x[:, None, :], (n, HP, x.shape[1])).reshape(n * HP, x.shape[1])


def tiled(x, n):
    return jnp.broadcast_to(x[None], (n,) + x.shape).reshape(n * HP, x.shape[1])


def head_sum(x, n):
    return jnp.sum(x.reshape(n, HP, x.shape[1]), axis=1)


def frame_row(fr, index):
    return fr[index : index + 1, :]


def to_world(fr, loc, rows):
    out = []
    for x in range(3):
        acc = frame_row(fr, 9 + x) + frame_row(fr, 3 * x) * loc[0]
        for y in range(1, 3):
            acc = acc + frame_row(fr, 3 * x + y) * loc[y]
        out.append(acc)
    return out


def to_local(fr, g):
    out = []
    for y in range(3):
        acc = frame_row(fr, y) * g[0]
        for x in range(1, 3):
            acc = acc + frame_row(fr, 3 * x + y) * g[x]
        out.append(acc)
    return out


def three(x, rows):
    return [x[k * rows : (k + 1) * rows] for k in range(3)]


def transpose_tiles(dst, src, tiles):
    for t in range(tiles):
        dst[t * 128 : (t + 1) * 128, :] = jnp.transpose(src[:, t * 128 : (t + 1) * 128])


def column(row, n):
    at = lax.broadcasted_iota(jnp.int32, (HP, n), 0) == lax.broadcasted_iota(
        jnp.int32, (HP, n), 1
    )
    return jnp.sum(jnp.where(at, jnp.broadcast_to(row, (HP, n)), 0.0), axis=1, keepdims=True)


def coefficient(head_weight):
    x = head_weight[...]
    soft = jnp.maximum(x, 0.0) + jnp.log1p(jnp.exp(-jnp.abs(x)))
    return column(WL * soft * math.sqrt(2.0 / (9.0 * PQ)) / 2.0, H)


def rows_mask(blocks, width):
    parts = []
    for rows, shift in blocks:
        head = lax.broadcasted_iota(jnp.int32, (rows, width), 0) >> shift
        parts.append(head == (lax.broadcasted_iota(jnp.int32, (rows, width), 1) & (HP - 1)))
    return parts


def expand_rows(x, blocks, expand):
    keep = rows_mask(blocks, expand.shape[1])
    out = []
    for part in split2(x):
        wide = dot(part, expand)
        pieces, start = [], 0
        for (rows, _), mask in zip(blocks, keep):
            pieces.append(jnp.where(mask, wide[start : start + rows], 0.0).astype(BF16))
            start += rows
        out.append(jnp.concatenate(pieces, axis=0))
    return out


Q_BLOCKS = ((HC, 4),) + ((H * PQ, 2),) * 3
V_BLOCKS = ((HC, 4),)
P_BLOCKS = ((H * PV, 3),) * 3


def grid(shape):
    return tuple(lax.broadcasted_iota(jnp.int32, shape, d) for d in range(2))


def lanes_of(shape, row, blocks):
    lane = lax.broadcasted_iota(jnp.int32, shape, 1)
    keep = None
    for first, count, shift in blocks:
        hit = (lane >= first) & (lane < first + count) & (((lane - first) >> shift) == row)
        keep = hit if keep is None else keep | hit
    return keep


Q_LANES = ((0, HC, 4),) + tuple((HC + x * H * PQ, H * PQ, 2) for x in range(3))
V_LANES = ((0, HC, 4),)
P_LANES = tuple((x * H * PV, H * PV, 3) for x in range(3))


def head_mask(width, blocks):
    shape = (HP, width)
    return lanes_of(shape, grid(shape)[0], blocks).astype(F32)


def stat_mask(width, first):
    row, lane = grid((HP, width))
    return (lane == row + first).astype(F32)


def spread_mask(offset):
    shape = (128, PW)
    head = grid(shape)[0] - (VP - 256) - offset
    lane = grid(shape)[1]
    keep = lanes_of(shape, head, P_LANES)
    for k in range(3):
        keep = keep | (lane == head + VP + k * HP)
    return (keep & (head >= 0) & (head < H)).astype(F32)


def to_column(x, ni, first):
    return jnp.sum(per_head(x, ni) * tiled(stat_mask(128, first), ni), axis=1, keepdims=True)


def expand_mask(ni):
    row, lane = grid((ni, ni * HP))
    return ((lane // HP) == row).astype(BF16)


def row_order(ni, ka, oq, slot):
    row, lane = grid((2 * ni, ka * slot))
    shift = oq.bit_length() - 1
    index = row & (ni - 1)
    source = (index >> shift) * slot + (index & (oq - 1))
    return (lane == source + jnp.where(row >= ni, oq, 0)).astype(F32)


class Fetched:
    def __init__(self, src, dst, sem):
        self.ref, self.pending = dst, pltpu.make_async_copy(src, dst, sem)
        self.shape = dst.shape
        self.pending.start()

    def get(self):
        if self.pending is not None:
            self.pending.wait()
            self.pending = None
        return self.ref

    def __getitem__(self, index):
        return self.get()[index]


def pack_kernel(pbc, k, kf, q, qf, du, pk, pq):
    nk, width = k.shape
    oq = q.shape[0]
    spot = lax.rem(lax.axis_index("ka"), pbc)
    for t in range(width // 128):
        pk[t * nk : (t + 1) * nk, :] = k[:, t * 128 : (t + 1) * 128]
    row = lax.broadcasted_iota(jnp.int32, (nk, 128), 0)
    lane = lax.broadcasted_iota(jnp.int32, (nk, 128), 1)
    pk[width // 128 * nk :, :] = jnp.zeros_like(pk[width // 128 * nk :, :])
    pk[width // 128 * nk : width // 128 * nk + 12, :] = dot_full(
        kf[...], (lane == row + spot * nk).astype(F32)
    )
    pq[...] = jnp.zeros_like(pq)
    pq[0:oq, 0:width] = q[...]
    pq[0:oq, width : width + 12] = qf[...]
    pq[oq : 2 * oq, 0:width] = du[...]


def route_kernel(pbc, *refs):
    pieces, rest = refs[:pbc], refs[pbc:]
    held = rest[-1]
    chips = (len(rest) - pbc - 2)
    rows, outs, gathered = rest[:chips], rest[chips : chips + pbc], rest[chips + pbc]
    spot = lax.rem(lax.axis_index("ka"), pbc)
    mine = lax.axis_index("pb")
    for d in range(pbc):
        held[d] = pieces[d][...]
    for s in range(pbc):
        outs[s][...] = held[(spot ^ s) ^ mine]
    for d in range(chips):
        gathered[d] = rows[d][...]


def load_kernel(n, *refs):
    sources, targets, sems = refs[1 : 1 + n], refs[1 + n : 1 + 2 * n], refs[1 + 2 * n]
    copies = [
        pltpu.make_async_copy(x, y, sems.at[k]) for k, (x, y) in enumerate(zip(sources, targets))
    ]
    for copy in copies:
        copy.start()
    for copy in copies:
        copy.wait()


def query_kernel(ni, ka, oq, slot, q_chain, *refs):
    pieces = refs[:2]
    (pair, w_query_t, w_out, w_bias_t, head_weight, chain_bias, k_chain,
     base_o, dap_o, gw_o, q_o, qt_o, l1_o, l2_o, l3_o, dmh_o, dml_o, dvt_o, dlt_o, frt_o,
     qd, nat, dnat) = refs[2:]
    me = lax.axis_index("ka")
    chip, core = me // 2, lax.rem(me, 2)
    for d in range(ka // 2):
        for e in range(2):
            owner = (chip ^ d) * 2 + (core ^ e)
            qd[pl.ds(pl.multiple_of(owner * slot, 8), slot), :] = pieces[e][d]
    n_row = ni * HP
    gw_o[...] = jnp.zeros_like(gw_o)
    gw_o[n_row : n_row + H, :] = w_bias_t[...].astype(F32)
    wb_t = gw_o[n_row : n_row + HP, :].astype(BF16)
    coef = coefficient(head_weight)
    gw_o[n_row + HP :, :] = jnp.broadcast_to(coef, (HP, gw_o.shape[1]))
    chain = column(chain_bias[...], H)
    rows = dot_full(row_order(ni, ka, oq, slot), qd[...])
    width = w_query_t.shape[1]
    q_raw, d_up = rows[:ni, :width], rows[ni:, :width]
    nat[...] = jnp.zeros_like(nat)
    nat[0:ni, 0:128] = rows[:ni, width : width + 128]
    nat[ni : 2 * ni, 0:128] = rows[:ni, width : width + 128]
    frt_o[...] = jnp.transpose(nat[:, 0:128])
    fr = frt_o[...]
    nat[...] = jnp.zeros_like(nat)
    nat[0:ni, 0 : HC + QP] = rows3(q_raw, w_query_t[...], 1, 1)
    transpose_tiles(qt_o, nat, QW // 128)
    rp = H * PQ
    world = to_world(fr, three(qt_o[HC : HC + QP, :], rp), rp)
    for x in range(3):
        qt_o[HC + x * rp : HC + (x + 1) * rp, :] = world[x]
    for t in range(QW // 128):
        nat[:, t * 128 : (t + 1) * 128] = jnp.transpose(qt_o[t * 128 : (t + 1) * 128, :])
    q_o[...] = nat[0:ni, :]
    mq = head_mask(QW, Q_LANES)
    is_pt = lax.broadcasted_iota(jnp.int32, (HP, QW), 1) >= HC
    q_rows = per_head(nat[0:ni, :], ni)
    left = q_rows * tiled(mq * jnp.where(is_pt, 2.0 * coef, WL / math.sqrt(HEAD)), ni)
    l1_o[...], l2_o[...], l3_o[...] = split3(left)
    q_sq = 0.5 * jnp.sum(
        left * jnp.where(lax.broadcasted_iota(jnp.int32, left.shape, 1) >= HC, q_rows, 0.0),
        axis=1, keepdims=True,
    )
    split = jnp.concatenate(split3(d_up), axis=0)

    def d_out(lo, hi):
        out = dot(split, w_out[lo:hi, :], 1, 1)
        return out[0:ni] + out[ni : 2 * ni] + out[2 * ni : 3 * ni]

    dnat[...] = jnp.zeros_like(dnat)
    dnat[0:ni, 0:HC] = d_out(0, HC)
    dmh_o[...], dml_o[...] = split2(
        per_head(dnat[0:ni, 0:256], ni) * tiled(head_mask(256, V_LANES), ni)
    )
    transpose_tiles(dvt_o, dnat, 2)
    cp = pair.shape[2]
    first = HC + H * cp
    dnat[0:ni, :] = d_out(first, first + VP + H * PV)
    transpose_tiles(dlt_o, dnat, 3)
    for h in range(H):
        gw_o[pl.ds(h, ni, stride=HP), :] = d_out(HC + h * cp, HC + (h + 1) * cp)
    for i in range(ni):
        gh, gl = split2(gw_o[i * HP : (i + 1) * HP, :])
        out = dot(jnp.concatenate([wb_t, gh, gl], axis=0), pair[i], 1, 1)
        sl = slice(i * HP, (i + 1) * HP)
        cross = jnp.where(k_chain[...] != q_chain[i], chain, 0.0)
        base_o[sl, :] = WL * out[0:HP] - q_sq[sl] + cross
        dap_o[sl, :] = out[HP : 2 * HP] + out[2 * HP : 3 * HP]


def key_kernel(ni, nk, n_pieces, *refs):
    pieces = refs[:n_pieces]
    (w_key_t, base, l1, l2, l3, dmh, dml, dap, gw, k_mask,
     w_o, da_o, pay_o, kq_o, vt_o, kraw, kt) = refs[n_pieces:]
    chip = lax.axis_index("ka") // 2
    width = w_key_t.shape[1]
    tiles = width // 128
    fr = None
    for s in range(n_pieces):
        start = pl.multiple_of((chip ^ s) * nk, 8)
        for t in range(tiles):
            kraw[pl.ds(start, nk), t * 128 : (t + 1) * 128] = pieces[s][t * nk : (t + 1) * nk, :]
        part = pieces[s][tiles * nk : tiles * nk + 16, :]
        fr = part if fr is None else fr + part
    parts = split3(kraw[...])
    w_t = w_key_t[...]
    kt[...] = dot(w_t, parts[0], 1, 1) + (dot(w_t, parts[1], 1, 1) + dot(w_t, parts[2], 1, 1))
    rk, rv = H * PQ, H * PV
    kp = to_world(fr, three(kt[2 * HC : 2 * HC + QP, :], rk), rk)
    vp = to_world(fr, three(kt[2 * HC + QP : 2 * HC + QP + VP, :], rv), rv)
    kq_o[0:HC, :] = kt[0:HC, :]
    vt_o[0:HC, :] = kt[HC : 2 * HC, :]
    for x in range(3):
        kq_o[HC + x * rk : HC + (x + 1) * rk, :] = kp[x]
        vt_o[HC + x * rv : HC + (x + 1) * rv, :] = vp[x]
    kq_o[HC + QP : HC + QP + 16, :] = fr
    kq_o[HC + QP + 16 :, :] = jnp.zeros_like(kq_o[HC + QP + 16 :, :])
    vt_o[HC + VP :, :] = jnp.zeros_like(vt_o[HC + VP :, :])
    mq = head_mask(QW, Q_LANES)
    coef = gw[ni * HP + HP :, 0:1]
    kpt = kq_o[HC : HC + QP, :]
    k_sq = dot_full(mq[:, HC : HC + QP] * coef, kpt * kpt)
    k1, k2, k3 = split3(kq_o[...])
    logits = dot(l2[...], k2) + (dot(l1[...], k3) + dot(l3[...], k1))
    logits = logits + (dot(l1[...], k2) + dot(l2[...], k1))
    logits = logits + dot(l1[...], k1)
    logits = logits + base[...] - tiled(k_sq, ni)
    logits = jnp.where(k_mask[...] == 1, logits, MASKED)
    top = jnp.max(logits, axis=1, keepdims=True)
    weights = jnp.exp(logits - top)
    w_o[...] = weights
    total = jnp.sum(weights, axis=1, keepdims=True)
    vh, vl = split2(vt_o[...])
    da = dap[...] + cross3(dmh[...], dml[...], vh[0:256], vl[0:256])
    da_o[...] = da
    s_sum = jnp.sum(weights * da, axis=1, keepdims=True)
    wh, wl = split2(weights)
    ph, po = vh[HC : HC + PW], vl[HC : HC + PW]
    num = dot(wh, ph, 1, 1) + (dot(wh, po, 1, 1) + dot(wl, ph, 1, 1))
    num = num * tiled(head_mask(PW, P_LANES), ni)
    for k, value in enumerate((top, total, s_sum)):
        num = num + value * tiled(stat_mask(PW, VP + k * HP), ni)
    pay_o[...] = head_sum(num, ni)


def combine_kernel(a, b, out):
    n = a.shape[0]
    tops = dot_full(jnp.concatenate([a[:, 256:384], b[:, 256:384]], axis=0), spread_mask(0))
    ta, tb = tops[0:n], tops[n : 2 * n]
    top = jnp.maximum(ta, tb)
    lane = lax.broadcasted_iota(jnp.int32, top.shape, 1)
    mixed = a[...] * jnp.exp(ta - top) + b[...] * jnp.exp(tb - top)
    out[...] = jnp.where((lane >= VP) & (lane < VP + HP), top, mixed)


def value_kernel(ni, w, pair, vt, w_out, u_o, npx, nv0, nv1):
    cp = pair.shape[2]
    for i in range(ni):
        wh, wl = split2(w[i * HP : (i + 1) * HP, :])
        out = dot(jnp.concatenate([wh, wl], axis=0), pair[i], 1, 0)
        npx[i * HP : (i + 1) * HP, :] = out[0:HP] + out[HP : 2 * HP]
    nv = pair3(w[...], vt[0:256, :], 1, 1) * tiled(head_mask(256, V_LANES), ni)
    nv0[...] = nv[:, 0:128]
    nv1[...] = nv[:, 128:256]
    for h in range(H):
        t = h * HEAD // 128
        wv = w_out[t * 128 : min(t * 128 + 128, HC), :]
        part = (nv0, nv1)[t][pl.ds(h, ni, stride=HP), :]
        u_o[h] = rows2(
            npx[pl.ds(h, ni, stride=HP), :], w_out[HC + h * cp : HC + (h + 1) * cp, :]
        ) + rows2(part[:, 0 : wv.shape[0]], wv)


def spread_kernel(ni, qt, dvt, gw, lh_o, ll_o, dh_o, dlo_o):
    e = expand_mask(ni)
    rq = H * PQ
    head = lax.broadcasted_iota(jnp.int32, (rq, HP), 0) >> 2
    pick = (head == lax.broadcasted_iota(jnp.int32, (rq, HP), 1)).astype(F32)
    twice = 2.0 * dot_full(pick, gw[ni * HP + HP :, :])[:, 0:1]
    qs = qt[0:HC, 0:ni] * (WL / math.sqrt(HEAD))
    qp = qt[HC : HC + QP, 0:ni] * jnp.concatenate([twice] * 3, axis=0)
    lh_o[...], ll_o[...] = expand_rows(jnp.concatenate([qs, qp], axis=0), Q_BLOCKS, e)
    dh_o[...], dlo_o[...] = expand_rows(dvt[0:HC, 0:ni], V_BLOCKS, e)


def cross3(ah, al, bh, bl):
    return dot(ah, bh) + (dot(ah, bl) + dot(al, bh))


def grad_kernel(
    ni, oq, ka, pay, pay_loc, w, da, dap, q_feat, dlt, frt, kq, vt, u, dvh, dvl, gw,
    w_out, w_key_t,
    att_o, dl_o, mine_o, theirs_o, keyv_o, nat, tr, knat, kt,
):
    me = lax.axis_index("ka")
    fr = frt[...]
    width = u.shape[2]
    mp, mq = head_mask(PW, P_LANES), head_mask(QW, Q_LANES)
    tops = dot_full(
        jnp.concatenate([pay[:, 256:384], pay_loc[:, 256:384]], axis=0), spread_mask(0)
    )
    grow = jnp.exp(tops[ni : 2 * ni] - tops[0:ni])
    totals = dot_full(pay[:, 256:384], spread_mask(HP))
    inv = jnp.where(totals > 0.0, 1.0 / totals, 0.0)
    inv_col = to_column(inv[:, 256:384], ni, VP - 256)
    weights = w[...] * to_column(grow[:, 256:384], ni, VP - 256)
    att = weights * inv_col
    att_o[...] = att
    lost = jnp.sum(
        (weights - weights.astype(BF16).astype(F32)) * dap[...], axis=1, keepdims=True
    )
    nat[...] = jnp.zeros_like(nat)
    nat[0:ni, 0:128] = head_sum(lost * inv_col * tiled(stat_mask(128, 0), ni), ni)
    eps_t = jnp.transpose(nat[:, 0:128])[0:HP, :]
    scaled = pay[...] * inv
    nat[0:ni, :] = scaled
    transpose_tiles(tr, nat, 3)
    rv = H * PV
    out_pt = three(tr[0:VP, :], rv)
    shifted = [out_pt[x] - frame_row(fr, 9 + x) for x in range(3)]
    loc = to_local(fr, shifted)
    length = jnp.sqrt(loc[0] * loc[0] + loc[1] * loc[1] + loc[2] * loc[2] + 1e-08)
    ratio = dlt[VP : VP + rv, :] / length
    d_loc = [dlt[y * rv : (y + 1) * rv, :] + ratio * loc[y] for y in range(3)]
    d_pt = []
    for x in range(3):
        acc = frame_row(fr, 3 * x) * d_loc[0]
        for y in range(1, 3):
            acc = acc + frame_row(fr, 3 * x + y) * d_loc[y]
        d_pt.append(acc)
    for y in range(3):
        tr[y * rv : (y + 1) * rv, :] = loc[y]
    tr[VP : VP + rv, :] = length
    for t in range(3):
        nat[:, t * 128 : (t + 1) * 128] = jnp.transpose(tr[t * 128 : (t + 1) * 128, :])
    own = rows2(nat[0:ni, :], w_out[w_out.shape[0] - PW :, :])
    row = lax.broadcasted_iota(jnp.int32, (ni, 1), 0)
    upd = jnp.where((row >= me * oq) & (row < (me + 1) * oq), own, 0.0)
    share = inv * grow
    for h in range(H):
        upd = upd + u[h] * share[:, VP + h : VP + h + 1]
    for x in range(3):
        tr[x * rv : (x + 1) * rv, :] = d_pt[x]
    tr[VP:, :] = jnp.zeros_like(tr[VP:, :])
    d_pt_t = tr[0:VP, 0:ni]
    for t in range(3):
        nat[:, t * 128 : (t + 1) * 128] = jnp.transpose(tr[t * 128 : (t + 1) * 128, :])
    d_nat = nat[0:ni, :]
    lane = lax.broadcasted_iota(jnp.int32, (ni, PW), 1)
    dots = jnp.where(lane < VP, d_nat * scaled, scaled)
    delta = jnp.sum(
        per_head(dots, ni) * tiled(mp + stat_mask(PW, VP + 2 * HP), ni), axis=1, keepdims=True
    )
    dptm = per_head(d_nat, ni) * tiled(mp, ni)
    d_att = da[...] + pair3(dptm, vt[HC : HC + PW, :])
    dl = att * (d_att - delta)
    dl_o[...] = dl
    coef = gw[ni * HP + HP :, 0:1]
    lane_h = lax.broadcasted_iota(jnp.int32, (HP, QW), 1)
    scale = tiled(mq * jnp.where(lane_h >= HC, 2.0 * coef, WL / math.sqrt(HEAD)), ni)
    kh, kl = split2(kq[...])
    points = per_head(jnp.where(lane >= HC, q_feat[...], 0.0), ni)
    dlh, dll = split2(dl)
    ath, atl = split2(att)
    for k, (full, high, low) in enumerate(((dl, dlh, dll), (att, ath, atl))):
        gq = dot(high, kh, 1, 1) + (dot(high, kl, 1, 1) + dot(low, kh, 1, 1))
        gq = gq - points * jnp.sum(full, axis=1, keepdims=True)
        nat[k * ni : (k + 1) * ni, :] = head_sum(gq * scale, ni)
    nat[2 * ni :, :] = jnp.zeros_like(nat[2 * ni :, :])
    transpose_tiles(tr, nat, 3)
    rq = H * PQ
    gl = to_local(fr, three(tr[HC : HC + QP, :], rq))
    for x in range(3):
        tr[HC + x * rq : HC + (x + 1) * rq, :] = gl[x]
    for t in range(3):
        nat[:, t * 128 : (t + 1) * 128] = jnp.transpose(tr[t * 128 : (t + 1) * 128, :])
    half = ni // 2
    r32, c32 = grid((ni, ni))
    rest = r32 & (half - 1)
    shift = oq.bit_length() - 1
    source = (
        (((me // 2) ^ (rest >> shift)) * 2 + (lax.rem(me, 2) ^ jnp.where(r32 >= half, 1, 0))) * oq
        + (rest & (oq - 1))
    )
    order = (c32 == source).astype(BF16)
    for k, block in enumerate((upd, nat[0:ni, :], nat[ni : 2 * ni, :])):
        p1, p2, p3 = split3(block)
        moved = dot(order, p1) + (dot(order, p2) + dot(order, p3))
        mine_o[:, k * width : (k + 1) * width] = moved[0:half]
        theirs_o[:, k * width : (k + 1) * width] = moved[half:]
    mine_o[:, 3 * width :] = jnp.zeros_like(mine_o[:, 3 * width :])
    mine_o[0:HP, 3 * width :] = eps_t
    theirs_o[:, 3 * width :] = jnp.zeros_like(theirs_o[:, 3 * width :])
    theirs_o[0:HP, 3 * width :] = eps_t
    kt[0:HC, :] = cross3(dvh[...], dvl[...], ath, atl)
    ph, plo = expand_rows(d_pt_t, P_BLOCKS, expand_mask(ni))
    gvl = to_local(kq[HC + QP : HC + QP + 16, :], three(cross3(ph, plo, ath, atl), rv))
    for x in range(3):
        kt[256 + x * rv : 256 + (x + 1) * rv, :] = gvl[x]
    for t in range(5):
        knat[:, t * 128 : (t + 1) * 128] = jnp.transpose(kt[t * 128 : (t + 1) * 128, :])
    keyv_o[...] = rows2(knat[:, 0:HC], w_key_t[HC : 2 * HC, :]) + rows2(
        knat[:, 256 : 256 + VP], w_key_t[2 * HC + QP :, :]
    )


def mid_kernel(oq, chips, width, mine, other, *outs):
    total = mine[...] + other[...]
    for d in range(chips):
        outs[d][:, 0 : 3 * width] = total[d * oq : (d + 1) * oq, 0 : 3 * width]
        for k in range(HP // oq):
            at = 3 * width + k * 128
            outs[d][:, at : at + 128] = total[k * oq : (k + 1) * oq, 3 * width :]


def correction(oq, width, slices, eps):
    eps[...] = jnp.zeros_like(eps)
    for k in range(HP // oq):
        at = 3 * width + k * 128
        acc = slices[0][:, at : at + 128]
        for piece in slices[1:]:
            acc = acc + piece[:, at : at + 128]
        eps[k * oq : (k + 1) * oq, :] = acc


def keyfix_kernel(ni, oq, width, chips, pbc, *refs):
    slices = refs[:chips]
    att, dl0, lh, ll, kq, gw, keyv, w_key_t = refs[chips : chips + 8]
    dl_o, outs = refs[chips + 8], refs[chips + 9 : chips + 9 + pbc]
    eps, kt, knat, total = refs[chips + 9 + pbc :]
    correction(oq, width, slices, eps)
    per_query = jnp.transpose(eps[...])[0:ni, :]
    dl = dl0[...] + att[...] * to_column(per_query, ni, 0)
    dl_o[...] = dl
    dlh, dll = split2(dl)
    gk = cross3(lh[...], ll[...], dlh, dll)
    kt[0:HC, :] = gk[0:HC]
    coef = gw[ni * HP + HP :, 0:1]
    col_sum = jnp.sum(dl.reshape(ni, HP, dl.shape[1]), axis=0)
    col = dot_full(head_mask(QW, Q_LANES)[:, HC : HC + QP] * (2.0 * coef), col_sum, 0, 0)
    rq = H * PQ
    gkp = gk[HC : HC + QP] - col * kq[HC : HC + QP, :]
    gkl = to_local(kq[HC + QP : HC + QP + 16, :], three(gkp, rq))
    for x in range(3):
        kt[256 + x * rq : 256 + (x + 1) * rq, :] = gkl[x]
    for t in range(4):
        knat[:, t * 128 : (t + 1) * 128] = jnp.transpose(kt[t * 128 : (t + 1) * 128, :])
    total[...] = keyv[...] + (
        rows2(knat[:, 0:HC], w_key_t[0:HC, :])
        + rows2(knat[:, 256 : 256 + QP], w_key_t[2 * HC : 2 * HC + QP, :])
    )
    block = total.shape[0] // pbc
    for d in range(pbc):
        start = pl.multiple_of((lax.axis_index("pb") ^ d) * block, 8)
        outs[d][...] = total[pl.ds(start, block), :]


def ownfix_kernel(oq, width, chips, *refs):
    slices, w_query_t = refs[:chips], refs[chips]
    upd_o, dq_o, eps, rows = refs[chips + 1 :]
    correction(oq, width, slices, eps)
    acc = slices[0][:, 0 : 3 * width]
    for piece in slices[1:]:
        acc = acc + piece[:, 0 : 3 * width]
    upd_o[...] = acc[:, 0:width].astype(BF16)
    rows[...] = jnp.zeros_like(rows)
    rows[0:oq, :] = acc[:, width:]
    r, lane = grid((8, 128))
    pick = (lane == lax.axis_index("ka") * oq + r).astype(F32)
    mine = dot_full(pick, eps[0:HP, :], 1, 1)
    full = dot_full(mine, head_mask(QW, Q_LANES))
    local_grad = rows[:, 0:QW] + full * rows[:, width : width + QW]
    dq = rows2(local_grad[:, 0 : HC + QP], w_query_t[...])
    dq_o[...] = dq[0:oq].astype(BF16)


def pair_kernel(ni, att, dl, gw, out):
    n_row = ni * HP
    wb_t = gw[n_row : n_row + HP, :].astype(BF16)
    for i in range(ni):
        sl = slice(i * HP, (i + 1) * HP)
        ah, al = split2(att[sl, :])
        dh, dlo = split2(dl[sl, :] * WL)
        gh, gl = split2(gw[sl, :])
        left = jnp.concatenate([ah, al, ah, dh, dlo], axis=0)
        right = jnp.concatenate([gh, gh, gl, wb_t, wb_t], axis=0)
        out[i] = dot(left, right, 0, 0).astype(BF16)


class Kept:
    def __init__(self, value):
        self.value = value


def call(kernel, outs, args, far=(), cut=None, kept=(), smem=0, scratch=(), name=None, limit=24):
    n_in, n_out = len(args), len(outs)
    held = [k for k, x in enumerate(args) if isinstance(x, Kept)]
    args = [x.value if isinstance(x, Kept) else x for x in args]
    far, far_out, after = list(far), [], []
    cut = cut or {}

    def body(*refs):
        ins, rest = list(refs[:n_in]), list(refs[n_in:])
        results, rest = rest[:n_out], rest[n_out:]
        own, rest = rest[: len(scratch)], rest[len(scratch) :]
        bufs, rest = rest[: len(far)], rest[len(far) :]
        out_bufs, sems = rest[: len(far_out)], rest[len(far_out) :]
        for k, (at, buf) in enumerate(zip(far, bufs)):
            src = ins[at]
            if at in cut:
                src = src.at[pl.ds(args[at].shape[0] - cut[at], cut[at]), :]
            ins[at] = Fetched(src, buf, sems[0].at[k])
        targets = list(results)
        for at, buf in zip(far_out, out_bufs):
            targets[at] = buf
        kernel(*ins, *targets, *own)
        copies = [
            pltpu.make_async_copy(buf, results[at], sems[0].at[len(far) + k])
            for k, (at, buf) in enumerate(zip(far_out, out_bufs))
        ]
        for copy in copies:
            copy.start()
        for at in far:
            ins[at].get()
        for copy in copies:
            copy.wait()

    specs = []
    for k in range(n_in):
        space = pltpu.SMEM if k < smem else pltpu.HBM if k in far or k in after else pltpu.VMEM
        specs.append(pl.BlockSpec(memory_space=space))
    results = pl.pallas_call(
        body,
        out_shape=[
            pltpu.VMEM(s, d) if k in kept else jax.ShapeDtypeStruct(s, d)
            for k, (s, d) in enumerate(outs)
        ],
        in_specs=specs,
        out_specs=[
            pl.BlockSpec(memory_space=pltpu.HBM if k in far_out else pltpu.VMEM)
            for k in range(n_out)
        ],
        scratch_shapes=[pltpu.VMEM(s, d) for s, d in scratch]
        + [pltpu.VMEM((cut.get(k, args[k].shape[0]),) + args[k].shape[1:], args[k].dtype)
           for k in far]
        + [pltpu.VMEM(*outs[k]) for k in far_out]
        + ([pltpu.SemaphoreType.DMA((len(far) + len(far_out),))] if far or far_out else []),
        compiler_params=pltpu.CompilerParams(vmem_limit_bytes=limit * 1024 * 1024),
        name=name,
    )(*[
        pltpu.with_memory_space_constraint(x, pltpu.HBM) if k in far
        else pltpu.with_memory_space_constraint(x, pltpu.VMEM) if k in held else x
        for k, x in enumerate(args)
    ])
    return [Kept(x) if k in kept else x for k, x in enumerate(results)]


def load(params, after):
    n = len(params)
    results = pl.pallas_call(
        functools.partial(load_kernel, n),
        out_shape=[pltpu.VMEM(x.shape, x.dtype) for x in params],
        in_specs=[pl.BlockSpec(memory_space=pltpu.VMEM)]
        + [pl.BlockSpec(memory_space=pltpu.HBM)] * n,
        out_specs=[pl.BlockSpec(memory_space=pltpu.VMEM)] * n,
        scratch_shapes=[pltpu.SemaphoreType.DMA((n,))],
        compiler_params=pltpu.CompilerParams(vmem_limit_bytes=2 * 1024 * 1024),
        name="load",
    )(after, *[pltpu.with_memory_space_constraint(x, pltpu.HBM) for x in params])
    return [Kept(x) for x in results]


def local(
    q_single, k_single, q_frames, k_frames, pair_tile, w_query, w_key, w_bias, w_out,
    head_weight, chain_bias, q_chain, k_chain, k_mask, d_update,
):
    pbc = lax.axis_size("pb")
    kac = lax.axis_size("ka")
    pb = lax.axis_index("pb")
    ka = lax.axis_index("ka")
    ni, nj, cp = pair_tile.shape
    oq, width = q_single.shape
    nk = k_single.shape[0]
    slot = -(-2 * oq // 8) * 8
    w_query_t, w_key_t, w_bias_t = (jnp.transpose(x) for x in (w_query, w_key, w_bias))

    def ka_xor(x, d):
        return lax.ppermute(x, "ka", [(i, i ^ d) for i in range(kac)])

    def pb_xor(x, d):
        return lax.ppermute(x, "pb", [(i, i ^ d) for i in range(pbc)])

    n_row = ni * HP
    f32 = lambda *s: (s, F32)
    bf16 = lambda *s: (s, BF16)
    k_rows = width // 128 * nk + 16
    pk, pq = call(
        functools.partial(pack_kernel, pbc),
        [f32(k_rows, 128), f32(slot, width + 128)],
        [k_single, k_frames, q_single, jnp.transpose(q_frames), d_update],
        far=range(5),
        name="pack",
    )
    own_pieces = [pq] + [ka_xor(pq, 2 * d) for d in range(1, kac // 2)]
    routed = call(
        functools.partial(route_kernel, pbc),
        [f32(k_rows, 128)] * pbc + [f32(kac // 2, slot, width + 128)],
        [pk] + [pb_xor(pk, d) for d in range(1, pbc)] + own_pieces,
        scratch=[f32(pbc, k_rows, 128)],
        name="route",
    )
    query_own = routed[pbc]
    query_other = ka_xor(query_own, 1)
    key_pieces = [
        lax.ppermute(
            routed[s], "ka",
            [(a, ((a % pbc) ^ s) * 2 + a // pbc) for a in range(kac)],
        )
        for s in range(pbc)
    ]
    params = [pair_tile, w_out, w_query_t, w_key_t]
    pair_v, w_out_v, w_query_v, w_key_v = load(params, pk)
    base, dap, gw, q_feat, qt, l1, l2, l3, dmh, dml, dvt, dlt, frt = call(
        functools.partial(query_kernel, ni, kac, oq, slot),
        [f32(n_row, nj), f32(n_row, nj), f32(n_row + 2 * HP, cp), f32(ni, QW), f32(QW, 128),
         bf16(n_row, QW), bf16(n_row, QW), bf16(n_row, QW), bf16(n_row, 256), bf16(n_row, 256),
         f32(256, 128), f32(384, 128), f32(128, 128)],
        [q_chain, query_own, query_other, pair_v, w_query_v, w_out_v, w_bias_t,
         head_weight[None, :], chain_bias[None, :], k_chain[None, :]],
        far=range(6, 10),
        kept=range(13),
        smem=1,
        scratch=[f32(kac * slot, width + 128), f32(128, QW), f32(128, 384)],
        name="query",
    )
    weights, da, pay, kq, vt = call(
        functools.partial(key_kernel, ni, nk, pbc),
        [f32(n_row, nj), f32(n_row, nj), f32(ni, PW), f32(QW, nj), f32(HC + PW, nj)],
        [*key_pieces, w_key_v, base, l1, l2, l3, dmh, dml, dap, gw, k_mask[None, :]],
        far=[pbc + 9],
        kept=[0, 1, 3, 4],
        scratch=[f32(nj, width), f32(w_key_t.shape[0], nj)],
        name="key",
    )
    lh, ll, dvh, dvl = call(
        functools.partial(spread_kernel, ni),
        [bf16(HC + QP, n_row), bf16(HC + QP, n_row), bf16(HC, n_row), bf16(HC, n_row)],
        [qt, dvt, gw],
        kept=range(4),
        name="spread",
    )
    (u,) = call(
        functools.partial(value_kernel, ni),
        [f32(H, ni, width)],
        [weights, pair_v, vt, w_out_v],
        kept=[0],
        scratch=[f32(n_row, cp), f32(n_row, 128), f32(n_row, 128)],
        name="value",
    )
    total = pay
    step = 1
    while step < kac:
        (total,) = call(
            combine_kernel, [f32(ni, PW)], [total, ka_xor(total, step)], name="combine"
        )
        step *= 2
    chips = kac // 2
    wide = 3 * width + 128
    att, dl0, mine, theirs, keyv = call(
        functools.partial(grad_kernel, ni, oq, kac),
        [f32(n_row, nj), f32(n_row, nj), f32(ni // 2, wide), f32(ni // 2, wide), f32(nj, width)],
        [total, pay, weights, da, dap, q_feat, dlt, frt, kq, vt, u, dvh, dvl, gw, w_out_v,
         w_key_v],
        kept=[0, 1, 4],
        scratch=[f32(128, 384), f32(384, 128), f32(nj, 640), f32(640, nj)],
        name="grad",
    )
    slices = call(
        functools.partial(mid_kernel, oq, chips, width),
        [f32(oq, 3 * width + HP // oq * 128)] * chips,
        [mine, ka_xor(theirs, 1)],
        name="mid",
    )
    slices = [slices[0]] + [ka_xor(slices[d], 2 * d) for d in range(1, chips)]
    fixed = call(
        functools.partial(keyfix_kernel, ni, oq, width, chips, pbc),
        [f32(n_row, nj)] + [f32(nj // pbc, width)] * pbc,
        [*slices, att, dl0, lh, ll, kq, gw, keyv, w_key_v],
        kept=[0],
        scratch=[f32(128, 128), f32(512, nj), f32(nj, 512), f32(nj, width)],
        name="keyfix",
    )
    dl, blocks = fixed[0], fixed[1:]
    update, d_query = call(
        functools.partial(ownfix_kernel, oq, width, chips),
        [bf16(oq, width), bf16(oq, width)],
        [*slices, w_query_v],
        scratch=[f32(128, 128), f32(8, 2 * width)],
        name="ownfix",
    )
    (d_pair,) = call(
        functools.partial(pair_kernel, ni),
        [((ni, nj, cp), BF16)],
        [att, dl, gw],
        name="pair",
    )
    key_own = blocks[0]
    for d in range(1, pbc):
        key_own = key_own + pb_xor(blocks[d], d)
    return update, d_pair, d_query, key_own


def solution(mesh):
    both = ("pb", "ka")
    placed = (
        P(both, None), P(both, None), P(None, both), P(None, both), P("pb", "ka", None),
        P(), P(), P(), P(), P(), P(), P("pb"), P("ka"), P("ka"), P(both, None),
    )
    return jax.shard_map(
        local,
        mesh=mesh,
        in_specs=placed,
        out_specs=(
            P(both, None), P("pb", "ka", None), P(both, None), P(("ka", "pb"), None),
        ),
        check_vma=False,
    )
```

```python
import functools
import math

import jax
import jax.numpy as jnp
from jax import lax
from jax.experimental import pallas as pl
from jax.experimental.pallas import tpu as pltpu
from jax.sharding import PartitionSpec as P

H = 12
HP = 16
HEAD = 16
PQ = 4
PV = 8
HC = H * HEAD
QP = 3 * H * PQ
VP = 3 * H * PV
QW = 384
PW = 384
MASKED = -1000000000.0
WL = math.sqrt(1.0 / 3.0)
F32 = jnp.float32
BF16 = jnp.bfloat16


def dot(a, b, ca=1, cb=0, precision=None):
    return lax.dot_general(
        a, b, (((ca,), (cb,)), ((), ())), precision=precision, preferred_element_type=F32
    )


def dot_full(a, b, ca=1, cb=0):
    return dot(a, b, ca, cb, lax.Precision.HIGHEST)


def split2(x):
    high = x.astype(BF16)
    return high, (x - high.astype(F32)).astype(BF16)


def split3(x):
    high = x.astype(BF16)
    rest = x - high.astype(F32)
    mid = rest.astype(BF16)
    return high, mid, (rest - mid.astype(F32)).astype(BF16)


def rows3(x, b, ca=1, cb=0):
    n = x.shape[0]
    out = dot(jnp.concatenate(split3(x), axis=0), b, ca, cb)
    return out[0:n] + out[n : 2 * n] + out[2 * n : 3 * n]


def rows2(x, b, ca=1, cb=0):
    n = x.shape[0]
    out = dot(jnp.concatenate(split2(x), axis=0), b, ca, cb)
    return out[0:n] + out[n : 2 * n]


def pair3(a, b, ca=1, cb=0):
    ah, al = split2(a)
    bh, bl = split2(b)
    return dot(ah, bh, ca, cb) + (dot(ah, bl, ca, cb) + dot(al, bh, ca, cb))


def per_head(x, n):
    return jnp.broadcast_to(x[:, None, :], (n, HP, x.shape[1])).reshape(n * HP, x.shape[1])


def tiled(x, n):
    return jnp.broadcast_to(x[None], (n,) + x.shape).reshape(n * HP, x.shape[1])


def head_sum(x, n):
    return jnp.sum(x.reshape(n, HP, x.shape[1]), axis=1)


def frame_row(fr, index):
    return fr[index : index + 1, :]


def to_world(fr, loc, rows):
    out = []
    for x in range(3):
        acc = frame_row(fr, 9 + x) + frame_row(fr, 3 * x) * loc[0]
        for y in range(1, 3):
            acc = acc + frame_row(fr, 3 * x + y) * loc[y]
        out.append(acc)
    return out


def to_local(fr, g):
    out = []
    for y in range(3):
        acc = frame_row(fr, y) * g[0]
        for x in range(1, 3):
            acc = acc + frame_row(fr, 3 * x + y) * g[x]
        out.append(acc)
    return out


def three(x, rows):
    return [x[k * rows : (k + 1) * rows] for k in range(3)]


def transpose_tiles(dst, src, tiles):
    for t in range(tiles):
        dst[t * 128 : (t + 1) * 128, :] = jnp.transpose(src[:, t * 128 : (t + 1) * 128])


def column(row, n):
    at = lax.broadcasted_iota(jnp.int32, (HP, n), 0) == lax.broadcasted_iota(
        jnp.int32, (HP, n), 1
    )
    return jnp.sum(jnp.where(at, jnp.broadcast_to(row, (HP, n)), 0.0), axis=1, keepdims=True)


def coefficient(head_weight):
    x = head_weight[...]
    soft = jnp.maximum(x, 0.0) + jnp.log1p(jnp.exp(-jnp.abs(x)))
    return column(WL * soft * math.sqrt(2.0 / (9.0 * PQ)) / 2.0, H)


def rows_mask(blocks, width):
    parts = []
    for rows, shift in blocks:
        head = lax.broadcasted_iota(jnp.int32, (rows, width), 0) >> shift
        parts.append(head == (lax.broadcasted_iota(jnp.int32, (rows, width), 1) & (HP - 1)))
    return parts


def expand_rows(x, blocks, expand):
    keep = rows_mask(blocks, expand.shape[1])
    out = []
    for part in split2(x):
        wide = dot(part, expand)
        pieces, start = [], 0
        for (rows, _), mask in zip(blocks, keep):
            pieces.append(jnp.where(mask, wide[start : start + rows], 0.0).astype(BF16))
            start += rows
        out.append(jnp.concatenate(pieces, axis=0))
    return out


Q_BLOCKS = ((HC, 4),) + ((H * PQ, 2),) * 3
V_BLOCKS = ((HC, 4),)
P_BLOCKS = ((H * PV, 3),) * 3


def grid(shape):
    return tuple(lax.broadcasted_iota(jnp.int32, shape, d) for d in range(2))


def lanes_of(shape, row, blocks):
    lane = lax.broadcasted_iota(jnp.int32, shape, 1)
    keep = None
    for first, count, shift in blocks:
        hit = (lane >= first) & (lane < first + count) & (((lane - first) >> shift) == row)
        keep = hit if keep is None else keep | hit
    return keep


Q_LANES = ((0, HC, 4),) + tuple((HC + x * H * PQ, H * PQ, 2) for x in range(3))
V_LANES = ((0, HC, 4),)
P_LANES = tuple((x * H * PV, H * PV, 3) for x in range(3))


def head_mask(width, blocks):
    shape = (HP, width)
    return lanes_of(shape, grid(shape)[0], blocks).astype(F32)


def stat_mask(width, first):
    row, lane = grid((HP, width))
    return (lane == row + first).astype(F32)


def spread_mask(offset):
    shape = (128, PW)
    head = grid(shape)[0] - (VP - 256) - offset
    lane = grid(shape)[1]
    keep = lanes_of(shape, head, P_LANES)
    for k in range(3):
        keep = keep | (lane == head + VP + k * HP)
    return (keep & (head >= 0) & (head < H)).astype(F32)


def to_column(x, ni, first):
    return jnp.sum(per_head(x, ni) * tiled(stat_mask(128, first), ni), axis=1, keepdims=True)


def expand_mask(ni):
    row, lane = grid((ni, ni * HP))
    return ((lane // HP) == row).astype(BF16)


def row_order(ni, ka, oq, slot):
    row, lane = grid((2 * ni, ka * slot))
    shift = oq.bit_length() - 1
    index = row & (ni - 1)
    source = (index >> shift) * slot + (index & (oq - 1))
    return (lane == source + jnp.where(row >= ni, oq, 0)).astype(F32)


class Fetched:
    def __init__(self, src, dst, sem):
        self.ref, self.pending = dst, pltpu.make_async_copy(src, dst, sem)
        self.shape = dst.shape
        self.pending.start()

    def get(self):
        if self.pending is not None:
            self.pending.wait()
            self.pending = None
        return self.ref

    def __getitem__(self, index):
        return self.get()[index]


def pack_kernel(pbc, k, kf, q, qf, du, pk, pq):
    nk, width = k.shape
    oq = q.shape[0]
    spot = lax.rem(lax.axis_index("ka"), pbc)
    for t in range(width // 128):
        pk[t * nk : (t + 1) * nk, :] = k[:, t * 128 : (t + 1) * 128]
    row = lax.broadcasted_iota(jnp.int32, (nk, 128), 0)
    lane = lax.broadcasted_iota(jnp.int32, (nk, 128), 1)
    pk[width // 128 * nk :, :] = jnp.zeros_like(pk[width // 128 * nk :, :])
    pk[width // 128 * nk : width // 128 * nk + 12, :] = dot_full(
        kf[...], (lane == row + spot * nk).astype(F32)
    )
    pq[...] = jnp.zeros_like(pq)
    pq[0:oq, 0:width] = q[...]
    pq[0:oq, width : width + 12] = qf[...]
    pq[oq : 2 * oq, 0:width] = du[...]


def route_kernel(pbc, _, *refs):
    pieces, rest = refs[:pbc], refs[pbc:]
    held = rest[-1]
    chips = (len(rest) - pbc - 2)
    rows, outs, gathered = rest[:chips], rest[chips : chips + pbc], rest[chips + pbc]
    chip = lax.axis_index("ka") // 2
    mine = lax.axis_index("pb")
    for d in range(pbc):
        held[d] = pieces[d][...]
    for s in range(pbc):
        outs[s][...] = held[(chip ^ s) ^ mine]
    for d in range(chips):
        gathered[d] = rows[d][...]


def sort_kernel(chips, _, *refs):
    pieces, (keep, give, held) = refs[:chips], refs[chips:]
    me = lax.axis_index("ka")
    for d in range(chips):
        held[d] = pieces[-d][...]
    half = chips // 2
    for k in range(half):
        keep[k] = held[(lax.rem(me, 2) * half + k) ^ (me // 2)]
        give[k] = held[((lax.rem(me, 2) ^ 1) * half + k) ^ (me // 2)]


def load_kernel(n, *refs):
    sources, targets, sems = refs[1 : 1 + n], refs[1 + n : 1 + 2 * n], refs[1 + 2 * n]
    copies = [
        pltpu.make_async_copy(x, y, sems.at[k]) for k, (x, y) in enumerate(zip(sources, targets))
    ]
    for copy in copies:
        copy.start()
    for copy in copies:
        copy.wait()


def query_kernel(ni, ka, oq, slot, q_chain, *refs):
    pieces = refs[:2]
    (pair, w_query_t, w_out, w_bias_t, head_weight, chain_bias, k_chain,
     base_o, dap_o, gw_o, q_o, qt_o, l1_o, l2_o, l3_o, dmh_o, dml_o, dv_o, du_o, frt_o,
     qd, nat) = refs[2:]
    me = lax.axis_index("ka")
    chip, core = me // 2, lax.rem(me, 2)
    for d in range(ka // 2):
        for e in range(2):
            owner = (chip ^ d) * 2 + (core ^ e)
            qd[pl.ds(pl.multiple_of(owner * slot, 8), slot), :] = pieces[e][d]
    n_row = ni * HP
    gw_o[...] = jnp.zeros_like(gw_o)
    rows = dot_full(row_order(ni, ka, oq, slot), qd[...])
    width = w_query_t.shape[1]
    q_raw, d_up = rows[:ni, :width], rows[ni:, :width]
    nat[...] = jnp.zeros_like(nat)
    nat[0:ni, 0:128] = rows[:ni, width : width + 128]
    nat[ni : 2 * ni, 0:128] = rows[:ni, width : width + 128]
    frt_o[...] = jnp.transpose(nat[:, 0:128])
    fr = frt_o[...]
    nat[...] = jnp.zeros_like(nat)
    nat[0:ni, 0 : HC + QP] = rows3(q_raw, w_query_t[...], 1, 1)
    transpose_tiles(qt_o, nat, QW // 128)
    rp = H * PQ
    world = to_world(fr, three(qt_o[HC : HC + QP, :], rp), rp)
    for x in range(3):
        qt_o[HC + x * rp : HC + (x + 1) * rp, :] = world[x]
    for t in range(QW // 128):
        nat[:, t * 128 : (t + 1) * 128] = jnp.transpose(qt_o[t * 128 : (t + 1) * 128, :])
    q_o[...] = nat[0:ni, :]
    gw_o[n_row : n_row + H, :] = w_bias_t[...].astype(F32)
    wb_t = gw_o[n_row : n_row + HP, :].astype(BF16)
    coef = coefficient(head_weight)
    gw_o[n_row + HP :, :] = jnp.broadcast_to(coef, (HP, gw_o.shape[1]))
    chain = column(chain_bias[...], H)
    mq = head_mask(QW, Q_LANES)
    is_pt = lax.broadcasted_iota(jnp.int32, (HP, QW), 1) >= HC
    q_rows = per_head(nat[0:ni, :], ni)
    left = q_rows * tiled(mq * jnp.where(is_pt, 2.0 * coef, WL / math.sqrt(HEAD)), ni)
    l1_o[...], l2_o[...], l3_o[...] = split3(left)
    q_sq = 0.5 * jnp.sum(
        left * jnp.where(lax.broadcasted_iota(jnp.int32, left.shape, 1) >= HC, q_rows, 0.0),
        axis=1, keepdims=True,
    )
    split = jnp.concatenate(split3(d_up), axis=0)

    def d_out(lo, hi):
        out = dot(split, w_out[lo:hi, :], 1, 1)
        return out[0:ni] + out[ni : 2 * ni] + out[2 * ni : 3 * ni]

    du_o[...] = d_up
    dv_o[...] = jnp.zeros_like(dv_o)
    dv_o[0:ni, 0:HC] = d_out(0, HC)
    dmh_o[...], dml_o[...] = split2(
        per_head(dv_o[0:ni, :], ni) * tiled(head_mask(256, V_LANES), ni)
    )
    cp = pair.shape[2]
    for h in range(H):
        gw_o[pl.ds(h, ni, stride=HP), :] = d_out(HC + h * cp, HC + (h + 1) * cp)
    for i in range(ni):
        gh, gl = split2(gw_o[i * HP : (i + 1) * HP, :])
        out = dot(jnp.concatenate([wb_t, gh, gl], axis=0), pair[i], 1, 1)
        sl = slice(i * HP, (i + 1) * HP)
        cross = jnp.where(k_chain[...] != q_chain[i], chain, 0.0)
        base_o[sl, :] = WL * out[0:HP] - q_sq[sl] + cross
        dap_o[sl, :] = out[HP : 2 * HP] + out[2 * HP : 3 * HP]


def key_kernel(ni, nk, n_pieces, *refs):
    pieces = refs[:2]
    (w_key_t, base, l1, l2, l3, dmh, dml, dap, gw, k_mask,
     w_o, da_o, pay_o, kq_o, vt_o, kraw, kt) = refs[2:]
    core = lax.rem(lax.axis_index("ka"), 2)
    width = w_key_t.shape[1]
    tiles = width // 128
    fr = None
    for k in range(n_pieces // 2):
        for e in range(2):
            start = pl.multiple_of((2 * k + (core ^ e)) * nk, 8)
            for t in range(tiles):
                kraw[pl.ds(start, nk), t * 128 : (t + 1) * 128] = pieces[e][
                    k, t * nk : (t + 1) * nk, :
                ]
            part = pieces[e][k, tiles * nk : tiles * nk + 16, :]
            fr = part if fr is None else fr + part
    parts = split3(kraw[...])
    w_t = w_key_t[...]
    kt[...] = dot(w_t, parts[0], 1, 1) + (dot(w_t, parts[1], 1, 1) + dot(w_t, parts[2], 1, 1))
    rk, rv = H * PQ, H * PV
    kp = to_world(fr, three(kt[2 * HC : 2 * HC + QP, :], rk), rk)
    vp = to_world(fr, three(kt[2 * HC + QP : 2 * HC + QP + VP, :], rv), rv)
    kq_o[0:HC, :] = kt[0:HC, :]
    vt_o[0:HC, :] = kt[HC : 2 * HC, :]
    for x in range(3):
        kq_o[HC + x * rk : HC + (x + 1) * rk, :] = kp[x]
        vt_o[HC + x * rv : HC + (x + 1) * rv, :] = vp[x]
    kq_o[HC + QP : HC + QP + 16, :] = fr
    kq_o[HC + QP + 16 :, :] = jnp.zeros_like(kq_o[HC + QP + 16 :, :])
    vt_o[HC + VP :, :] = jnp.zeros_like(vt_o[HC + VP :, :])
    mq = head_mask(QW, Q_LANES)
    coef = gw[ni * HP + HP :, 0:1]
    kpt = kq_o[HC : HC + QP, :]
    k_sq = dot_full(mq[:, HC : HC + QP] * coef, kpt * kpt)
    k1, k2, k3 = split3(kq_o[...])
    logits = dot(l2[...], k2) + (dot(l1[...], k3) + dot(l3[...], k1))
    logits = logits + (dot(l1[...], k2) + dot(l2[...], k1))
    logits = logits + dot(l1[...], k1)
    logits = logits + base[...] - tiled(k_sq, ni)
    logits = jnp.where(k_mask[...] == 1, logits, MASKED)
    top = jnp.max(logits, axis=1, keepdims=True)
    weights = jnp.exp(logits - top)
    w_o[...] = weights
    total = jnp.sum(weights, axis=1, keepdims=True)
    vh, vl = split2(vt_o[...])
    da = dap[...] + cross3(dmh[...], dml[...], vh[0:256], vl[0:256])
    da_o[...] = da
    s_sum = jnp.sum(weights * da, axis=1, keepdims=True)
    wh, wl = split2(weights)
    ph, po = vh[HC : HC + PW], vl[HC : HC + PW]
    num = dot(wh, ph, 1, 1) + (dot(wh, po, 1, 1) + dot(wl, ph, 1, 1))
    num = num * tiled(head_mask(PW, P_LANES), ni)
    for k, value in enumerate((top, total, s_sum)):
        num = num + value * tiled(stat_mask(PW, VP + k * HP), ni)
    pay_o[...] = head_sum(num, ni)


def combine_kernel(*refs):
    parts, out = refs[:-1], refs[-1]
    n = parts[0].shape[0]
    tops = dot_full(jnp.concatenate([x[:, 256:384] for x in parts], axis=0), spread_mask(0))
    tops = [tops[k * n : (k + 1) * n] for k in range(len(parts))]
    top = functools.reduce(jnp.maximum, tops)
    lane = lax.broadcasted_iota(jnp.int32, top.shape, 1)
    mixed = None
    for x, t in zip(parts, tops):
        term = x[...] * jnp.exp(t - top)
        mixed = term if mixed is None else mixed + term
    out[...] = jnp.where((lane >= VP) & (lane < VP + HP), top, mixed)


def value_kernel(ni, w, pair, vt, w_out, u_o, npx, nv0, nv1):
    cp = pair.shape[2]
    for i in range(ni):
        wh, wl = split2(w[i * HP : (i + 1) * HP, :])
        out = dot(jnp.concatenate([wh, wl], axis=0), pair[i], 1, 0)
        npx[i * HP : (i + 1) * HP, :] = out[0:HP] + out[HP : 2 * HP]
    nv = pair3(w[...], vt[0:256, :], 1, 1) * tiled(head_mask(256, V_LANES), ni)
    nv0[...] = nv[:, 0:128]
    nv1[...] = nv[:, 128:256]
    for h in range(H):
        t = h * HEAD // 128
        wv = w_out[t * 128 : min(t * 128 + 128, HC), :]
        part = (nv0, nv1)[t][pl.ds(h, ni, stride=HP), :]
        u_o[h] = rows2(
            npx[pl.ds(h, ni, stride=HP), :], w_out[HC + h * cp : HC + (h + 1) * cp, :]
        ) + rows2(part[:, 0 : wv.shape[0]], wv)


def spread_kernel(ni, qt, dv, du, gw, w_out, lh_o, ll_o, dh_o, dlo_o, dlt_o, nat, dvt):
    e = expand_mask(ni)
    rq = H * PQ
    head = lax.broadcasted_iota(jnp.int32, (rq, HP), 0) >> 2
    pick = (head == lax.broadcasted_iota(jnp.int32, (rq, HP), 1)).astype(F32)
    twice = 2.0 * dot_full(pick, gw[ni * HP + HP :, :])[:, 0:1]
    qs = qt[0:HC, 0:ni] * (WL / math.sqrt(HEAD))
    qp = qt[HC : HC + QP, 0:ni] * jnp.concatenate([twice] * 3, axis=0)
    lh_o[...], ll_o[...] = expand_rows(jnp.concatenate([qs, qp], axis=0), Q_BLOCKS, e)
    transpose_tiles(dvt, dv, 2)
    dh_o[...], dlo_o[...] = expand_rows(dvt[0:HC, 0:ni], V_BLOCKS, e)
    nat[...] = jnp.zeros_like(nat)
    nat[0:ni, :] = rows3(du[...], w_out[w_out.shape[0] - PW :, :], 1, 1)
    transpose_tiles(dlt_o, nat, 3)


def cross3(ah, al, bh, bl):
    return dot(ah, bh) + (dot(ah, bl) + dot(al, bh))


def grad_kernel(
    ni, oq, ka, pay, pay_loc, w, da, dap, q_feat, dlt, frt, kq, vt, u, gw, w_out,
    att_o, dl_o, mine_o, theirs_o, dpt_o, nat, tr,
):
    me = lax.axis_index("ka")
    fr = frt[...]
    width = u.shape[2]
    mp, mq = head_mask(PW, P_LANES), head_mask(QW, Q_LANES)
    tops = dot_full(
        jnp.concatenate([pay[:, 256:384], pay_loc[:, 256:384]], axis=0), spread_mask(0)
    )
    grow = jnp.exp(tops[ni : 2 * ni] - tops[0:ni])
    totals = dot_full(pay[:, 256:384], spread_mask(HP))
    inv = jnp.where(totals > 0.0, 1.0 / totals, 0.0)
    inv_col = to_column(inv[:, 256:384], ni, VP - 256)
    weights = w[...] * to_column(grow[:, 256:384], ni, VP - 256)
    att = weights * inv_col
    att_o[...] = att
    lost = jnp.sum(
        (weights - weights.astype(BF16).astype(F32)) * dap[...], axis=1, keepdims=True
    )
    nat[...] = jnp.zeros_like(nat)
    nat[0:ni, 0:128] = head_sum(lost * inv_col * tiled(stat_mask(128, 0), ni), ni)
    eps_t = jnp.transpose(nat[:, 0:128])[0:HP, :]
    scaled = pay[...] * inv
    nat[0:ni, :] = scaled
    transpose_tiles(tr, nat, 3)
    rv = H * PV
    out_pt = three(tr[0:VP, :], rv)
    shifted = [out_pt[x] - frame_row(fr, 9 + x) for x in range(3)]
    loc = to_local(fr, shifted)
    length = jnp.sqrt(loc[0] * loc[0] + loc[1] * loc[1] + loc[2] * loc[2] + 1e-08)
    ratio = dlt[VP : VP + rv, :] / length
    d_loc = [dlt[y * rv : (y + 1) * rv, :] + ratio * loc[y] for y in range(3)]
    d_pt = []
    for x in range(3):
        acc = frame_row(fr, 3 * x) * d_loc[0]
        for y in range(1, 3):
            acc = acc + frame_row(fr, 3 * x + y) * d_loc[y]
        d_pt.append(acc)
    for y in range(3):
        tr[y * rv : (y + 1) * rv, :] = loc[y]
    tr[VP : VP + rv, :] = length
    for t in range(3):
        nat[:, t * 128 : (t + 1) * 128] = jnp.transpose(tr[t * 128 : (t + 1) * 128, :])
    own = rows2(nat[0:ni, :], w_out[w_out.shape[0] - PW :, :])
    row = lax.broadcasted_iota(jnp.int32, (ni, 1), 0)
    upd = jnp.where((row >= me * oq) & (row < (me + 1) * oq), own, 0.0)
    share = inv * grow
    for h in range(H):
        upd = upd + u[h] * share[:, VP + h : VP + h + 1]
    for x in range(3):
        tr[x * rv : (x + 1) * rv, :] = d_pt[x]
    tr[VP:, :] = jnp.zeros_like(tr[VP:, :])
    dpt_o[...] = tr[0:VP, :]
    for t in range(3):
        nat[:, t * 128 : (t + 1) * 128] = jnp.transpose(tr[t * 128 : (t + 1) * 128, :])
    d_nat = nat[0:ni, :]
    lane = lax.broadcasted_iota(jnp.int32, (ni, PW), 1)
    dots = jnp.where(lane < VP, d_nat * scaled, scaled)
    delta = jnp.sum(
        per_head(dots, ni) * tiled(mp + stat_mask(PW, VP + 2 * HP), ni), axis=1, keepdims=True
    )
    dptm = per_head(d_nat, ni) * tiled(mp, ni)
    d_att = da[...] + pair3(dptm, vt[HC : HC + PW, :])
    dl = att * (d_att - delta)
    dl_o[...] = dl
    coef = gw[ni * HP + HP :, 0:1]
    lane_h = lax.broadcasted_iota(jnp.int32, (HP, QW), 1)
    scale = tiled(mq * jnp.where(lane_h >= HC, 2.0 * coef, WL / math.sqrt(HEAD)), ni)
    kh, kl = split2(kq[...])
    points = per_head(jnp.where(lane >= HC, q_feat[...], 0.0), ni)
    dlh, dll = split2(dl)
    ath, atl = split2(att)
    for k, (full, high, low) in enumerate(((dl, dlh, dll), (att, ath, atl))):
        gq = dot(high, kh, 1, 1) + (dot(high, kl, 1, 1) + dot(low, kh, 1, 1))
        gq = gq - points * jnp.sum(full, axis=1, keepdims=True)
        nat[k * ni : (k + 1) * ni, :] = head_sum(gq * scale, ni)
    nat[2 * ni :, :] = jnp.zeros_like(nat[2 * ni :, :])
    transpose_tiles(tr, nat, 3)
    rq = H * PQ
    gl = to_local(fr, three(tr[HC : HC + QP, :], rq))
    for x in range(3):
        tr[HC + x * rq : HC + (x + 1) * rq, :] = gl[x]
    for t in range(3):
        nat[:, t * 128 : (t + 1) * 128] = jnp.transpose(tr[t * 128 : (t + 1) * 128, :])
    half = ni // 2
    r32, c32 = grid((ni, ni))
    rest = r32 & (half - 1)
    shift = oq.bit_length() - 1
    source = (
        (((me // 2) ^ (rest >> shift)) * 2 + (lax.rem(me, 2) ^ jnp.where(r32 >= half, 1, 0))) * oq
        + (rest & (oq - 1))
    )
    order = (c32 == source).astype(BF16)
    for k, block in enumerate((upd, nat[0:ni, :], nat[ni : 2 * ni, :])):
        p1, p2, p3 = split3(block)
        moved = dot(order, p1) + (dot(order, p2) + dot(order, p3))
        mine_o[:, k * width : (k + 1) * width] = moved[0:half]
        theirs_o[:, k * width : (k + 1) * width] = moved[half:]
    mine_o[:, 3 * width :] = jnp.zeros_like(mine_o[:, 3 * width :])
    mine_o[0:HP, 3 * width :] = eps_t
    theirs_o[:, 3 * width :] = jnp.zeros_like(theirs_o[:, 3 * width :])
    theirs_o[0:HP, 3 * width :] = eps_t


def keyv_kernel(ni, att, dvh, dvl, dpt, kq, w_key_t, keyv_o, knat, kt):
    ath, atl = split2(att[...])
    rv = H * PV
    kt[0:HC, :] = cross3(dvh[...], dvl[...], ath, atl)
    ph, plo = expand_rows(dpt[:, 0:ni], P_BLOCKS, expand_mask(ni))
    gvl = to_local(kq[HC + QP : HC + QP + 16, :], three(cross3(ph, plo, ath, atl), rv))
    for x in range(3):
        kt[256 + x * rv : 256 + (x + 1) * rv, :] = gvl[x]
    for t in range(5):
        knat[:, t * 128 : (t + 1) * 128] = jnp.transpose(kt[t * 128 : (t + 1) * 128, :])
    keyv_o[...] = rows2(knat[:, 0:HC], w_key_t[HC : 2 * HC, :]) + rows2(
        knat[:, 256 : 256 + VP], w_key_t[2 * HC + QP :, :]
    )


def mid_kernel(ni, oq, chips, width, mine, other, *outs):
    total = mine[...] + other[...]
    per = min(128 // ni, HP // oq)
    packed = []
    for g in range(HP // oq // per):
        acc = None
        for k in range(per):
            at = (g * per + k) * oq
            part = total[at : at + oq, 3 * width :]
            part = part if k == 0 else pltpu.roll(part, k * ni, 1)
            acc = part if acc is None else acc + part
        packed.append(acc)
    packed = jnp.concatenate(packed, axis=1)
    for d in range(chips):
        outs[d][:, 0 : 3 * width] = total[d * oq : (d + 1) * oq, 0 : 3 * width]
        outs[d][:, 3 * width :] = packed


def correction(ni, oq, width, slices, eps):
    eps[...] = jnp.zeros_like(eps)
    per = min(128 // ni, HP // oq)
    for g in range(HP // oq // per):
        at = 3 * width + g * 128
        acc = slices[0][:, at : at + 128]
        for piece in slices[1:]:
            acc = acc + piece[:, at : at + 128]
        for k in range(per):
            row = (g * per + k) * oq
            eps[row : row + oq, :] = acc if k == 0 else pltpu.roll(acc, 128 - k * ni, 1)


def keyfix_kernel(ni, oq, width, chips, pbc, *refs):
    slices = refs[:chips]
    att, dl0, lh, ll, kq, gw, keyv, w_key_t = refs[chips : chips + 8]
    dl_o, outs = refs[chips + 8], refs[chips + 9 : chips + 9 + pbc]
    eps, kt, knat, total = refs[chips + 9 + pbc :]
    correction(ni, oq, width, slices, eps)
    per_query = jnp.transpose(eps[...])[0:ni, :]
    dl = dl0[...] + att[...] * to_column(per_query, ni, 0)
    dl_o[...] = dl
    dlh, dll = split2(dl)
    gk = cross3(lh[...], ll[...], dlh, dll)
    kt[0:HC, :] = gk[0:HC]
    coef = gw[ni * HP + HP :, 0:1]
    col_sum = jnp.sum(dl.reshape(ni, HP, dl.shape[1]), axis=0)
    col = dot_full(head_mask(QW, Q_LANES)[:, HC : HC + QP] * (2.0 * coef), col_sum, 0, 0)
    rq = H * PQ
    gkp = gk[HC : HC + QP] - col * kq[HC : HC + QP, :]
    gkl = to_local(kq[HC + QP : HC + QP + 16, :], three(gkp, rq))
    for x in range(3):
        kt[256 + x * rq : 256 + (x + 1) * rq, :] = gkl[x]
    for t in range(4):
        knat[:, t * 128 : (t + 1) * 128] = jnp.transpose(kt[t * 128 : (t + 1) * 128, :])
    total[...] = keyv[...] + (
        rows2(knat[:, 0:HC], w_key_t[0:HC, :])
        + rows2(knat[:, 256 : 256 + QP], w_key_t[2 * HC : 2 * HC + QP, :])
    )
    block = total.shape[0] // pbc
    for d in range(pbc):
        start = pl.multiple_of((lax.axis_index("pb") ^ d) * block, 8)
        outs[d][...] = total[pl.ds(start, block), :]


def ownfix_kernel(ni, oq, width, chips, *refs):
    slices, w_query_t = refs[:chips], refs[chips]
    upd_o, dq_o, eps, rows = refs[chips + 1 :]
    correction(ni, oq, width, slices, eps)
    acc = slices[0][:, 0 : 3 * width]
    for piece in slices[1:]:
        acc = acc + piece[:, 0 : 3 * width]
    upd_o[...] = acc[:, 0:width].astype(BF16)
    rows[...] = jnp.zeros_like(rows)
    rows[0:oq, :] = acc[:, width:]
    r, lane = grid((8, 128))
    pick = (lane == lax.axis_index("ka") * oq + r).astype(F32)
    mine = dot_full(pick, eps[0:HP, :], 1, 1)
    full = dot_full(mine, head_mask(QW, Q_LANES))
    local_grad = rows[:, 0:QW] + full * rows[:, width : width + QW]
    dq = rows2(local_grad[:, 0 : HC + QP], w_query_t[...])
    dq_o[...] = dq[0:oq].astype(BF16)


def pair_kernel(ni, att, dl, gw, out):
    n_row = ni * HP
    wb_t = gw[n_row : n_row + HP, :].astype(BF16)
    for i in range(ni):
        sl = slice(i * HP, (i + 1) * HP)
        ah, al = split2(att[sl, :])
        dh, dlo = split2(dl[sl, :] * WL)
        gh, gl = split2(gw[sl, :])
        left = jnp.concatenate([ah, al, ah, dh, dlo], axis=0)
        right = jnp.concatenate([gh, gh, gl, wb_t, wb_t], axis=0)
        out[i] = dot(left, right, 0, 0).astype(BF16)


class Kept:
    def __init__(self, value):
        self.value = value


def call(kernel, outs, args, far=(), cut=None, kept=(), smem=0, scratch=(), name=None, limit=24):
    n_in, n_out = len(args), len(outs)
    held = [k for k, x in enumerate(args) if isinstance(x, Kept)]
    args = [x.value if isinstance(x, Kept) else x for x in args]
    far, far_out, after = list(far), [], []
    cut = cut or {}

    def body(*refs):
        ins, rest = list(refs[:n_in]), list(refs[n_in:])
        results, rest = rest[:n_out], rest[n_out:]
        own, rest = rest[: len(scratch)], rest[len(scratch) :]
        bufs, rest = rest[: len(far)], rest[len(far) :]
        out_bufs, sems = rest[: len(far_out)], rest[len(far_out) :]
        for k, (at, buf) in enumerate(zip(far, bufs)):
            src = ins[at]
            if at in cut:
                src = src.at[pl.ds(args[at].shape[0] - cut[at], cut[at]), :]
            ins[at] = Fetched(src, buf, sems[0].at[k])
        targets = list(results)
        for at, buf in zip(far_out, out_bufs):
            targets[at] = buf
        kernel(*ins, *targets, *own)
        copies = [
            pltpu.make_async_copy(buf, results[at], sems[0].at[len(far) + k])
            for k, (at, buf) in enumerate(zip(far_out, out_bufs))
        ]
        for copy in copies:
            copy.start()
        for at in far:
            ins[at].get()
        for copy in copies:
            copy.wait()

    specs = []
    for k in range(n_in):
        space = pltpu.SMEM if k < smem else pltpu.HBM if k in far or k in after else pltpu.VMEM
        specs.append(pl.BlockSpec(memory_space=space))
    results = pl.pallas_call(
        body,
        out_shape=[
            pltpu.VMEM(s, d) if k in kept else jax.ShapeDtypeStruct(s, d)
            for k, (s, d) in enumerate(outs)
        ],
        in_specs=specs,
        out_specs=[
            pl.BlockSpec(memory_space=pltpu.HBM if k in far_out else pltpu.VMEM)
            for k in range(n_out)
        ],
        scratch_shapes=[pltpu.VMEM(s, d) for s, d in scratch]
        + [pltpu.VMEM((cut.get(k, args[k].shape[0]),) + args[k].shape[1:], args[k].dtype)
           for k in far]
        + [pltpu.VMEM(*outs[k]) for k in far_out]
        + ([pltpu.SemaphoreType.DMA((len(far) + len(far_out),))] if far or far_out else []),
        compiler_params=pltpu.CompilerParams(vmem_limit_bytes=limit * 1024 * 1024),
        name=name,
    )(*[
        pltpu.with_memory_space_constraint(x, pltpu.HBM) if k in far
        else pltpu.with_memory_space_constraint(x, pltpu.VMEM) if k in held else x
        for k, x in enumerate(args)
    ])
    return [Kept(x) if k in kept else x for k, x in enumerate(results)]


def load(params, after):
    n = len(params)
    results = pl.pallas_call(
        functools.partial(load_kernel, n),
        out_shape=[pltpu.VMEM(x.shape, x.dtype) for x in params],
        in_specs=[pl.BlockSpec(memory_space=pltpu.VMEM)]
        + [pl.BlockSpec(memory_space=pltpu.HBM)] * n,
        out_specs=[pl.BlockSpec(memory_space=pltpu.VMEM)] * n,
        scratch_shapes=[pltpu.SemaphoreType.DMA((n,))],
        compiler_params=pltpu.CompilerParams(vmem_limit_bytes=2 * 1024 * 1024),
        name="load",
    )(after, *[pltpu.with_memory_space_constraint(x, pltpu.HBM) for x in params])
    return [Kept(x) for x in results]


def local(
    q_single, k_single, q_frames, k_frames, pair_tile, w_query, w_key, w_bias, w_out,
    head_weight, chain_bias, q_chain, k_chain, k_mask, d_update,
):
    pbc = lax.axis_size("pb")
    kac = lax.axis_size("ka")
    pb = lax.axis_index("pb")
    ka = lax.axis_index("ka")
    ni, nj, cp = pair_tile.shape
    oq, width = q_single.shape
    nk = k_single.shape[0]
    slot = -(-2 * oq // 8) * 8
    w_query_t, w_key_t, w_bias_t = (jnp.transpose(x) for x in (w_query, w_key, w_bias))

    def ka_xor(x, d):
        return lax.ppermute(x, "ka", [(i, i ^ d) for i in range(kac)])

    def pb_xor(x, d):
        return lax.ppermute(x, "pb", [(i, i ^ d) for i in range(pbc)])

    n_row = ni * HP
    f32 = lambda *s: (s, F32)
    bf16 = lambda *s: (s, BF16)
    k_rows = width // 128 * nk + 16
    pk, pq = call(
        functools.partial(pack_kernel, pbc),
        [f32(k_rows, 128), f32(slot, width + 128)],
        [k_single, k_frames, q_single, jnp.transpose(q_frames), d_update],
        far=range(5),
        name="pack",
    )
    params = [pair_tile, w_out, w_query_t, w_key_t]
    pair_v, w_out_v, w_query_v, w_key_v = load(params, pk)
    own_pieces = [pq] + [ka_xor(pq, 2 * d) for d in range(1, kac // 2)]
    routed = call(
        functools.partial(route_kernel, pbc),
        [f32(k_rows, 128)] * pbc + [f32(kac // 2, slot, width + 128)],
        [w_query_v, pk] + [pb_xor(pk, d) for d in range(1, pbc)] + own_pieces,
        scratch=[f32(pbc, k_rows, 128)],
        name="route",
    )
    query_own = routed[pbc]
    query_other = ka_xor(query_own, 1)
    crossed = [ka_xor(routed[d], 2 * d) for d in reversed(range(1, pbc))]
    base, dap, gw, q_feat, qt, l1, l2, l3, dmh, dml, dv, du, frt = call(
        functools.partial(query_kernel, ni, kac, oq, slot),
        [f32(n_row, nj), f32(n_row, nj), f32(n_row + 2 * HP, cp), f32(ni, QW), f32(QW, 128),
         bf16(n_row, QW), bf16(n_row, QW), bf16(n_row, QW), bf16(n_row, 256), bf16(n_row, 256),
         f32(128, 256), f32(ni, width), f32(128, 128)],
        [q_chain, query_own, query_other, pair_v, w_query_v, w_out_v, w_bias_t,
         head_weight[None, :], chain_bias[None, :], k_chain[None, :]],
        far=range(6, 10),
        kept=range(13),
        smem=1,
        scratch=[f32(kac * slot, width + 128), f32(128, QW)],
        name="query",
    )
    keep, give = call(
        functools.partial(sort_kernel, pbc),
        [f32(pbc // 2, k_rows, 128)] * 2,
        [q_feat, routed[0], *crossed],
        scratch=[f32(pbc, k_rows, 128)],
        name="sort",
    )
    key_pieces = [keep, ka_xor(give, 1)]
    weights, da, pay, kq, vt = call(
        functools.partial(key_kernel, ni, nk, pbc),
        [f32(n_row, nj), f32(n_row, nj), f32(ni, PW), f32(QW, nj), f32(HC + PW, nj)],
        [*key_pieces, w_key_v, base, l1, l2, l3, dmh, dml, dap, gw, k_mask[None, :]],
        far=[11],
        kept=[0, 1, 3, 4],
        scratch=[f32(nj, width), f32(w_key_t.shape[0], nj)],
        name="key",
    )
    lh, ll, dvh, dvl, dlt = call(
        functools.partial(spread_kernel, ni),
        [bf16(HC + QP, n_row), bf16(HC + QP, n_row), bf16(HC, n_row), bf16(HC, n_row),
         f32(PW, 128)],
        [qt, dv, du, gw, w_out_v],
        kept=range(5),
        scratch=[f32(128, PW), f32(256, 128)],
        name="spread",
    )
    (u,) = call(
        functools.partial(value_kernel, ni),
        [f32(H, ni, width)],
        [weights, pair_v, vt, w_out_v],
        kept=[0],
        scratch=[f32(n_row, cp), f32(n_row, 128), f32(n_row, 128)],
        name="value",
    )
    chips = kac // 2
    (near,) = call(combine_kernel, [f32(ni, PW)], [pay, ka_xor(pay, 1)], name="combine")
    (total,) = call(
        combine_kernel,
        [f32(ni, PW)],
        [near] + [ka_xor(near, 2 * d) for d in range(1, chips)],
        name="combine",
    )
    wide = 3 * width + 128
    att, dl0, mine, theirs, dpt = call(
        functools.partial(grad_kernel, ni, oq, kac),
        [f32(n_row, nj), f32(n_row, nj), f32(ni // 2, wide), f32(ni // 2, wide), f32(VP, 128)],
        [total, pay, weights, da, dap, q_feat, dlt, frt, kq, vt, u, gw, w_out_v],
        kept=[0, 1, 4],
        scratch=[f32(128, 384), f32(384, 128)],
        name="grad",
    )
    (keyv,) = call(
        functools.partial(keyv_kernel, ni),
        [f32(nj, width)],
        [att, dvh, dvl, dpt, kq, w_key_v],
        kept=[0],
        scratch=[f32(nj, 640), f32(640, nj)],
        name="keyv",
    )
    slices = call(
        functools.partial(mid_kernel, ni, oq, chips, width),
        [f32(oq, 3 * width + HP // oq // min(128 // ni, HP // oq) * 128)] * chips,
        [mine, ka_xor(theirs, 1)],
        name="mid",
    )
    slices = [slices[0]] + [ka_xor(slices[d], 2 * d) for d in reversed(range(1, chips))]
    fixed = call(
        functools.partial(keyfix_kernel, ni, oq, width, chips, pbc),
        [f32(n_row, nj)] + [f32(nj // pbc, width)] * pbc,
        [*slices, att, dl0, lh, ll, kq, gw, keyv, w_key_v],
        kept=[0],
        scratch=[f32(128, 128), f32(512, nj), f32(nj, 512), f32(nj, width)],
        name="keyfix",
    )
    dl, blocks = fixed[0], fixed[1:]
    update, d_query = call(
        functools.partial(ownfix_kernel, ni, oq, width, chips),
        [bf16(oq, width), bf16(oq, width)],
        [*slices, w_query_v],
        scratch=[f32(128, 128), f32(8, 2 * width)],
        name="ownfix",
    )
    (d_pair,) = call(
        functools.partial(pair_kernel, ni),
        [((ni, nj, cp), BF16)],
        [att, dl, gw],
        name="pair",
    )
    key_own = blocks[0]
    for d in reversed(range(1, pbc)):
        key_own = key_own + pb_xor(blocks[d], d)
    return update, d_pair, d_query, key_own


def solution(mesh):
    both = ("pb", "ka")
    placed = (
        P(both, None), P(both, None), P(None, both), P(None, both), P("pb", "ka", None),
        P(), P(), P(), P(), P(), P(), P("pb"), P("ka"), P("ka"), P(both, None),
    )
    return jax.shard_map(
        local,
        mesh=mesh,
        in_specs=placed,
        out_specs=(
            P(both, None), P("pb", "ka", None), P(both, None), P(("ka", "pb"), None),
        ),
        check_vma=False,
    )
```

```python
import functools
import math

import jax
import jax.numpy as jnp
from jax import lax
from jax.experimental import pallas as pl
from jax.experimental.pallas import tpu as pltpu
from jax.sharding import PartitionSpec as P

H = 12
HP = 16
HEAD = 16
PQ = 4
PV = 8
HC = H * HEAD
QP = 3 * H * PQ
VP = 3 * H * PV
QW = 384
PW = 384
MASKED = -1000000000.0
WL = math.sqrt(1.0 / 3.0)
F32 = jnp.float32
BF16 = jnp.bfloat16


def dot(a, b, ca=1, cb=0, precision=None):
    return lax.dot_general(
        a, b, (((ca,), (cb,)), ((), ())), precision=precision, preferred_element_type=F32
    )


def dot_full(a, b, ca=1, cb=0):
    return dot(a, b, ca, cb, lax.Precision.HIGHEST)


def split2(x):
    high = x.astype(BF16)
    return high, (x - high.astype(F32)).astype(BF16)


def split3(x):
    high = x.astype(BF16)
    rest = x - high.astype(F32)
    mid = rest.astype(BF16)
    return high, mid, (rest - mid.astype(F32)).astype(BF16)


def rows3(x, b, ca=1, cb=0):
    n = x.shape[0]
    out = dot(jnp.concatenate(split3(x), axis=0), b, ca, cb)
    return out[0:n] + out[n : 2 * n] + out[2 * n : 3 * n]


def rows2(x, b, ca=1, cb=0):
    n = x.shape[0]
    out = dot(jnp.concatenate(split2(x), axis=0), b, ca, cb)
    return out[0:n] + out[n : 2 * n]


def pair3(a, b, ca=1, cb=0):
    ah, al = split2(a)
    bh, bl = split2(b)
    return dot(ah, bh, ca, cb) + (dot(ah, bl, ca, cb) + dot(al, bh, ca, cb))


def per_head(x, n):
    return jnp.broadcast_to(x[:, None, :], (n, HP, x.shape[1])).reshape(n * HP, x.shape[1])


def tiled(x, n):
    return jnp.broadcast_to(x[None], (n,) + x.shape).reshape(n * HP, x.shape[1])


def head_sum(x, n):
    return jnp.sum(x.reshape(n, HP, x.shape[1]), axis=1)


def frame_row(fr, index):
    return fr[index : index + 1, :]


def to_world(fr, loc, rows):
    out = []
    for x in range(3):
        acc = frame_row(fr, 9 + x) + frame_row(fr, 3 * x) * loc[0]
        for y in range(1, 3):
            acc = acc + frame_row(fr, 3 * x + y) * loc[y]
        out.append(acc)
    return out


def to_local(fr, g):
    out = []
    for y in range(3):
        acc = frame_row(fr, y) * g[0]
        for x in range(1, 3):
            acc = acc + frame_row(fr, 3 * x + y) * g[x]
        out.append(acc)
    return out


def three(x, rows):
    return [x[k * rows : (k + 1) * rows] for k in range(3)]


def transpose_tiles(dst, src, tiles):
    for t in range(tiles):
        dst[t * 128 : (t + 1) * 128, :] = jnp.transpose(src[:, t * 128 : (t + 1) * 128])


def column(row, n):
    at = lax.broadcasted_iota(jnp.int32, (HP, n), 0) == lax.broadcasted_iota(
        jnp.int32, (HP, n), 1
    )
    return jnp.sum(jnp.where(at, jnp.broadcast_to(row, (HP, n)), 0.0), axis=1, keepdims=True)


def coefficient(head_weight):
    x = head_weight[...]
    soft = jnp.maximum(x, 0.0) + jnp.log1p(jnp.exp(-jnp.abs(x)))
    return column(WL * soft * math.sqrt(2.0 / (9.0 * PQ)) / 2.0, H)


def rows_mask(blocks, width):
    parts = []
    for rows, shift in blocks:
        head = lax.broadcasted_iota(jnp.int32, (rows, width), 0) >> shift
        parts.append(head == (lax.broadcasted_iota(jnp.int32, (rows, width), 1) & (HP - 1)))
    return parts


def expand_rows(x, blocks, expand):
    keep = rows_mask(blocks, expand.shape[1])
    out = []
    for part in split2(x):
        wide = dot(part, expand)
        pieces, start = [], 0
        for (rows, _), mask in zip(blocks, keep):
            pieces.append(jnp.where(mask, wide[start : start + rows], 0.0).astype(BF16))
            start += rows
        out.append(jnp.concatenate(pieces, axis=0))
    return out


Q_BLOCKS = ((HC, 4),) + ((H * PQ, 2),) * 3
V_BLOCKS = ((HC, 4),)
P_BLOCKS = ((H * PV, 3),) * 3


def grid(shape):
    return tuple(lax.broadcasted_iota(jnp.int32, shape, d) for d in range(2))


def lanes_of(shape, row, blocks):
    lane = lax.broadcasted_iota(jnp.int32, shape, 1)
    keep = None
    for first, count, shift in blocks:
        hit = (lane >= first) & (lane < first + count) & (((lane - first) >> shift) == row)
        keep = hit if keep is None else keep | hit
    return keep


Q_LANES = ((0, HC, 4),) + tuple((HC + x * H * PQ, H * PQ, 2) for x in range(3))
V_LANES = ((0, HC, 4),)
P_LANES = tuple((x * H * PV, H * PV, 3) for x in range(3))


def head_mask(width, blocks):
    shape = (HP, width)
    return lanes_of(shape, grid(shape)[0], blocks).astype(F32)


def stat_mask(width, first):
    row, lane = grid((HP, width))
    return (lane == row + first).astype(F32)


def spread_mask(offset):
    shape = (128, PW)
    head = grid(shape)[0] - (VP - 256) - offset
    lane = grid(shape)[1]
    keep = lanes_of(shape, head, P_LANES)
    for k in range(3):
        keep = keep | (lane == head + VP + k * HP)
    return (keep & (head >= 0) & (head < H)).astype(F32)


def to_column(x, ni, first):
    return jnp.sum(per_head(x, ni) * tiled(stat_mask(128, first), ni), axis=1, keepdims=True)


def expand_mask(ni):
    row, lane = grid((ni, ni * HP))
    return ((lane // HP) == row).astype(BF16)


def row_order(ni, ka, oq, slot):
    row, lane = grid((2 * ni, ka * slot))
    shift = oq.bit_length() - 1
    index = row & (ni - 1)
    source = (index >> shift) * slot + (index & (oq - 1))
    return (lane == source + jnp.where(row >= ni, oq, 0)).astype(F32)


class Fetched:
    def __init__(self, src, dst, sem):
        self.ref, self.pending = dst, pltpu.make_async_copy(src, dst, sem)
        self.shape = dst.shape
        self.pending.start()

    def get(self):
        if self.pending is not None:
            self.pending.wait()
            self.pending = None
        return self.ref

    def __getitem__(self, index):
        return self.get()[index]


def pack_kernel(pbc, k, kf, q, qf, du, pk, pq):
    nk, width = k.shape
    oq = q.shape[0]
    spot = lax.rem(lax.axis_index("ka"), pbc)
    for t in range(width // 128):
        pk[t * nk : (t + 1) * nk, :] = k[:, t * 128 : (t + 1) * 128]
    row = lax.broadcasted_iota(jnp.int32, (nk, 128), 0)
    lane = lax.broadcasted_iota(jnp.int32, (nk, 128), 1)
    pk[width // 128 * nk :, :] = jnp.zeros_like(pk[width // 128 * nk :, :])
    pk[width // 128 * nk : width // 128 * nk + 12, :] = dot_full(
        kf[...], (lane == row + spot * nk).astype(F32)
    )
    pq[...] = jnp.zeros_like(pq)
    pq[0:oq, 0:width] = q[...]
    pq[0:oq, width : width + 12] = qf[...]
    pq[oq : 2 * oq, 0:width] = du[...]


def stack_kernel(_, *refs):
    rows, out = refs[:-1], refs[-1]
    for d, row in enumerate(rows):
        out[d] = row[...]


def sort_kernel(chips, _, *refs):
    pieces, (keep, give, held) = refs[:chips], refs[chips:]
    me = lax.axis_index("ka")
    for d in range(chips):
        held[d] = pieces[-d][...]
    half = chips // 2
    at = (me // 2) ^ lax.axis_index("pb")
    for k in range(half):
        keep[k] = held[(lax.rem(me, 2) * half + k) ^ at]
        give[k] = held[((lax.rem(me, 2) ^ 1) * half + k) ^ at]


def load_kernel(n, *refs):
    sources, targets, sems = refs[1 : 1 + n], refs[1 + n : 1 + 2 * n], refs[1 + 2 * n]
    copies = [
        pltpu.make_async_copy(x, y, sems.at[k]) for k, (x, y) in enumerate(zip(sources, targets))
    ]
    for copy in copies:
        copy.start()
    for copy in copies:
        copy.wait()


def query_kernel(ni, ka, oq, slot, q_chain, *refs):
    pieces = refs[:2]
    (pair, w_query_t, w_out, w_bias_t, head_weight, chain_bias, k_chain,
     base_o, dap_o, gw_o, q_o, qt_o, l1_o, l2_o, l3_o, dmh_o, dml_o, dv_o, du_o, frt_o,
     qd, nat) = refs[2:]
    me = lax.axis_index("ka")
    chip, core = me // 2, lax.rem(me, 2)
    for d in range(ka // 2):
        for e in range(2):
            owner = (chip ^ d) * 2 + (core ^ e)
            qd[pl.ds(pl.multiple_of(owner * slot, 8), slot), :] = pieces[e][d]
    n_row = ni * HP
    gw_o[...] = jnp.zeros_like(gw_o)
    rows = dot_full(row_order(ni, ka, oq, slot), qd[...])
    width = w_query_t.shape[1]
    q_raw, d_up = rows[:ni, :width], rows[ni:, :width]
    nat[...] = jnp.zeros_like(nat)
    nat[0:ni, 0:128] = rows[:ni, width : width + 128]
    nat[ni : 2 * ni, 0:128] = rows[:ni, width : width + 128]
    frt_o[...] = jnp.transpose(nat[:, 0:128])
    fr = frt_o[...]
    nat[...] = jnp.zeros_like(nat)
    nat[0:ni, 0 : HC + QP] = rows3(q_raw, w_query_t[...], 1, 1)
    transpose_tiles(qt_o, nat, QW // 128)
    rp = H * PQ
    world = to_world(fr, three(qt_o[HC : HC + QP, :], rp), rp)
    for x in range(3):
        qt_o[HC + x * rp : HC + (x + 1) * rp, :] = world[x]
    for t in range(QW // 128):
        nat[:, t * 128 : (t + 1) * 128] = jnp.transpose(qt_o[t * 128 : (t + 1) * 128, :])
    q_o[...] = nat[0:ni, :]
    gw_o[n_row : n_row + H, :] = w_bias_t[...].astype(F32)
    wb_t = gw_o[n_row : n_row + HP, :].astype(BF16)
    coef = coefficient(head_weight)
    gw_o[n_row + HP :, :] = jnp.broadcast_to(coef, (HP, gw_o.shape[1]))
    chain = column(chain_bias[...], H)
    mq = head_mask(QW, Q_LANES)
    is_pt = lax.broadcasted_iota(jnp.int32, (HP, QW), 1) >= HC
    q_rows = per_head(nat[0:ni, :], ni)
    left = q_rows * tiled(mq * jnp.where(is_pt, 2.0 * coef, WL / math.sqrt(HEAD)), ni)
    l1_o[...], l2_o[...], l3_o[...] = split3(left)
    q_sq = 0.5 * jnp.sum(
        left * jnp.where(lax.broadcasted_iota(jnp.int32, left.shape, 1) >= HC, q_rows, 0.0),
        axis=1, keepdims=True,
    )
    split = jnp.concatenate(split3(d_up), axis=0)

    def d_out(lo, hi):
        out = dot(split, w_out[lo:hi, :], 1, 1)
        return out[0:ni] + out[ni : 2 * ni] + out[2 * ni : 3 * ni]

    du_o[...] = d_up
    dv_o[...] = jnp.zeros_like(dv_o)
    dv_o[0:ni, 0:HC] = d_out(0, HC)
    dmh_o[...], dml_o[...] = split2(
        per_head(dv_o[0:ni, :], ni) * tiled(head_mask(256, V_LANES), ni)
    )
    cp = pair.shape[2]
    d_pairs = d_out(HC, HC + H * cp)
    for h in range(H):
        gw_o[pl.ds(h, ni, stride=HP), :] = d_pairs[:, h * cp : (h + 1) * cp]
    for i in range(ni):
        gh, gl = split2(gw_o[i * HP : (i + 1) * HP, :])
        out = dot(jnp.concatenate([wb_t, gh, gl], axis=0), pair[i], 1, 1)
        sl = slice(i * HP, (i + 1) * HP)
        cross = jnp.where(k_chain[...] != q_chain[i], chain, 0.0)
        base_o[sl, :] = WL * out[0:HP] - q_sq[sl] + cross
        dap_o[sl, :] = out[HP : 2 * HP] + out[2 * HP : 3 * HP]


def key_kernel(ni, nk, n_pieces, *refs):
    pieces = refs[:2]
    (w_key_t, base, l1, l2, l3, dmh, dml, dap, gw, k_mask,
     w_o, da_o, pay_o, kq_o, vt_o, kraw, kt) = refs[2:]
    core = lax.rem(lax.axis_index("ka"), 2)
    width = w_key_t.shape[1]
    tiles = width // 128
    fr = None
    for k in range(n_pieces // 2):
        for e in range(2):
            start = pl.multiple_of((2 * k + (core ^ e)) * nk, 8)
            for t in range(tiles):
                kraw[pl.ds(start, nk), t * 128 : (t + 1) * 128] = pieces[e][
                    k, t * nk : (t + 1) * nk, :
                ]
            part = pieces[e][k, tiles * nk : tiles * nk + 16, :]
            fr = part if fr is None else fr + part
    nj = kraw.shape[0]
    wide = dot(w_key_t[...], jnp.concatenate(split3(kraw[...]), axis=0), 1, 1)
    kt[...] = wide[:, 0:nj] + (wide[:, nj : 2 * nj] + wide[:, 2 * nj :])
    rk, rv = H * PQ, H * PV
    kp = to_world(fr, three(kt[2 * HC : 2 * HC + QP, :], rk), rk)
    vp = to_world(fr, three(kt[2 * HC + QP : 2 * HC + QP + VP, :], rv), rv)
    kq_o[0:HC, :] = kt[0:HC, :]
    vt_o[0:HC, :] = kt[HC : 2 * HC, :]
    for x in range(3):
        kq_o[HC + x * rk : HC + (x + 1) * rk, :] = kp[x]
        vt_o[HC + x * rv : HC + (x + 1) * rv, :] = vp[x]
    kq_o[HC + QP : HC + QP + 16, :] = fr
    kq_o[HC + QP + 16 :, :] = jnp.zeros_like(kq_o[HC + QP + 16 :, :])
    vt_o[HC + VP :, :] = jnp.zeros_like(vt_o[HC + VP :, :])
    mq = head_mask(QW, Q_LANES)
    coef = gw[ni * HP + HP :, 0:1]
    kpt = kq_o[HC : HC + QP, :]
    k_sq = dot_full(mq[:, HC : HC + QP] * coef, kpt * kpt)
    k1, k2, k3 = split3(kq_o[...])
    by1 = dot(l1[...], jnp.concatenate([k1, k2, k3], axis=1))
    by2 = dot(l2[...], jnp.concatenate([k1, k2], axis=1))
    logits = by2[:, nj:] + (by1[:, 2 * nj :] + dot(l3[...], k1))
    logits = logits + (by1[:, nj : 2 * nj] + by2[:, 0:nj])
    logits = logits + by1[:, 0:nj]
    logits = logits + base[...] - tiled(k_sq, ni)
    logits = jnp.where(k_mask[...] == 1, logits, MASKED)
    top = jnp.max(logits, axis=1, keepdims=True)
    weights = jnp.exp(logits - top)
    w_o[...] = weights
    total = jnp.sum(weights, axis=1, keepdims=True)
    vh, vl = split2(vt_o[...])
    da = dap[...] + cross3(dmh[...], dml[...], vh[0:256], vl[0:256])
    da_o[...] = da
    s_sum = jnp.sum(weights * da, axis=1, keepdims=True)
    wh, wl = split2(weights)
    ph, po = vh[HC : HC + PW], vl[HC : HC + PW]
    num = lanes3(wh, wl, ph, po)
    num = num * tiled(head_mask(PW, P_LANES), ni)
    for k, value in enumerate((top, total, s_sum)):
        num = num + value * tiled(stat_mask(PW, VP + k * HP), ni)
    pay_o[...] = head_sum(num, ni)


def combine_kernel(*refs):
    parts, out = refs[:-1], refs[-1]
    n = parts[0].shape[0]
    tops = dot_full(jnp.concatenate([x[:, 256:384] for x in parts], axis=0), spread_mask(0))
    tops = [tops[k * n : (k + 1) * n] for k in range(len(parts))]
    top = functools.reduce(jnp.maximum, tops)
    lane = lax.broadcasted_iota(jnp.int32, top.shape, 1)
    mixed = None
    for x, t in zip(parts, tops):
        term = x[...] * jnp.exp(t - top)
        mixed = term if mixed is None else mixed + term
    out[...] = jnp.where((lane >= VP) & (lane < VP + HP), top, mixed)


def value_kernel(ni, w, pair, vt, w_out, u_o, npx, nv0, nv1):
    cp = pair.shape[2]
    for i in range(ni):
        wh, wl = split2(w[i * HP : (i + 1) * HP, :])
        out = dot(jnp.concatenate([wh, wl], axis=0), pair[i], 1, 0)
        npx[i * HP : (i + 1) * HP, :] = out[0:HP] + out[HP : 2 * HP]
    nv = lanes3(*split2(w[...]), *split2(vt[0:256, :])) * tiled(head_mask(256, V_LANES), ni)
    nv0[...] = nv[:, 0:128]
    nv1[...] = nv[:, 128:256]
    for h in range(H):
        t = h * HEAD // 128
        wv = w_out[t * 128 : min(t * 128 + 128, HC), :]
        part = (nv0, nv1)[t][pl.ds(h, ni, stride=HP), :]
        u_o[h] = rows2(
            npx[pl.ds(h, ni, stride=HP), :], w_out[HC + h * cp : HC + (h + 1) * cp, :]
        ) + rows2(part[:, 0 : wv.shape[0]], wv)


def spread_kernel(ni, qt, dv, du, gw, w_out, lh_o, ll_o, dh_o, dlo_o, dlt_o, nat, dvt):
    e = expand_mask(ni)
    rq = H * PQ
    head = lax.broadcasted_iota(jnp.int32, (rq, HP), 0) >> 2
    pick = (head == lax.broadcasted_iota(jnp.int32, (rq, HP), 1)).astype(F32)
    twice = 2.0 * dot_full(pick, gw[ni * HP + HP :, :])[:, 0:1]
    qs = qt[0:HC, 0:ni] * (WL / math.sqrt(HEAD))
    qp = qt[HC : HC + QP, 0:ni] * jnp.concatenate([twice] * 3, axis=0)
    lh_o[...], ll_o[...] = expand_rows(jnp.concatenate([qs, qp], axis=0), Q_BLOCKS, e)
    transpose_tiles(dvt, dv, 2)
    dh_o[...], dlo_o[...] = expand_rows(dvt[0:HC, 0:ni], V_BLOCKS, e)
    nat[...] = jnp.zeros_like(nat)
    nat[0:ni, :] = rows3(du[...], w_out[w_out.shape[0] - PW :, :], 1, 1)
    transpose_tiles(dlt_o, nat, 3)


def cross3(ah, al, bh, bl):
    n = bh.shape[1]
    out = dot(ah, jnp.concatenate([bh, bl], axis=1))
    return out[:, 0:n] + (out[:, n:] + dot(al, bh))


def lanes3(ah, al, bh, bl):
    return dot(
        jnp.concatenate([ah, ah, al], axis=1), jnp.concatenate([bh, bl, bh], axis=1), 1, 1
    )


def grad_kernel(
    ni, oq, ka, pay, pay_loc, w, da, dap, q_feat, dlt, frt, kq, vt, u, gw, w_out,
    att_o, dl_o, mine_o, theirs_o, dpt_o, nat, tr,
):
    me = lax.axis_index("ka")
    fr = frt[...]
    width = u.shape[2]
    mp, mq = head_mask(PW, P_LANES), head_mask(QW, Q_LANES)
    tops = dot_full(
        jnp.concatenate([pay[:, 256:384], pay_loc[:, 256:384]], axis=0), spread_mask(0)
    )
    grow = jnp.exp(tops[ni : 2 * ni] - tops[0:ni])
    totals = dot_full(pay[:, 256:384], spread_mask(HP))
    inv = jnp.where(totals > 0.0, 1.0 / totals, 0.0)
    inv_col = to_column(inv[:, 256:384], ni, VP - 256)
    weights = w[...] * to_column(grow[:, 256:384], ni, VP - 256)
    att = weights * inv_col
    att_o[...] = att
    lost = jnp.sum(
        (weights - weights.astype(BF16).astype(F32)) * dap[...], axis=1, keepdims=True
    )
    nat[...] = jnp.zeros_like(nat)
    nat[0:ni, 0:128] = head_sum(lost * inv_col * tiled(stat_mask(128, 0), ni), ni)
    eps_t = jnp.transpose(nat[:, 0:128])[0:HP, :]
    scaled = pay[...] * inv
    nat[0:ni, :] = scaled
    transpose_tiles(tr, nat, 3)
    rv = H * PV
    out_pt = three(tr[0:VP, :], rv)
    shifted = [out_pt[x] - frame_row(fr, 9 + x) for x in range(3)]
    loc = to_local(fr, shifted)
    length = jnp.sqrt(loc[0] * loc[0] + loc[1] * loc[1] + loc[2] * loc[2] + 1e-08)
    ratio = dlt[VP : VP + rv, :] / length
    d_loc = [dlt[y * rv : (y + 1) * rv, :] + ratio * loc[y] for y in range(3)]
    d_pt = []
    for x in range(3):
        acc = frame_row(fr, 3 * x) * d_loc[0]
        for y in range(1, 3):
            acc = acc + frame_row(fr, 3 * x + y) * d_loc[y]
        d_pt.append(acc)
    for y in range(3):
        tr[y * rv : (y + 1) * rv, :] = loc[y]
    tr[VP : VP + rv, :] = length
    for t in range(3):
        nat[:, t * 128 : (t + 1) * 128] = jnp.transpose(tr[t * 128 : (t + 1) * 128, :])
    own = rows2(nat[0:ni, :], w_out[w_out.shape[0] - PW :, :])
    row = lax.broadcasted_iota(jnp.int32, (ni, 1), 0)
    upd = jnp.where((row >= me * oq) & (row < (me + 1) * oq), own, 0.0)
    share = inv * grow
    for h in range(H):
        upd = upd + u[h] * share[:, VP + h : VP + h + 1]
    for x in range(3):
        tr[x * rv : (x + 1) * rv, :] = d_pt[x]
    tr[VP:, :] = jnp.zeros_like(tr[VP:, :])
    dpt_o[...] = tr[0:VP, :]
    for t in range(3):
        nat[:, t * 128 : (t + 1) * 128] = jnp.transpose(tr[t * 128 : (t + 1) * 128, :])
    d_nat = nat[0:ni, :]
    lane = lax.broadcasted_iota(jnp.int32, (ni, PW), 1)
    dots = jnp.where(lane < VP, d_nat * scaled, scaled)
    delta = jnp.sum(
        per_head(dots, ni) * tiled(mp + stat_mask(PW, VP + 2 * HP), ni), axis=1, keepdims=True
    )
    dptm = per_head(d_nat, ni) * tiled(mp, ni)
    d_att = da[...] + cross3(*split2(dptm), *split2(vt[HC : HC + PW, :]))
    dl = att * (d_att - delta)
    dl_o[...] = dl
    coef = gw[ni * HP + HP :, 0:1]
    lane_h = lax.broadcasted_iota(jnp.int32, (HP, QW), 1)
    scale = tiled(mq * jnp.where(lane_h >= HC, 2.0 * coef, WL / math.sqrt(HEAD)), ni)
    kh, kl = split2(kq[...])
    points = per_head(jnp.where(lane >= HC, q_feat[...], 0.0), ni)
    dlh, dll = split2(dl)
    ath, atl = split2(att)
    for k, (full, high, low) in enumerate(((dl, dlh, dll), (att, ath, atl))):
        gq = lanes3(high, low, kh, kl)
        gq = gq - points * jnp.sum(full, axis=1, keepdims=True)
        nat[k * ni : (k + 1) * ni, :] = head_sum(gq * scale, ni)
    nat[2 * ni :, :] = jnp.zeros_like(nat[2 * ni :, :])
    transpose_tiles(tr, nat, 3)
    rq = H * PQ
    gl = to_local(fr, three(tr[HC : HC + QP, :], rq))
    for x in range(3):
        tr[HC + x * rq : HC + (x + 1) * rq, :] = gl[x]
    for t in range(3):
        nat[:, t * 128 : (t + 1) * 128] = jnp.transpose(tr[t * 128 : (t + 1) * 128, :])
    half = ni // 2
    r32, c32 = grid((ni, ni))
    rest = r32 & (half - 1)
    shift = oq.bit_length() - 1
    source = (
        (((me // 2) ^ (rest >> shift)) * 2 + (lax.rem(me, 2) ^ jnp.where(r32 >= half, 1, 0))) * oq
        + (rest & (oq - 1))
    )
    order = (c32 == source).astype(BF16)
    block = jnp.concatenate([upd, nat[0:ni, :], nat[ni : 2 * ni, :]], axis=1)
    moved = dot(jnp.concatenate([order] * 3, axis=1), jnp.concatenate(split3(block), axis=0))
    mine_o[:, 0 : 3 * width] = moved[0:half]
    theirs_o[:, 0 : 3 * width] = moved[half:]
    mine_o[:, 3 * width :] = jnp.zeros_like(mine_o[:, 3 * width :])
    mine_o[0:HP, 3 * width :] = eps_t
    theirs_o[:, 3 * width :] = jnp.zeros_like(theirs_o[:, 3 * width :])
    theirs_o[0:HP, 3 * width :] = eps_t


def keyv_kernel(ni, att, dvh, dvl, dpt, kq, w_key_t, keyv_o, knat, kt):
    ath, atl = split2(att[...])
    rv = H * PV
    kt[0:HC, :] = cross3(dvh[...], dvl[...], ath, atl)
    ph, plo = expand_rows(dpt[:, 0:ni], P_BLOCKS, expand_mask(ni))
    gvl = to_local(kq[HC + QP : HC + QP + 16, :], three(cross3(ph, plo, ath, atl), rv))
    for x in range(3):
        kt[256 + x * rv : 256 + (x + 1) * rv, :] = gvl[x]
    for t in range(5):
        knat[:, t * 128 : (t + 1) * 128] = jnp.transpose(kt[t * 128 : (t + 1) * 128, :])
    keyv_o[...] = rows2(knat[:, 0:HC], w_key_t[HC : 2 * HC, :]) + rows2(
        knat[:, 256 : 256 + VP], w_key_t[2 * HC + QP :, :]
    )


def mid_kernel(ni, oq, chips, width, mine, other, *outs):
    total = mine[...] + other[...]
    per = min(128 // ni, HP // oq)
    packed = []
    for g in range(HP // oq // per):
        acc = None
        for k in range(per):
            at = (g * per + k) * oq
            part = total[at : at + oq, 3 * width :]
            part = part if k == 0 else pltpu.roll(part, k * ni, 1)
            acc = part if acc is None else acc + part
        packed.append(acc)
    packed = jnp.concatenate(packed, axis=1)
    for d in range(chips):
        outs[d][:, 0 : 3 * width] = total[d * oq : (d + 1) * oq, 0 : 3 * width]
        outs[d][:, 3 * width :] = packed


def correction(ni, oq, width, slices, eps):
    eps[...] = jnp.zeros_like(eps)
    per = min(128 // ni, HP // oq)
    for g in range(HP // oq // per):
        at = 3 * width + g * 128
        acc = slices[0][:, at : at + 128]
        for piece in slices[1:]:
            acc = acc + piece[:, at : at + 128]
        for k in range(per):
            row = (g * per + k) * oq
            eps[row : row + oq, :] = acc if k == 0 else pltpu.roll(acc, 128 - k * ni, 1)


def keyfix_kernel(ni, oq, width, chips, pbc, *refs):
    slices = refs[:chips]
    att, dl0, lh, ll, kq, gw, keyv, w_key_t = refs[chips : chips + 8]
    dl_o, outs = refs[chips + 8], refs[chips + 9 : chips + 9 + pbc]
    eps, kt, knat, total = refs[chips + 9 + pbc :]
    correction(ni, oq, width, slices, eps)
    per_query = jnp.transpose(eps[...])[0:ni, :]
    dl = dl0[...] + att[...] * to_column(per_query, ni, 0)
    dl_o[...] = dl
    dlh, dll = split2(dl)
    gk = cross3(lh[...], ll[...], dlh, dll)
    kt[0:HC, :] = gk[0:HC]
    coef = gw[ni * HP + HP :, 0:1]
    col_sum = jnp.sum(dl.reshape(ni, HP, dl.shape[1]), axis=0)
    col = dot_full(head_mask(QW, Q_LANES)[:, HC : HC + QP] * (2.0 * coef), col_sum, 0, 0)
    rq = H * PQ
    gkp = gk[HC : HC + QP] - col * kq[HC : HC + QP, :]
    gkl = to_local(kq[HC + QP : HC + QP + 16, :], three(gkp, rq))
    for x in range(3):
        kt[256 + x * rq : 256 + (x + 1) * rq, :] = gkl[x]
    for t in range(4):
        knat[:, t * 128 : (t + 1) * 128] = jnp.transpose(kt[t * 128 : (t + 1) * 128, :])
    total[...] = keyv[...] + (
        rows2(knat[:, 0:HC], w_key_t[0:HC, :])
        + rows2(knat[:, 256 : 256 + QP], w_key_t[2 * HC : 2 * HC + QP, :])
    )
    block = total.shape[0] // pbc
    for d in range(pbc):
        start = pl.multiple_of((lax.axis_index("pb") ^ d) * block, 8)
        outs[d][...] = total[pl.ds(start, block), :]


def ownfix_kernel(ni, oq, width, chips, *refs):
    slices, w_query_t = refs[:chips], refs[chips]
    upd_o, dq_o, eps, rows = refs[chips + 1 :]
    correction(ni, oq, width, slices, eps)
    acc = slices[0][:, 0 : 3 * width]
    for piece in slices[1:]:
        acc = acc + piece[:, 0 : 3 * width]
    upd_o[...] = acc[:, 0:width].astype(BF16)
    rows[...] = jnp.zeros_like(rows)
    rows[0:oq, :] = acc[:, width:]
    r, lane = grid((8, 128))
    pick = (lane == lax.axis_index("ka") * oq + r).astype(F32)
    mine = dot_full(pick, eps[0:HP, :], 1, 1)
    full = dot_full(mine, head_mask(QW, Q_LANES))
    local_grad = rows[:, 0:QW] + full * rows[:, width : width + QW]
    dq = rows2(local_grad[:, 0 : HC + QP], w_query_t[...])
    dq_o[...] = dq[0:oq].astype(BF16)


def pair_kernel(ni, att, dl, gw, out):
    n_row = ni * HP
    wb_t = gw[n_row : n_row + HP, :].astype(BF16)
    for i in range(ni):
        sl = slice(i * HP, (i + 1) * HP)
        ah, al = split2(att[sl, :])
        dh, dlo = split2(dl[sl, :] * WL)
        gh, gl = split2(gw[sl, :])
        left = jnp.concatenate([ah, al, ah, dh, dlo], axis=0)
        right = jnp.concatenate([gh, gh, gl, wb_t, wb_t], axis=0)
        out[i] = dot(left, right, 0, 0).astype(BF16)


class Kept:
    def __init__(self, value):
        self.value = value


def call(kernel, outs, args, far=(), cut=None, kept=(), smem=0, scratch=(), name=None, limit=24):
    n_in, n_out = len(args), len(outs)
    held = [k for k, x in enumerate(args) if isinstance(x, Kept)]
    args = [x.value if isinstance(x, Kept) else x for x in args]
    far, far_out, after = list(far), [], []
    cut = cut or {}

    def body(*refs):
        ins, rest = list(refs[:n_in]), list(refs[n_in:])
        results, rest = rest[:n_out], rest[n_out:]
        own, rest = rest[: len(scratch)], rest[len(scratch) :]
        bufs, rest = rest[: len(far)], rest[len(far) :]
        out_bufs, sems = rest[: len(far_out)], rest[len(far_out) :]
        for k, (at, buf) in enumerate(zip(far, bufs)):
            src = ins[at]
            if at in cut:
                src = src.at[pl.ds(args[at].shape[0] - cut[at], cut[at]), :]
            ins[at] = Fetched(src, buf, sems[0].at[k])
        targets = list(results)
        for at, buf in zip(far_out, out_bufs):
            targets[at] = buf
        kernel(*ins, *targets, *own)
        copies = [
            pltpu.make_async_copy(buf, results[at], sems[0].at[len(far) + k])
            for k, (at, buf) in enumerate(zip(far_out, out_bufs))
        ]
        for copy in copies:
            copy.start()
        for at in far:
            ins[at].get()
        for copy in copies:
            copy.wait()

    specs = []
    for k in range(n_in):
        space = pltpu.SMEM if k < smem else pltpu.HBM if k in far or k in after else pltpu.VMEM
        specs.append(pl.BlockSpec(memory_space=space))
    results = pl.pallas_call(
        body,
        out_shape=[
            pltpu.VMEM(s, d) if k in kept else jax.ShapeDtypeStruct(s, d)
            for k, (s, d) in enumerate(outs)
        ],
        in_specs=specs,
        out_specs=[
            pl.BlockSpec(memory_space=pltpu.HBM if k in far_out else pltpu.VMEM)
            for k in range(n_out)
        ],
        scratch_shapes=[pltpu.VMEM(s, d) for s, d in scratch]
        + [pltpu.VMEM((cut.get(k, args[k].shape[0]),) + args[k].shape[1:], args[k].dtype)
           for k in far]
        + [pltpu.VMEM(*outs[k]) for k in far_out]
        + ([pltpu.SemaphoreType.DMA((len(far) + len(far_out),))] if far or far_out else []),
        compiler_params=pltpu.CompilerParams(vmem_limit_bytes=limit * 1024 * 1024),
        name=name,
    )(*[
        pltpu.with_memory_space_constraint(x, pltpu.HBM) if k in far
        else pltpu.with_memory_space_constraint(x, pltpu.VMEM) if k in held else x
        for k, x in enumerate(args)
    ])
    return [Kept(x) if k in kept else x for k, x in enumerate(results)]


def load(params, after):
    n = len(params)
    results = pl.pallas_call(
        functools.partial(load_kernel, n),
        out_shape=[pltpu.VMEM(x.shape, x.dtype) for x in params],
        in_specs=[pl.BlockSpec(memory_space=pltpu.VMEM)]
        + [pl.BlockSpec(memory_space=pltpu.HBM)] * n,
        out_specs=[pl.BlockSpec(memory_space=pltpu.VMEM)] * n,
        scratch_shapes=[pltpu.SemaphoreType.DMA((n,))],
        compiler_params=pltpu.CompilerParams(vmem_limit_bytes=2 * 1024 * 1024),
        name="load",
    )(after, *[pltpu.with_memory_space_constraint(x, pltpu.HBM) for x in params])
    return [Kept(x) for x in results]


def local(
    q_single, k_single, q_frames, k_frames, pair_tile, w_query, w_key, w_bias, w_out,
    head_weight, chain_bias, q_chain, k_chain, k_mask, d_update,
):
    pbc = lax.axis_size("pb")
    kac = lax.axis_size("ka")
    pb = lax.axis_index("pb")
    ka = lax.axis_index("ka")
    ni, nj, cp = pair_tile.shape
    oq, width = q_single.shape
    nk = k_single.shape[0]
    slot = -(-2 * oq // 8) * 8
    w_query_t, w_key_t, w_bias_t = (jnp.transpose(x) for x in (w_query, w_key, w_bias))

    def ka_xor(x, d):
        return lax.ppermute(x, "ka", [(i, i ^ d) for i in range(kac)])

    def pb_xor(x, d):
        return lax.ppermute(x, "pb", [(i, i ^ d) for i in range(pbc)])

    n_row = ni * HP
    f32 = lambda *s: (s, F32)
    bf16 = lambda *s: (s, BF16)
    k_rows = width // 128 * nk + 16
    pk, pq = call(
        functools.partial(pack_kernel, pbc),
        [f32(k_rows, 128), f32(slot, width + 128)],
        [k_single, k_frames, q_single, jnp.transpose(q_frames), d_update],
        far=range(5),
        name="pack",
    )
    params = [pair_tile, w_out, w_query_t, w_key_t]
    pair_v, w_out_v, w_query_v, w_key_v = load(params, pk)
    own_pieces = [pq] + [ka_xor(pq, 2 * d) for d in range(1, kac // 2)]
    (query_own,) = call(
        stack_kernel,
        [f32(kac // 2, slot, width + 128)],
        [w_query_v] + own_pieces,
        name="stack",
    )
    query_other = ka_xor(query_own, 1)
    devices = [(p, a) for p in range(pbc) for a in range(kac)]
    moved = lax.ppermute(
        pk, ("pb", "ka"),
        [(p * kac + a, (p ^ (a // 2)) * kac + 2 * p + a % 2) for p, a in devices],
    )
    crossed = [pb_xor(moved, d) for d in reversed(range(1, pbc))]
    base, dap, gw, q_feat, qt, l1, l2, l3, dmh, dml, dv, du, frt = call(
        functools.partial(query_kernel, ni, kac, oq, slot),
        [f32(n_row, nj), f32(n_row, nj), f32(n_row + 2 * HP, cp), f32(ni, QW), f32(QW, 128),
         bf16(n_row, QW), bf16(n_row, QW), bf16(n_row, QW), bf16(n_row, 256), bf16(n_row, 256),
         f32(128, 256), f32(ni, width), f32(128, 128)],
        [q_chain, query_own, query_other, pair_v, w_query_v, w_out_v, w_bias_t,
         head_weight[None, :], chain_bias[None, :], k_chain[None, :]],
        far=range(6, 10),
        kept=range(13),
        smem=1,
        scratch=[f32(kac * slot, width + 128), f32(128, QW)],
        name="query",
    )
    keep, give = call(
        functools.partial(sort_kernel, pbc),
        [f32(pbc // 2, k_rows, 128)] * 2,
        [q_feat, moved, *crossed],
        scratch=[f32(pbc, k_rows, 128)],
        name="sort",
    )
    key_pieces = [keep, ka_xor(give, 1)]
    weights, da, pay, kq, vt = call(
        functools.partial(key_kernel, ni, nk, pbc),
        [f32(n_row, nj), f32(n_row, nj), f32(ni, PW), f32(QW, nj), f32(HC + PW, nj)],
        [*key_pieces, w_key_v, base, l1, l2, l3, dmh, dml, dap, gw, k_mask[None, :]],
        far=[11],
        kept=[0, 1, 3, 4],
        scratch=[f32(nj, width), f32(w_key_t.shape[0], nj)],
        name="key",
    )
    lh, ll, dvh, dvl, dlt = call(
        functools.partial(spread_kernel, ni),
        [bf16(HC + QP, n_row), bf16(HC + QP, n_row), bf16(HC, n_row), bf16(HC, n_row),
         f32(PW, 128)],
        [qt, dv, du, gw, w_out_v],
        kept=range(5),
        scratch=[f32(128, PW), f32(256, 128)],
        name="spread",
    )
    (u,) = call(
        functools.partial(value_kernel, ni),
        [f32(H, ni, width)],
        [weights, pair_v, vt, w_out_v],
        kept=[0],
        scratch=[f32(n_row, cp), f32(n_row, 128), f32(n_row, 128)],
        name="value",
    )
    chips = kac // 2
    (near,) = call(combine_kernel, [f32(ni, PW)], [pay, ka_xor(pay, 1)], name="combine")
    (total,) = call(
        combine_kernel,
        [f32(ni, PW)],
        [near] + [ka_xor(near, 2 * d) for d in range(1, chips)],
        name="combine",
    )
    wide = 3 * width + 128
    att, dl0, mine, theirs, dpt = call(
        functools.partial(grad_kernel, ni, oq, kac),
        [f32(n_row, nj), f32(n_row, nj), f32(ni // 2, wide), f32(ni // 2, wide), f32(VP, 128)],
        [total, pay, weights, da, dap, q_feat, dlt, frt, kq, vt, u, gw, w_out_v],
        kept=[0, 1, 4],
        scratch=[f32(128, 384), f32(384, 128)],
        name="grad",
    )
    (keyv,) = call(
        functools.partial(keyv_kernel, ni),
        [f32(nj, width)],
        [att, dvh, dvl, dpt, kq, w_key_v],
        kept=[0],
        scratch=[f32(nj, 640), f32(640, nj)],
        name="keyv",
    )
    slices = call(
        functools.partial(mid_kernel, ni, oq, chips, width),
        [f32(oq, 3 * width + HP // oq // min(128 // ni, HP // oq) * 128)] * chips,
        [mine, ka_xor(theirs, 1)],
        name="mid",
    )
    slices = [slices[0]] + [ka_xor(slices[d], 2 * d) for d in reversed(range(1, chips))]
    fixed = call(
        functools.partial(keyfix_kernel, ni, oq, width, chips, pbc),
        [f32(n_row, nj)] + [f32(nj // pbc, width)] * pbc,
        [*slices, att, dl0, lh, ll, kq, gw, keyv, w_key_v],
        kept=[0],
        scratch=[f32(128, 128), f32(512, nj), f32(nj, 512), f32(nj, width)],
        name="keyfix",
    )
    dl, blocks = fixed[0], fixed[1:]
    update, d_query = call(
        functools.partial(ownfix_kernel, ni, oq, width, chips),
        [bf16(oq, width), bf16(oq, width)],
        [*slices, w_query_v],
        scratch=[f32(128, 128), f32(8, 2 * width)],
        name="ownfix",
    )
    (d_pair,) = call(
        functools.partial(pair_kernel, ni),
        [((ni, nj, cp), BF16)],
        [att, dl, gw],
        name="pair",
    )
    key_own = blocks[0]
    for d in reversed(range(1, pbc)):
        key_own = key_own + pb_xor(blocks[d], d)
    return update, d_pair, d_query, key_own


def solution(mesh):
    both = ("pb", "ka")
    placed = (
        P(both, None), P(both, None), P(None, both), P(None, both), P("pb", "ka", None),
        P(), P(), P(), P(), P(), P(), P("pb"), P("ka"), P("ka"), P(both, None),
    )
    return jax.shard_map(
        local,
        mesh=mesh,
        in_specs=placed,
        out_specs=(
            P(both, None), P("pb", "ka", None), P(both, None), P(("ka", "pb"), None),
        ),
        check_vma=False,
    )
```

```python
import functools
import math

import jax
import jax.numpy as jnp
from jax import lax
from jax.experimental import pallas as pl
from jax.experimental.pallas import tpu as pltpu
from jax.sharding import PartitionSpec as P

H = 12
HP = 16
HEAD = 16
PQ = 4
PV = 8
HC = H * HEAD
QP = 3 * H * PQ
VP = 3 * H * PV
QW = 384
PW = 384
MASKED = -1000000000.0
WL = math.sqrt(1.0 / 3.0)
F32 = jnp.float32
BF16 = jnp.bfloat16


def dot(a, b, ca=1, cb=0, precision=None):
    return lax.dot_general(
        a, b, (((ca,), (cb,)), ((), ())), precision=precision, preferred_element_type=F32
    )


def dot_full(a, b, ca=1, cb=0):
    return dot(a, b, ca, cb, lax.Precision.HIGHEST)


def split2(x):
    high = x.astype(BF16)
    return high, (x - high.astype(F32)).astype(BF16)


def split3(x):
    high = x.astype(BF16)
    rest = x - high.astype(F32)
    mid = rest.astype(BF16)
    return high, mid, (rest - mid.astype(F32)).astype(BF16)


def rows3(x, b, ca=1, cb=0):
    n = x.shape[0]
    out = dot(jnp.concatenate(split3(x), axis=0), b, ca, cb)
    return out[0:n] + out[n : 2 * n] + out[2 * n : 3 * n]


def rows2(x, b, ca=1, cb=0):
    n = x.shape[0]
    out = dot(jnp.concatenate(split2(x), axis=0), b, ca, cb)
    return out[0:n] + out[n : 2 * n]


def pair3(a, b, ca=1, cb=0):
    ah, al = split2(a)
    bh, bl = split2(b)
    return dot(ah, bh, ca, cb) + (dot(ah, bl, ca, cb) + dot(al, bh, ca, cb))


def per_head(x, n):
    return jnp.broadcast_to(x[:, None, :], (n, HP, x.shape[1])).reshape(n * HP, x.shape[1])


def tiled(x, n):
    return jnp.broadcast_to(x[None], (n,) + x.shape).reshape(n * HP, x.shape[1])


def head_sum(x, n):
    return jnp.sum(x.reshape(n, HP, x.shape[1]), axis=1)


def frame_row(fr, index):
    return fr[index : index + 1, :]


def to_world(fr, loc, rows):
    out = []
    for x in range(3):
        acc = frame_row(fr, 9 + x) + frame_row(fr, 3 * x) * loc[0]
        for y in range(1, 3):
            acc = acc + frame_row(fr, 3 * x + y) * loc[y]
        out.append(acc)
    return out


def to_local(fr, g):
    out = []
    for y in range(3):
        acc = frame_row(fr, y) * g[0]
        for x in range(1, 3):
            acc = acc + frame_row(fr, 3 * x + y) * g[x]
        out.append(acc)
    return out


def three(x, rows):
    return [x[k * rows : (k + 1) * rows] for k in range(3)]


def transpose_tiles(dst, src, tiles):
    for t in range(tiles):
        dst[t * 128 : (t + 1) * 128, :] = jnp.transpose(src[:, t * 128 : (t + 1) * 128])


def column(row, n):
    at = lax.broadcasted_iota(jnp.int32, (HP, n), 0) == lax.broadcasted_iota(
        jnp.int32, (HP, n), 1
    )
    return jnp.sum(jnp.where(at, jnp.broadcast_to(row, (HP, n)), 0.0), axis=1, keepdims=True)


def coefficient(head_weight):
    x = head_weight[...]
    soft = jnp.maximum(x, 0.0) + jnp.log1p(jnp.exp(-jnp.abs(x)))
    return column(WL * soft * math.sqrt(2.0 / (9.0 * PQ)) / 2.0, H)


def rows_mask(blocks, width):
    parts = []
    for rows, shift in blocks:
        head = lax.broadcasted_iota(jnp.int32, (rows, width), 0) >> shift
        parts.append(head == (lax.broadcasted_iota(jnp.int32, (rows, width), 1) & (HP - 1)))
    return parts


def expand_rows(x, blocks, expand):
    keep = rows_mask(blocks, expand.shape[1])
    out = []
    for part in split2(x):
        wide = dot(part, expand)
        pieces, start = [], 0
        for (rows, _), mask in zip(blocks, keep):
            pieces.append(jnp.where(mask, wide[start : start + rows], 0.0).astype(BF16))
            start += rows
        out.append(jnp.concatenate(pieces, axis=0))
    return out


Q_BLOCKS = ((HC, 4),) + ((H * PQ, 2),) * 3
V_BLOCKS = ((HC, 4),)
P_BLOCKS = ((H * PV, 3),) * 3


def grid(shape):
    return tuple(lax.broadcasted_iota(jnp.int32, shape, d) for d in range(2))


def lanes_of(shape, row, blocks):
    lane = lax.broadcasted_iota(jnp.int32, shape, 1)
    keep = None
    for first, count, shift in blocks:
        hit = (lane >= first) & (lane < first + count) & (((lane - first) >> shift) == row)
        keep = hit if keep is None else keep | hit
    return keep


Q_LANES = ((0, HC, 4),) + tuple((HC + x * H * PQ, H * PQ, 2) for x in range(3))
V_LANES = ((0, HC, 4),)
P_LANES = tuple((x * H * PV, H * PV, 3) for x in range(3))


def head_mask(width, blocks):
    shape = (HP, width)
    return lanes_of(shape, grid(shape)[0], blocks).astype(F32)


def stat_mask(width, first):
    row, lane = grid((HP, width))
    return (lane == row + first).astype(F32)


def spread_mask(offset):
    shape = (128, PW)
    head = grid(shape)[0] - (VP - 256) - offset
    lane = grid(shape)[1]
    keep = lanes_of(shape, head, P_LANES)
    for k in range(3):
        keep = keep | (lane == head + VP + k * HP)
    return (keep & (head >= 0) & (head < H)).astype(F32)


def to_column(x, ni, first):
    return jnp.sum(per_head(x, ni) * tiled(stat_mask(128, first), ni), axis=1, keepdims=True)


def expand_mask(ni):
    row, lane = grid((ni, ni * HP))
    return ((lane // HP) == row).astype(BF16)


def row_order(ni, ka, oq, slot):
    row, lane = grid((2 * ni, ka * slot))
    shift = oq.bit_length() - 1
    index = row & (ni - 1)
    source = (index >> shift) * slot + (index & (oq - 1))
    return (lane == source + jnp.where(row >= ni, oq, 0)).astype(F32)


class Fetched:
    def __init__(self, src, dst, sem):
        self.ref, self.pending = dst, pltpu.make_async_copy(src, dst, sem)
        self.shape = dst.shape
        self.pending.start()

    def get(self):
        if self.pending is not None:
            self.pending.wait()
            self.pending = None
        return self.ref

    def __getitem__(self, index):
        return self.get()[index]


def pack_kernel(pbc, k, kf, q, qf, du, pk, pq):
    nk, width = k.shape
    oq = q.shape[0]
    spot = lax.rem(lax.axis_index("ka"), pbc)
    for t in range(width // 128):
        pk[t * nk : (t + 1) * nk, :] = k[:, t * 128 : (t + 1) * 128]
    row = lax.broadcasted_iota(jnp.int32, (nk, 128), 0)
    lane = lax.broadcasted_iota(jnp.int32, (nk, 128), 1)
    pk[width // 128 * nk :, :] = jnp.zeros_like(pk[width // 128 * nk :, :])
    pk[width // 128 * nk : width // 128 * nk + 12, :] = dot_full(
        kf[...], (lane == row + spot * nk).astype(F32)
    )
    pq[...] = jnp.zeros_like(pq)
    pq[0:oq, 0:width] = q[...]
    pq[0:oq, width : width + 12] = qf[...]
    pq[oq : 2 * oq, 0:width] = du[...]


def stack_kernel(_, *refs):
    rows, out = refs[:-1], refs[-1]
    for d, row in enumerate(rows):
        out[d] = row[...]


def load_kernel(n, *refs):
    sources, targets, sems = refs[1 : 1 + n], refs[1 + n : 1 + 2 * n], refs[1 + 2 * n]
    copies = [
        pltpu.make_async_copy(x, y, sems.at[k]) for k, (x, y) in enumerate(zip(sources, targets))
    ]
    for copy in copies:
        copy.start()
    for copy in copies:
        copy.wait()


def query_kernel(ni, ka, oq, slot, q_chain, *refs):
    pieces = refs[:2]
    (pair, w_query_t, w_out, w_bias_t, head_weight, chain_bias, k_chain,
     base_o, dap_o, gw_o, q_o, qt_o, l1_o, l2_o, l3_o, dmh_o, dml_o, dv_o, du_o, frt_o,
     qd, nat) = refs[2:]
    me = lax.axis_index("ka")
    chip, core = me // 2, lax.rem(me, 2)
    for d in range(ka // 2):
        for e in range(2):
            owner = (chip ^ d) * 2 + (core ^ e)
            qd[pl.ds(pl.multiple_of(owner * slot, 8), slot), :] = pieces[e][d]
    n_row = ni * HP
    gw_o[...] = jnp.zeros_like(gw_o)
    rows = dot_full(row_order(ni, ka, oq, slot), qd[...])
    width = w_query_t.shape[1]
    q_raw, d_up = rows[:ni, :width], rows[ni:, :width]
    nat[...] = jnp.zeros_like(nat)
    nat[0:ni, 0:128] = rows[:ni, width : width + 128]
    nat[ni : 2 * ni, 0:128] = rows[:ni, width : width + 128]
    frt_o[...] = jnp.transpose(nat[:, 0:128])
    fr = frt_o[...]
    nat[...] = jnp.zeros_like(nat)
    nat[0:ni, 0 : HC + QP] = rows3(q_raw, w_query_t[...], 1, 1)
    transpose_tiles(qt_o, nat, QW // 128)
    rp = H * PQ
    world = to_world(fr, three(qt_o[HC : HC + QP, :], rp), rp)
    for x in range(3):
        qt_o[HC + x * rp : HC + (x + 1) * rp, :] = world[x]
    for t in range(QW // 128):
        nat[:, t * 128 : (t + 1) * 128] = jnp.transpose(qt_o[t * 128 : (t + 1) * 128, :])
    q_o[...] = nat[0:ni, :]
    gw_o[n_row : n_row + H, :] = w_bias_t[...].astype(F32)
    wb_t = gw_o[n_row : n_row + HP, :].astype(BF16)
    coef = coefficient(head_weight)
    gw_o[n_row + HP :, :] = jnp.broadcast_to(coef, (HP, gw_o.shape[1]))
    chain = column(chain_bias[...], H)
    mq = head_mask(QW, Q_LANES)
    is_pt = lax.broadcasted_iota(jnp.int32, (HP, QW), 1) >= HC
    q_rows = per_head(nat[0:ni, :], ni)
    left = q_rows * tiled(mq * jnp.where(is_pt, 2.0 * coef, WL / math.sqrt(HEAD)), ni)
    l1_o[...], l2_o[...], l3_o[...] = split3(left)
    q_sq = 0.5 * jnp.sum(
        left * jnp.where(lax.broadcasted_iota(jnp.int32, left.shape, 1) >= HC, q_rows, 0.0),
        axis=1, keepdims=True,
    )
    split = jnp.concatenate(split3(d_up), axis=0)

    def d_out(lo, hi):
        out = dot(split, w_out[lo:hi, :], 1, 1)
        return out[0:ni] + out[ni : 2 * ni] + out[2 * ni : 3 * ni]

    du_o[...] = d_up
    dv_o[...] = jnp.zeros_like(dv_o)
    dv_o[0:ni, 0:HC] = d_out(0, HC)
    dmh_o[...], dml_o[...] = split2(
        per_head(dv_o[0:ni, :], ni) * tiled(head_mask(256, V_LANES), ni)
    )
    cp = pair.shape[2]
    d_pairs = d_out(HC, HC + H * cp)
    for h in range(H):
        gw_o[pl.ds(h, ni, stride=HP), :] = d_pairs[:, h * cp : (h + 1) * cp]
    for i in range(ni):
        gh, gl = split2(gw_o[i * HP : (i + 1) * HP, :])
        out = dot(jnp.concatenate([wb_t, gh, gl], axis=0), pair[i], 1, 1)
        sl = slice(i * HP, (i + 1) * HP)
        cross = jnp.where(k_chain[...] != q_chain[i], chain, 0.0)
        base_o[sl, :] = WL * out[0:HP] - q_sq[sl] + cross
        dap_o[sl, :] = out[HP : 2 * HP] + out[2 * HP : 3 * HP]


def key_kernel(ni, nk, n_pieces, *refs):
    pieces = refs[:n_pieces]
    (w_key_t, base, l1, l2, l3, dmh, dml, dap, gw, k_mask,
     w_o, da_o, pay_o, kq_o, vt_o, kraw, kt) = refs[n_pieces:]
    here = lax.axis_index("pb") ^ (lax.axis_index("ka") // 2)
    width = w_key_t.shape[1]
    tiles = width // 128
    fr = None
    for d in range(n_pieces):
        piece = pieces[d]
        start = pl.multiple_of((here ^ d) * nk, 8)
        for t in range(tiles):
            kraw[pl.ds(start, nk), t * 128 : (t + 1) * 128] = piece[t * nk : (t + 1) * nk, :]
        part = piece[tiles * nk : tiles * nk + 16, :]
        fr = part if fr is None else fr + part
    nj = kraw.shape[0]
    wide = dot(w_key_t[...], jnp.concatenate(split3(kraw[...]), axis=0), 1, 1)
    kt[...] = wide[:, 0:nj] + (wide[:, nj : 2 * nj] + wide[:, 2 * nj :])
    rk, rv = H * PQ, H * PV
    kp = to_world(fr, three(kt[2 * HC : 2 * HC + QP, :], rk), rk)
    vp = to_world(fr, three(kt[2 * HC + QP : 2 * HC + QP + VP, :], rv), rv)
    kq_o[0:HC, :] = kt[0:HC, :]
    vt_o[0:HC, :] = kt[HC : 2 * HC, :]
    for x in range(3):
        kq_o[HC + x * rk : HC + (x + 1) * rk, :] = kp[x]
        vt_o[HC + x * rv : HC + (x + 1) * rv, :] = vp[x]
    kq_o[HC + QP : HC + QP + 16, :] = fr
    kq_o[HC + QP + 16 :, :] = jnp.zeros_like(kq_o[HC + QP + 16 :, :])
    vt_o[HC + VP :, :] = jnp.zeros_like(vt_o[HC + VP :, :])
    mq = head_mask(QW, Q_LANES)
    coef = gw[ni * HP + HP :, 0:1]
    kpt = kq_o[HC : HC + QP, :]
    k_sq = dot_full(mq[:, HC : HC + QP] * coef, kpt * kpt)
    k1, k2, k3 = split3(kq_o[...])
    by1 = dot(l1[...], jnp.concatenate([k1, k2, k3], axis=1))
    by2 = dot(l2[...], jnp.concatenate([k1, k2], axis=1))
    logits = by2[:, nj:] + (by1[:, 2 * nj :] + dot(l3[...], k1))
    logits = logits + (by1[:, nj : 2 * nj] + by2[:, 0:nj])
    logits = logits + by1[:, 0:nj]
    logits = logits + base[...] - tiled(k_sq, ni)
    logits = jnp.where(k_mask[...] == 1, logits, MASKED)
    top = jnp.max(logits, axis=1, keepdims=True)
    weights = jnp.exp(logits - top)
    w_o[...] = weights
    total = jnp.sum(weights, axis=1, keepdims=True)
    vh, vl = split2(vt_o[...])
    da = dap[...] + cross3(dmh[...], dml[...], vh[0:256], vl[0:256])
    da_o[...] = da
    s_sum = jnp.sum(weights * da, axis=1, keepdims=True)
    wh, wl = split2(weights)
    ph, po = vh[HC : HC + PW], vl[HC : HC + PW]
    num = lanes3(wh, wl, ph, po)
    num = num * tiled(head_mask(PW, P_LANES), ni)
    for k, value in enumerate((top, total, s_sum)):
        num = num + value * tiled(stat_mask(PW, VP + k * HP), ni)
    pay_o[...] = head_sum(num, ni)


def combine_kernel(*refs):
    parts, out = refs[:-1], refs[-1]
    n = parts[0].shape[0]
    tops = dot_full(jnp.concatenate([x[:, 256:384] for x in parts], axis=0), spread_mask(0))
    tops = [tops[k * n : (k + 1) * n] for k in range(len(parts))]
    top = functools.reduce(jnp.maximum, tops)
    lane = lax.broadcasted_iota(jnp.int32, top.shape, 1)
    mixed = None
    for x, t in zip(parts, tops):
        term = x[...] * jnp.exp(t - top)
        mixed = term if mixed is None else mixed + term
    out[...] = jnp.where((lane >= VP) & (lane < VP + HP), top, mixed)


def value_kernel(ni, w, pair, vt, w_out, u_o, npx, nv0, nv1):
    cp = pair.shape[2]
    for i in range(ni):
        wh, wl = split2(w[i * HP : (i + 1) * HP, :])
        out = dot(jnp.concatenate([wh, wl], axis=0), pair[i], 1, 0)
        npx[i * HP : (i + 1) * HP, :] = out[0:HP] + out[HP : 2 * HP]
    nv = lanes3(*split2(w[...]), *split2(vt[0:256, :])) * tiled(head_mask(256, V_LANES), ni)
    nv0[...] = nv[:, 0:128]
    nv1[...] = nv[:, 128:256]
    for h in range(H):
        t = h * HEAD // 128
        wv = w_out[t * 128 : min(t * 128 + 128, HC), :]
        part = (nv0, nv1)[t][pl.ds(h, ni, stride=HP), :]
        u_o[h] = rows2(
            npx[pl.ds(h, ni, stride=HP), :], w_out[HC + h * cp : HC + (h + 1) * cp, :]
        ) + rows2(part[:, 0 : wv.shape[0]], wv)


def spread_kernel(ni, qt, dv, du, gw, w_out, lh_o, ll_o, dh_o, dlo_o, dlt_o, nat, dvt):
    e = expand_mask(ni)
    rq = H * PQ
    head = lax.broadcasted_iota(jnp.int32, (rq, HP), 0) >> 2
    pick = (head == lax.broadcasted_iota(jnp.int32, (rq, HP), 1)).astype(F32)
    twice = 2.0 * dot_full(pick, gw[ni * HP + HP :, :])[:, 0:1]
    qs = qt[0:HC, 0:ni] * (WL / math.sqrt(HEAD))
    qp = qt[HC : HC + QP, 0:ni] * jnp.concatenate([twice] * 3, axis=0)
    lh_o[...], ll_o[...] = expand_rows(jnp.concatenate([qs, qp], axis=0), Q_BLOCKS, e)
    transpose_tiles(dvt, dv, 2)
    dh_o[...], dlo_o[...] = expand_rows(dvt[0:HC, 0:ni], V_BLOCKS, e)
    nat[...] = jnp.zeros_like(nat)
    nat[0:ni, :] = rows3(du[...], w_out[w_out.shape[0] - PW :, :], 1, 1)
    transpose_tiles(dlt_o, nat, 3)


def cross3(ah, al, bh, bl):
    n = bh.shape[1]
    out = dot(ah, jnp.concatenate([bh, bl], axis=1))
    return out[:, 0:n] + (out[:, n:] + dot(al, bh))


def lanes3(ah, al, bh, bl):
    return dot(
        jnp.concatenate([ah, ah, al], axis=1), jnp.concatenate([bh, bl, bh], axis=1), 1, 1
    )


def grad_kernel(
    ni, oq, ka, pay, pay_loc, w, da, dap, q_feat, dlt, frt, kq, vt, u, gw, w_out,
    att_o, dl_o, mine_o, theirs_o, dpt_o, nat, tr,
):
    me = lax.axis_index("ka")
    fr = frt[...]
    width = u.shape[2]
    mp, mq = head_mask(PW, P_LANES), head_mask(QW, Q_LANES)
    tops = dot_full(
        jnp.concatenate([pay[:, 256:384], pay_loc[:, 256:384]], axis=0), spread_mask(0)
    )
    grow = jnp.exp(tops[ni : 2 * ni] - tops[0:ni])
    totals = dot_full(pay[:, 256:384], spread_mask(HP))
    inv = jnp.where(totals > 0.0, 1.0 / totals, 0.0)
    inv_col = to_column(inv[:, 256:384], ni, VP - 256)
    weights = w[...] * to_column(grow[:, 256:384], ni, VP - 256)
    att = weights * inv_col
    att_o[...] = att
    lost = jnp.sum(
        (weights - weights.astype(BF16).astype(F32)) * dap[...], axis=1, keepdims=True
    )
    nat[...] = jnp.zeros_like(nat)
    nat[0:ni, 0:128] = head_sum(lost * inv_col * tiled(stat_mask(128, 0), ni), ni)
    eps_t = jnp.transpose(nat[:, 0:128])[0:HP, :]
    scaled = pay[...] * inv
    nat[0:ni, :] = scaled
    transpose_tiles(tr, nat, 3)
    rv = H * PV
    out_pt = three(tr[0:VP, :], rv)
    shifted = [out_pt[x] - frame_row(fr, 9 + x) for x in range(3)]
    loc = to_local(fr, shifted)
    length = jnp.sqrt(loc[0] * loc[0] + loc[1] * loc[1] + loc[2] * loc[2] + 1e-08)
    ratio = dlt[VP : VP + rv, :] / length
    d_loc = [dlt[y * rv : (y + 1) * rv, :] + ratio * loc[y] for y in range(3)]
    d_pt = []
    for x in range(3):
        acc = frame_row(fr, 3 * x) * d_loc[0]
        for y in range(1, 3):
            acc = acc + frame_row(fr, 3 * x + y) * d_loc[y]
        d_pt.append(acc)
    for y in range(3):
        tr[y * rv : (y + 1) * rv, :] = loc[y]
    tr[VP : VP + rv, :] = length
    for t in range(3):
        nat[:, t * 128 : (t + 1) * 128] = jnp.transpose(tr[t * 128 : (t + 1) * 128, :])
    own = rows2(nat[0:ni, :], w_out[w_out.shape[0] - PW :, :])
    row = lax.broadcasted_iota(jnp.int32, (ni, 1), 0)
    upd = jnp.where((row >= me * oq) & (row < (me + 1) * oq), own, 0.0)
    share = inv * grow
    for h in range(H):
        upd = upd + u[h] * share[:, VP + h : VP + h + 1]
    for x in range(3):
        tr[x * rv : (x + 1) * rv, :] = d_pt[x]
    tr[VP:, :] = jnp.zeros_like(tr[VP:, :])
    dpt_o[...] = tr[0:VP, :]
    for t in range(3):
        nat[:, t * 128 : (t + 1) * 128] = jnp.transpose(tr[t * 128 : (t + 1) * 128, :])
    d_nat = nat[0:ni, :]
    lane = lax.broadcasted_iota(jnp.int32, (ni, PW), 1)
    dots = jnp.where(lane < VP, d_nat * scaled, scaled)
    delta = jnp.sum(
        per_head(dots, ni) * tiled(mp + stat_mask(PW, VP + 2 * HP), ni), axis=1, keepdims=True
    )
    dptm = per_head(d_nat, ni) * tiled(mp, ni)
    d_att = da[...] + cross3(*split2(dptm), *split2(vt[HC : HC + PW, :]))
    dl = att * (d_att - delta)
    dl_o[...] = dl
    coef = gw[ni * HP + HP :, 0:1]
    lane_h = lax.broadcasted_iota(jnp.int32, (HP, QW), 1)
    scale = tiled(mq * jnp.where(lane_h >= HC, 2.0 * coef, WL / math.sqrt(HEAD)), ni)
    kh, kl = split2(kq[...])
    points = per_head(jnp.where(lane >= HC, q_feat[...], 0.0), ni)
    dlh, dll = split2(dl)
    ath, atl = split2(att)
    for k, (full, high, low) in enumerate(((dl, dlh, dll), (att, ath, atl))):
        gq = lanes3(high, low, kh, kl)
        gq = gq - points * jnp.sum(full, axis=1, keepdims=True)
        nat[k * ni : (k + 1) * ni, :] = head_sum(gq * scale, ni)
    nat[2 * ni :, :] = jnp.zeros_like(nat[2 * ni :, :])
    transpose_tiles(tr, nat, 3)
    rq = H * PQ
    gl = to_local(fr, three(tr[HC : HC + QP, :], rq))
    for x in range(3):
        tr[HC + x * rq : HC + (x + 1) * rq, :] = gl[x]
    for t in range(3):
        nat[:, t * 128 : (t + 1) * 128] = jnp.transpose(tr[t * 128 : (t + 1) * 128, :])
    half = ni // 2
    r32, c32 = grid((ni, ni))
    rest = r32 & (half - 1)
    shift = oq.bit_length() - 1
    source = (
        (((me // 2) ^ (rest >> shift)) * 2 + (lax.rem(me, 2) ^ jnp.where(r32 >= half, 1, 0))) * oq
        + (rest & (oq - 1))
    )
    order = (c32 == source).astype(BF16)
    block = jnp.concatenate([upd, nat[0:ni, :], nat[ni : 2 * ni, :]], axis=1)
    moved = dot(jnp.concatenate([order] * 3, axis=1), jnp.concatenate(split3(block), axis=0))
    mine_o[:, 0 : 3 * width] = moved[0:half]
    theirs_o[:, 0 : 3 * width] = moved[half:]
    mine_o[:, 3 * width :] = jnp.zeros_like(mine_o[:, 3 * width :])
    mine_o[0:HP, 3 * width :] = eps_t
    theirs_o[:, 3 * width :] = jnp.zeros_like(theirs_o[:, 3 * width :])
    theirs_o[0:HP, 3 * width :] = eps_t


def keyv_kernel(ni, att, dvh, dvl, dpt, kq, w_key_t, keyv_o, knat, kt):
    ath, atl = split2(att[...])
    rv = H * PV
    kt[0:HC, :] = cross3(dvh[...], dvl[...], ath, atl)
    ph, plo = expand_rows(dpt[:, 0:ni], P_BLOCKS, expand_mask(ni))
    gvl = to_local(kq[HC + QP : HC + QP + 16, :], three(cross3(ph, plo, ath, atl), rv))
    for x in range(3):
        kt[256 + x * rv : 256 + (x + 1) * rv, :] = gvl[x]
    for t in range(5):
        knat[:, t * 128 : (t + 1) * 128] = jnp.transpose(kt[t * 128 : (t + 1) * 128, :])
    keyv_o[...] = rows2(knat[:, 0:HC], w_key_t[HC : 2 * HC, :]) + rows2(
        knat[:, 256 : 256 + VP], w_key_t[2 * HC + QP :, :]
    )


def mid_kernel(ni, oq, chips, width, mine, other, *outs):
    total = mine[...] + other[...]
    per = min(128 // ni, HP // oq)
    packed = []
    for g in range(HP // oq // per):
        acc = None
        for k in range(per):
            at = (g * per + k) * oq
            part = total[at : at + oq, 3 * width :]
            part = part if k == 0 else pltpu.roll(part, k * ni, 1)
            acc = part if acc is None else acc + part
        packed.append(acc)
    packed = jnp.concatenate(packed, axis=1)
    for d in range(chips):
        outs[d][:, 0 : 3 * width] = total[d * oq : (d + 1) * oq, 0 : 3 * width]
        outs[d][:, 3 * width :] = packed


def correction(ni, oq, width, slices, eps):
    eps[...] = jnp.zeros_like(eps)
    per = min(128 // ni, HP // oq)
    for g in range(HP // oq // per):
        at = 3 * width + g * 128
        acc = slices[0][:, at : at + 128]
        for piece in slices[1:]:
            acc = acc + piece[:, at : at + 128]
        for k in range(per):
            row = (g * per + k) * oq
            eps[row : row + oq, :] = acc if k == 0 else pltpu.roll(acc, 128 - k * ni, 1)


def keyfix_kernel(ni, oq, width, chips, pbc, *refs):
    slices = refs[:chips]
    att, dl0, lh, ll, kq, gw, keyv, w_key_t = refs[chips : chips + 8]
    dl_o, outs = refs[chips + 8], refs[chips + 9 : chips + 9 + pbc]
    eps, kt, knat, total = refs[chips + 9 + pbc :]
    correction(ni, oq, width, slices, eps)
    per_query = jnp.transpose(eps[...])[0:ni, :]
    dl = dl0[...] + att[...] * to_column(per_query, ni, 0)
    dl_o[...] = dl
    dlh, dll = split2(dl)
    gk = cross3(lh[...], ll[...], dlh, dll)
    kt[0:HC, :] = gk[0:HC]
    coef = gw[ni * HP + HP :, 0:1]
    col_sum = jnp.sum(dl.reshape(ni, HP, dl.shape[1]), axis=0)
    col = dot_full(head_mask(QW, Q_LANES)[:, HC : HC + QP] * (2.0 * coef), col_sum, 0, 0)
    rq = H * PQ
    gkp = gk[HC : HC + QP] - col * kq[HC : HC + QP, :]
    gkl = to_local(kq[HC + QP : HC + QP + 16, :], three(gkp, rq))
    for x in range(3):
        kt[256 + x * rq : 256 + (x + 1) * rq, :] = gkl[x]
    for t in range(4):
        knat[:, t * 128 : (t + 1) * 128] = jnp.transpose(kt[t * 128 : (t + 1) * 128, :])
    total[...] = keyv[...] + (
        rows2(knat[:, 0:HC], w_key_t[0:HC, :])
        + rows2(knat[:, 256 : 256 + QP], w_key_t[2 * HC : 2 * HC + QP, :])
    )
    block = total.shape[0] // pbc
    for d in range(pbc):
        start = pl.multiple_of((lax.axis_index("pb") ^ d) * block, 8)
        outs[d][...] = total[pl.ds(start, block), :]


def own_rows(ni, oq, width, slices, w_query_t, upd_o, dq_o, eps, rows):
    correction(ni, oq, width, slices, eps)
    acc = slices[0][:, 0 : 3 * width]
    for piece in slices[1:]:
        acc = acc + piece[:, 0 : 3 * width]
    upd_o[...] = acc[:, 0:width].astype(BF16)
    rows[...] = jnp.zeros_like(rows)
    rows[0:oq, :] = acc[:, width:]
    r, lane = grid((8, 128))
    pick = (lane == lax.axis_index("ka") * oq + r).astype(F32)
    mine = dot_full(pick, eps[0:HP, :], 1, 1)
    full = dot_full(mine, head_mask(QW, Q_LANES))
    local_grad = rows[:, 0:QW] + full * rows[:, width : width + QW]
    dq = rows2(local_grad[:, 0 : HC + QP], w_query_t[...])
    dq_o[...] = dq[0:oq].astype(BF16)


def tail_kernel(ni, oq, width, chips, steps, *refs):
    slices, (w_query_t, att, dl, gw) = refs[:chips], refs[chips : chips + 4]
    out, upd_o, dq_o, eps, rows, held, sems = refs[chips + 4 :]
    n_row = ni * HP
    wb_t = gw[n_row : n_row + HP, :].astype(BF16)
    each = ni // steps
    copies = []
    for i in range(ni):
        sl = slice(i * HP, (i + 1) * HP)
        ah, al = split2(att[sl, :])
        dh, dlo = split2(dl[sl, :] * WL)
        gh, gl = split2(gw[sl, :])
        left = jnp.concatenate([ah, al, ah, dh, dlo], axis=0)
        right = jnp.concatenate([gh, gh, gl, wb_t, wb_t], axis=0)
        held[i] = dot(left, right, 0, 0).astype(BF16)
        if i % each == each - 1:
            part = pl.ds(i + 1 - each, each)
            copies.append(
                pltpu.make_async_copy(held.at[part], out.at[part], sems.at[i // each])
            )
            copies[-1].start()
        if i == 0:
            own_rows(ni, oq, width, slices, w_query_t, upd_o, dq_o, eps, rows)
    for copy in copies:
        copy.wait()


class Kept:
    def __init__(self, value):
        self.value = value


def call(kernel, outs, args, far=(), cut=None, kept=(), smem=0, scratch=(), name=None, limit=24):
    n_in, n_out = len(args), len(outs)
    held = [k for k, x in enumerate(args) if isinstance(x, Kept)]
    args = [x.value if isinstance(x, Kept) else x for x in args]
    far, far_out, after = list(far), [], []
    cut = cut or {}

    def body(*refs):
        ins, rest = list(refs[:n_in]), list(refs[n_in:])
        results, rest = rest[:n_out], rest[n_out:]
        own, rest = rest[: len(scratch)], rest[len(scratch) :]
        bufs, rest = rest[: len(far)], rest[len(far) :]
        out_bufs, sems = rest[: len(far_out)], rest[len(far_out) :]
        for k, (at, buf) in enumerate(zip(far, bufs)):
            src = ins[at]
            if at in cut:
                src = src.at[pl.ds(args[at].shape[0] - cut[at], cut[at]), :]
            ins[at] = Fetched(src, buf, sems[0].at[k])
        targets = list(results)
        for at, buf in zip(far_out, out_bufs):
            targets[at] = buf
        kernel(*ins, *targets, *own)
        copies = [
            pltpu.make_async_copy(buf, results[at], sems[0].at[len(far) + k])
            for k, (at, buf) in enumerate(zip(far_out, out_bufs))
        ]
        for copy in copies:
            copy.start()
        for at in far:
            ins[at].get()
        for copy in copies:
            copy.wait()

    specs = []
    for k in range(n_in):
        space = pltpu.SMEM if k < smem else pltpu.HBM if k in far or k in after else pltpu.VMEM
        specs.append(pl.BlockSpec(memory_space=space))
    results = pl.pallas_call(
        body,
        out_shape=[
            pltpu.VMEM(s, d) if k in kept else jax.ShapeDtypeStruct(s, d)
            for k, (s, d) in enumerate(outs)
        ],
        in_specs=specs,
        out_specs=[
            pl.BlockSpec(memory_space=pltpu.HBM if k in far_out else pltpu.VMEM)
            for k in range(n_out)
        ],
        scratch_shapes=[pltpu.VMEM(s, d) for s, d in scratch]
        + [pltpu.VMEM((cut.get(k, args[k].shape[0]),) + args[k].shape[1:], args[k].dtype)
           for k in far]
        + [pltpu.VMEM(*outs[k]) for k in far_out]
        + ([pltpu.SemaphoreType.DMA((len(far) + len(far_out),))] if far or far_out else []),
        compiler_params=pltpu.CompilerParams(vmem_limit_bytes=limit * 1024 * 1024),
        name=name,
    )(*[
        pltpu.with_memory_space_constraint(x, pltpu.HBM) if k in far
        else pltpu.with_memory_space_constraint(x, pltpu.VMEM) if k in held else x
        for k, x in enumerate(args)
    ])
    return [Kept(x) if k in kept else x for k, x in enumerate(results)]


def load(params, after):
    n = len(params)
    results = pl.pallas_call(
        functools.partial(load_kernel, n),
        out_shape=[pltpu.VMEM(x.shape, x.dtype) for x in params],
        in_specs=[pl.BlockSpec(memory_space=pltpu.VMEM)]
        + [pl.BlockSpec(memory_space=pltpu.HBM)] * n,
        out_specs=[pl.BlockSpec(memory_space=pltpu.VMEM)] * n,
        scratch_shapes=[pltpu.SemaphoreType.DMA((n,))],
        compiler_params=pltpu.CompilerParams(vmem_limit_bytes=2 * 1024 * 1024),
        name="load",
    )(after, *[pltpu.with_memory_space_constraint(x, pltpu.HBM) for x in params])
    return [Kept(x) for x in results]


def local(
    q_single, k_single, q_frames, k_frames, pair_tile, w_query, w_key, w_bias, w_out,
    head_weight, chain_bias, q_chain, k_chain, k_mask, d_update,
):
    pbc = lax.axis_size("pb")
    kac = lax.axis_size("ka")
    pb = lax.axis_index("pb")
    ka = lax.axis_index("ka")
    ni, nj, cp = pair_tile.shape
    oq, width = q_single.shape
    nk = k_single.shape[0]
    slot = -(-2 * oq // 8) * 8
    w_query_t, w_key_t, w_bias_t = (jnp.transpose(x) for x in (w_query, w_key, w_bias))

    def ka_xor(x, d):
        return lax.ppermute(x, "ka", [(i, i ^ d) for i in range(kac)])

    def pb_xor(x, d):
        return lax.ppermute(x, "pb", [(i, i ^ d) for i in range(pbc)])

    n_row = ni * HP
    chips = kac // 2
    f32 = lambda *s: (s, F32)
    bf16 = lambda *s: (s, BF16)
    k_rows = width // 128 * nk + 16
    pk, pq = call(
        functools.partial(pack_kernel, pbc),
        [f32(k_rows, 128), f32(slot, width + 128)],
        [k_single, k_frames, q_single, jnp.transpose(q_frames), d_update],
        far=range(5),
        name="pack",
    )
    params = [pair_tile, w_out, w_query_t, w_key_t]
    pair_v, w_out_v, w_query_v, w_key_v = load(params, pk)
    own_pieces = [pq] + [ka_xor(pq, 2 * d) for d in range(1, kac // 2)]
    (query_own,) = call(
        stack_kernel,
        [f32(kac // 2, slot, width + 128)],
        [w_query_v] + own_pieces,
        name="stack",
    )
    query_other = ka_xor(query_own, 1)
    part = chips // 2
    there = []
    for p in range(pbc):
        for a in range(kac):
            z, core = a // 2, a % 2
            column = (2 * (z % part) + core) ^ p
            there.append((p * kac + a, column * kac + 2 * p + z // part))
    moved = lax.ppermute(pk, ("pb", "ka"), there)
    crossed = [pb_xor(moved, d) for d in range(1, pbc)]
    base, dap, gw, q_feat, qt, l1, l2, l3, dmh, dml, dv, du, frt = call(
        functools.partial(query_kernel, ni, kac, oq, slot),
        [f32(n_row, nj), f32(n_row, nj), f32(n_row + 2 * HP, cp), f32(ni, QW), f32(QW, 128),
         bf16(n_row, QW), bf16(n_row, QW), bf16(n_row, QW), bf16(n_row, 256), bf16(n_row, 256),
         f32(128, 256), f32(ni, width), f32(128, 128)],
        [q_chain, query_own, query_other, pair_v, w_query_v, w_out_v, w_bias_t,
         head_weight[None, :], chain_bias[None, :], k_chain[None, :]],
        far=range(6, 10),
        kept=range(13),
        smem=1,
        scratch=[f32(kac * slot, width + 128), f32(128, QW)],
        name="query",
    )
    weights, da, pay, kq, vt = call(
        functools.partial(key_kernel, ni, nk, pbc),
        [f32(n_row, nj), f32(n_row, nj), f32(ni, PW), f32(QW, nj), f32(HC + PW, nj)],
        [moved, *crossed, w_key_v, base, l1, l2, l3, dmh, dml, dap, gw, k_mask[None, :]],
        far=[pbc + 9],
        kept=[0, 1, 3, 4],
        scratch=[f32(nj, width), f32(w_key_t.shape[0], nj)],
        name="key",
    )
    lh, ll, dvh, dvl, dlt = call(
        functools.partial(spread_kernel, ni),
        [bf16(HC + QP, n_row), bf16(HC + QP, n_row), bf16(HC, n_row), bf16(HC, n_row),
         f32(PW, 128)],
        [qt, dv, du, gw, w_out_v],
        kept=range(5),
        scratch=[f32(128, PW), f32(256, 128)],
        name="spread",
    )
    (u,) = call(
        functools.partial(value_kernel, ni),
        [f32(H, ni, width)],
        [weights, pair_v, vt, w_out_v],
        kept=[0],
        scratch=[f32(n_row, cp), f32(n_row, 128), f32(n_row, 128)],
        name="value",
    )
    (near,) = call(combine_kernel, [f32(ni, PW)], [pay, ka_xor(pay, 1)], name="combine")
    (total,) = call(
        combine_kernel,
        [f32(ni, PW)],
        [near] + [ka_xor(near, 2 * d) for d in range(1, chips)],
        name="combine",
    )
    wide = 3 * width + 128
    att, dl0, mine, theirs, dpt = call(
        functools.partial(grad_kernel, ni, oq, kac),
        [f32(n_row, nj), f32(n_row, nj), f32(ni // 2, wide), f32(ni // 2, wide), f32(VP, 128)],
        [total, pay, weights, da, dap, q_feat, dlt, frt, kq, vt, u, gw, w_out_v],
        kept=[0, 1, 4],
        scratch=[f32(128, 384), f32(384, 128)],
        name="grad",
    )
    (keyv,) = call(
        functools.partial(keyv_kernel, ni),
        [f32(nj, width)],
        [att, dvh, dvl, dpt, kq, w_key_v],
        kept=[0],
        scratch=[f32(nj, 640), f32(640, nj)],
        name="keyv",
    )
    slices = call(
        functools.partial(mid_kernel, ni, oq, chips, width),
        [f32(oq, 3 * width + HP // oq // min(128 // ni, HP // oq) * 128)] * chips,
        [mine, ka_xor(theirs, 1)],
        name="mid",
    )
    slices = [slices[0]] + [ka_xor(slices[d], 2 * d) for d in reversed(range(1, chips))]
    fixed = call(
        functools.partial(keyfix_kernel, ni, oq, width, chips, pbc),
        [f32(n_row, nj)] + [f32(nj // pbc, width)] * pbc,
        [*slices, att, dl0, lh, ll, kq, gw, keyv, w_key_v],
        kept=[0],
        scratch=[f32(128, 128), f32(512, nj), f32(nj, 512), f32(nj, width)],
        name="keyfix",
    )
    dl, blocks = fixed[0], fixed[1:]
    steps = 4
    d_pair, update, d_query = pl.pallas_call(
        functools.partial(tail_kernel, ni, oq, width, chips, steps),
        out_shape=[
            pltpu.HBM((ni, nj, cp), BF16),
            jax.ShapeDtypeStruct((oq, width), BF16),
            jax.ShapeDtypeStruct((oq, width), BF16),
        ],
        in_specs=[pl.BlockSpec(memory_space=pltpu.VMEM)] * (chips + 4),
        out_specs=[pl.BlockSpec(memory_space=pltpu.HBM)]
        + [pl.BlockSpec(memory_space=pltpu.VMEM)] * 2,
        scratch_shapes=[
            pltpu.VMEM((128, 128), F32),
            pltpu.VMEM((8, 2 * width), F32),
            pltpu.VMEM((ni, nj, cp), BF16),
            pltpu.SemaphoreType.DMA((steps,)),
        ],
        compiler_params=pltpu.CompilerParams(vmem_limit_bytes=24 * 1024 * 1024),
        name="tail",
    )(
        *slices,
        *[
            pltpu.with_memory_space_constraint(x.value, pltpu.VMEM)
            for x in (w_query_v, att, dl, gw)
        ],
    )
    key_own = blocks[0]
    for d in reversed(range(1, pbc)):
        key_own = key_own + pb_xor(blocks[d], d)
    return update, d_pair, d_query, key_own


def solution(mesh):
    both = ("pb", "ka")
    placed = (
        P(both, None), P(both, None), P(None, both), P(None, both), P("pb", "ka", None),
        P(), P(), P(), P(), P(), P(), P("pb"), P("ka"), P("ka"), P(both, None),
    )
    return jax.shard_map(
        local,
        mesh=mesh,
        in_specs=placed,
        out_specs=(
            P(both, None), P("pb", "ka", None), P(both, None), P(("ka", "pb"), None),
        ),
        check_vma=False,
    )
```
